256 devices in a mesh: dp: 8 (over x_hi, y), ctx: 32 (over x_lo, z, core).
Axes of the slice: x: 4 (x_hi: 2, x_lo: 2; x = x_hi * 2 + x_lo), y: 4, z: 8, core: 2. Of those that a mesh axis runs over, the one named last changes fastest.
Arguments:
- query: bfloat16 [32768, 512], P(('dp', 'ctx')), may hold values from -6 to 6
- key: bfloat16 [32768, 512], P(('dp', 'ctx')), may hold values from -6 to 6
- value: bfloat16 [32768, 512], P(('dp', 'ctx'))
- gate: bfloat16 [32768, 512], P(('dp', 'ctx')), may hold values from -6 to 6
- out_weight: bfloat16 [512, 1024], replicated, may hold values from -0.25 to 0.25
- items: bfloat16 [1024, 1024], P('ctx'), may hold values from -0.1875 to 0.1875
- cotangent: bfloat16 [32768, 1024], P(('dp', 'ctx')), may hold values from -6 to 6
- user_blocks: int32 [8, 4], P('dp'), may hold values from 1 to 16, 32 in all within a row
- tail_rows: int32 [8, 4], P('dp'), may hold values from 1 to 128
- packing: int32 [8, 32], P('dp'), may hold values from 0 to 31, each once within a row
- cand_ids: int32 [8, 4, 128], P('dp'), may hold values from 0 to 1023
Outputs:
- scores: float32 [32768, 128], P(('dp', 'ctx'))
- grad_query: bfloat16 [32768, 512], P(('dp', 'ctx'))
- grad_key: bfloat16 [32768, 512], P(('dp', 'ctx'))
- grad_value: bfloat16 [32768, 512], P(('dp', 'ctx'))
- grad_gate: bfloat16 [32768, 512], P(('dp', 'ctx'))
- grad_out_weight: float32 [512, 1024], replicated
The draws below stay inside these ranges and needn't reach their ends.
Inputs may be any that keep to these rules, and one draw needn't show every extreme that they name: `user_blocks`: in each group the 4 counts sum to 32 and the largest is exactly 16. `packing`: each group's row is a permutation of its 32 logical blocks; slots run device by device along ctx. `cand_ids`: rows of the item table.
All inputs are finite; a program needn't handle non-finite values.
Results may differ from the reference program's by a relative error of at most 0.0058.
Values may be sent and summed in bfloat16 or wider, within the bound.
No kernel may reach another device: no remote copies, remote signals or barrier semaphores. Data moves between devices by JAX's collectives and lax.ppermute only.
A program may use at most 128 MiB of HBM per device.

```python
import math
import jax
import jax.numpy as jnp
import numpy as np
from jax import lax

D = 1024
HEADS = 4
HEAD_DIM = 128
BLOCK = 128
TOK_DEV = 128
USERS = 4
CAND = 128
ATTN_WIDTH = 512
TOKENS = 32768
BLOCKS_G = 32
MOST_BLOCKS = 16
ITEMS = 1024
N_DP = 8
N_CTX = 32


def draw_value(key, part):
    sample_key, spread_key = jax.random.split(key)
    columns = HEADS * HEAD_DIM
    spread = jnp.exp(jax.random.uniform(spread_key, (columns,), jnp.float32, 0.0, math.log(10.0)))
    sample = jnp.clip(jax.random.normal(sample_key, (TOKENS, columns), jnp.float32), -4.0, 4.0)
    return (sample * spread[None, :] * 0.3).astype(jnp.bfloat16)


def place_ends(values, key, least, largest):
    spot = [jax.random.randint(jax.random.fold_in(key, axis), (), 0, length) for axis, length in enumerate(values.shape)]
    main_axis = values.shape.index(max(values.shape))
    beside = spot[:main_axis] + [(spot[main_axis] + 1) % values.shape[main_axis]] + spot[main_axis + 1:]
    return values.at[tuple(spot)].set(least).at[tuple(beside)].set(largest)


def level_of(stream_key, extent, cuts, least, high):
    def one(dim, blocks):
        heights = jax.random.uniform(jax.random.fold_in(jax.random.fold_in(stream_key, 6), dim), (blocks,), jnp.float32, least / len(cuts), high / len(cuts))
        return jnp.repeat(jnp.exp(heights), extent[dim] // blocks).reshape((-1,) + (1,) * (len(extent) - dim - 1))

    loudness = one(*cuts[0])
    for cut in cuts[1:]:
        loudness = loudness * one(*cut)
    return loudness


def split_up(number_of, total, bound, skew):
    loads = [(1 << 20) // math.isqrt(rank ** skew) + 1 for rank in range(2, number_of + 1)]
    rest, holding = total - bound - (number_of - 1), [1] * (number_of - 1)
    while rest > 0:
        free = [i for i in range(number_of - 1) if holding[i] < bound]
        whole, remaining = sum([loads[i] for i in free]), rest
        for i in free:
            more = min(bound - holding[i], max(1, remaining * loads[i] // whole), rest)
            holding[i] = holding[i] + more
            rest = rest - more
    return np.array([bound] + holding)


def uneven_parts(rng, number_of, total, reach, skew):
    if number_of == 2:
        one = jax.random.randint(rng, (), max(1, total - reach), min(reach, total - 1) + 1)
        return jnp.stack([one, total - one])
    tallies = jnp.asarray(split_up(number_of, total, reach, skew), jnp.int32)
    twos = (number_of - 1) // 2
    donor, sink = tallies[1:1 + 2 * twos:2], tallies[2:2 + 2 * twos:2]
    room = jnp.minimum(donor - 1, reach - sink)
    shifted = jax.random.randint(jax.random.fold_in(rng, 1), (twos,), 0, 1 << 20) % (room + 1)
    tallies = tallies.at[1:1 + 2 * twos:2].set(donor - shifted).at[2:2 + 2 * twos:2].set(sink + shifted)
    return tallies[jax.random.permutation(jax.random.fold_in(rng, 2), number_of)]


def bell_draw(rng, shape, scale, most, cuts=(), kind=jnp.bfloat16):
    result = scale * jax.random.normal(rng, shape, jnp.float32)
    if cuts:
        result = result * level_of(rng, shape, cuts, -0.22, 0.18)
    return jnp.clip(result, -most, most).astype(kind)


def setup_inputs(seed: int = 0) -> dict:
    key_list = jax.random.split(jax.random.key(seed), 12)
    query = bell_draw(key_list[0], (TOKENS, ATTN_WIDTH), 1.0, 6.0, ((0, 256),))
    key = bell_draw(key_list[1], (TOKENS, ATTN_WIDTH), 1.0, 6.0, ((0, 256),))
    value = draw_value(jax.random.fold_in(key_list[11], 71), 0)
    gate = bell_draw(key_list[3], (TOKENS, ATTN_WIDTH), 1.0, 6.0, ((0, 256),))
    out_weight = bell_draw(key_list[4], (ATTN_WIDTH, D), ATTN_WIDTH ** -0.5, 0.25)
    items = bell_draw(key_list[5], (ITEMS, D), D ** -0.5, 0.1875, ((0, 32),))
    cotangent = bell_draw(key_list[6], (TOKENS, D), 1.0, 6.0, ((0, 256),))
    user_blocks = jax.vmap(lambda own: uneven_parts(own, USERS, BLOCKS_G, MOST_BLOCKS, 1))(jax.random.split(key_list[7], N_DP)).reshape((N_DP, USERS)).astype(jnp.int32)
    tail_rows = place_ends(jax.random.randint(key_list[8], (N_DP, USERS), 1, BLOCK + 1), jax.random.fold_in(key_list[8], 1), 1, BLOCK).astype(jnp.int32)
    packing = jax.vmap(lambda own: jax.random.permutation(own, BLOCKS_G))(jax.random.split(key_list[9], N_DP)).reshape((N_DP, BLOCKS_G)).astype(jnp.int32)
    cand_ids = place_ends(jax.random.randint(key_list[10], (N_DP, USERS, CAND), 0, ITEMS), jax.random.fold_in(key_list[10], 1), 0, ITEMS - 1).astype(jnp.int32)
    return dict(query=query, key=key, value=value, gate=gate, out_weight=out_weight, items=items, cotangent=cotangent, user_blocks=user_blocks, tail_rows=tail_rows, packing=packing, cand_ids=cand_ids)


norm_eps = 1e-05

def row_facts(blocks, tails, layout, offset, length):
    row_index = offset + jnp.arange(length, dtype=jnp.int32)
    slot_index = (row_index // BLOCK).astype(jnp.int32)
    within = (row_index % BLOCK).astype(jnp.int32)
    user_ends = jnp.cumsum(blocks).astype(jnp.int32)
    user_starts = (user_ends - blocks).astype(jnp.int32)
    user_rows = ((blocks - 1) * BLOCK + tails).astype(jnp.int32)
    slot_match = slot_index[:, None] == jnp.arange(layout.shape[0], dtype=jnp.int32)[None, :]
    logical = lax.optimization_barrier(jnp.sum(jnp.where(slot_match, layout[None, :], 0), axis=1)).astype(jnp.int32)
    user_of = lax.optimization_barrier(jnp.sum((logical[:, None] >= user_ends[None, :]).astype(jnp.int32), axis=1)).astype(jnp.int32)
    user_match = user_of[:, None] == jnp.arange(blocks.shape[0], dtype=jnp.int32)[None, :]
    first_row = (lax.optimization_barrier(jnp.sum(jnp.where(user_match, user_starts[None, :], 0), axis=1)) * BLOCK).astype(jnp.int32)
    row_limit = lax.optimization_barrier(jnp.sum(jnp.where(user_match, user_rows[None, :], 0), axis=1)).astype(jnp.int32)
    position = (logical * BLOCK + within).astype(jnp.int32)
    is_valid = position - first_row < row_limit
    return (user_of, position, is_valid)

def pair_mask(query_facts, key_facts):
    same_user = query_facts[0][:, None] == key_facts[0][None, :]
    earlier = key_facts[1][None, :] <= query_facts[1][:, None]
    both_valid = query_facts[2][:, None] & key_facts[2][None, :]
    return same_user & earlier & both_valid

def silu_slope(values):
    sigma = jax.nn.sigmoid(values)
    return sigma * (1.0 + values * (1.0 - sigma))

def to_float(array):
    return lax.optimization_barrier(array).astype(jnp.float32)

def one_group(query, key, value, gate, out_weight, items, cotangent, blocks, tails, layout, candidates):
    row_count = query.shape[0]
    score_scale = HEAD_DIM ** (-0.5)
    facts = row_facts(blocks, tails, layout, 0, row_count)
    query_heads = query.astype(jnp.float32).reshape(row_count, HEADS, HEAD_DIM)
    key_heads = key.astype(jnp.float32).reshape(row_count, HEADS, HEAD_DIM)
    value_heads = value.astype(jnp.float32).reshape(row_count, HEADS, HEAD_DIM)
    block_starts = (jnp.arange(row_count // BLOCK) * BLOCK).astype(jnp.int32)

    def block_facts(offset_row):
        return tuple((lax.dynamic_slice_in_dim(entry, offset_row, BLOCK) for entry in facts))

    def forward_block(offset_row):
        query_block = lax.dynamic_slice_in_dim(query_heads, offset_row, BLOCK, 0)
        allowed = pair_mask(block_facts(offset_row), facts)
        logits = jnp.einsum('qhd,khd->hqk', query_block, key_heads) * score_scale
        weights = (jax.nn.silu(logits) * allowed[None]).astype(jnp.bfloat16)
        return jnp.einsum('hqk,khd->qhd', to_float(weights), value_heads)
    attended = lax.map(forward_block, block_starts).reshape(row_count, HEADS * HEAD_DIM)
    row_mean = lax.optimization_barrier(jnp.mean(attended, axis=1, keepdims=True))
    centered = attended - row_mean
    inv_std = lax.rsqrt(lax.optimization_barrier(jnp.mean(centered * centered, axis=1, keepdims=True)) + norm_eps)
    normed = centered * inv_std
    valid_col = facts[2].astype(jnp.float32)[:, None]
    gate_float = gate.astype(jnp.float32)
    mixed = (valid_col * normed * gate_float).astype(jnp.bfloat16)
    output = jnp.dot(mixed, out_weight, preferred_element_type=jnp.float32).astype(jnp.bfloat16)
    all_scores = lax.dot_general(output, items, (((1,), (1,)), ((), ())), preferred_element_type=jnp.float32)
    user_match = facts[0][:, None] == jnp.arange(candidates.shape[0], dtype=jnp.int32)[None, :]
    picked = lax.optimization_barrier(jnp.sum(jnp.where(user_match[:, :, None], candidates[None, :, :], 0), axis=1)).astype(jnp.int32)
    scores = jnp.take_along_axis(all_scores, picked, axis=1)
    weight_term = lax.dot_general(mixed, cotangent, (((0,), (0,)), ((), ())), preferred_element_type=jnp.float32)
    grad_mixed = lax.dot_general(cotangent, out_weight, (((1,), (1,)), ((), ())), preferred_element_type=jnp.float32)
    grad_gate = (grad_mixed * valid_col * normed).astype(jnp.bfloat16)
    grad_normed = grad_mixed * valid_col * gate_float
    grad_attended = ((grad_normed - lax.optimization_barrier(jnp.mean(grad_normed, axis=1, keepdims=True)) - normed * lax.optimization_barrier(jnp.mean(grad_normed * normed, axis=1, keepdims=True))) * inv_std).astype(jnp.bfloat16)
    grad_heads = to_float(grad_attended).reshape(row_count, HEADS, HEAD_DIM)

    def backward_block(running, offset_row):
        query_block = lax.dynamic_slice_in_dim(query_heads, offset_row, BLOCK, 0)
        grad_block = lax.dynamic_slice_in_dim(grad_heads, offset_row, BLOCK, 0)
        allowed = pair_mask(block_facts(offset_row), facts)
        logits = jnp.einsum('qhd,khd->hqk', query_block, key_heads) * score_scale
        weights = to_float((jax.nn.silu(logits) * allowed[None]).astype(jnp.bfloat16))
        slopes = jnp.einsum('qhd,khd->hqk', grad_block, value_heads)
        grad_logits = to_float((slopes * allowed[None] * silu_slope(logits)).astype(jnp.bfloat16))
        query_part = jnp.einsum('hqk,khd->qhd', grad_logits, key_heads)
        key_sum = running[0] + jnp.einsum('hqk,qhd->khd', grad_logits, query_block)
        value_sum = running[1] + jnp.einsum('hqk,qhd->khd', weights, grad_block)
        return ((key_sum, value_sum), query_part)
    zeros_heads = jnp.zeros((row_count, HEADS, HEAD_DIM), jnp.float32)
    sums, query_parts = lax.scan(backward_block, (zeros_heads, zeros_heads), block_starts)
    grad_query = (query_parts.reshape(row_count, HEADS * HEAD_DIM) * score_scale).astype(jnp.bfloat16)
    grad_key = (sums[0].reshape(row_count, HEADS * HEAD_DIM) * score_scale).astype(jnp.bfloat16)
    grad_value = sums[1].reshape(row_count, HEADS * HEAD_DIM).astype(jnp.bfloat16)
    return (scores, grad_query, grad_key, grad_value, grad_gate, weight_term)

def reference(query, key, value, gate, out_weight, items, cotangent, user_blocks, tail_rows, packing, cand_ids):
    group_rows = TOK_DEV * N_CTX
    results = []
    for group in range(N_DP):
        lower = group * group_rows
        upper = lower + group_rows
        results.append(one_group(query[lower:upper], key[lower:upper], value[lower:upper], gate[lower:upper], out_weight, items, cotangent[lower:upper], user_blocks[group], tail_rows[group], packing[group], cand_ids[group]))
    scores = jnp.concatenate([entry[0] for entry in results], axis=0)
    grad_query = jnp.concatenate([entry[1] for entry in results], axis=0)
    grad_key = jnp.concatenate([entry[2] for entry in results], axis=0)
    grad_value = jnp.concatenate([entry[3] for entry in results], axis=0)
    grad_gate = jnp.concatenate([entry[4] for entry in results], axis=0)
    grad_out_weight = results[0][5]
    for entry in results[1:]:
        grad_out_weight = grad_out_weight + entry[5]
    return (scores, grad_query, grad_key, grad_value, grad_gate, grad_out_weight)
```

```python
import jax
import jax.numpy as jnp
from jax import lax
from jax.experimental import pallas as pl
from jax.experimental.pallas import tpu as pltpu
from jax.sharding import Mesh, PartitionSpec as P

AXES = ("xh", "y", "xl", "zh", "zl", "core")
SIZES = (2, 4, 2, 4, 2, 2)
DP = ("xh", "y")
CTX = ("xl", "zh", "zl", "core")
SCALE = 128 ** (-0.5)
EPS = 1e-05
F32 = jnp.float32
BF16 = jnp.bfloat16
I32 = jnp.int32

VM = pl.BlockSpec(memory_space=pltpu.VMEM)
SM = pl.BlockSpec(memory_space=pltpu.SMEM)
ANY = pl.BlockSpec(memory_space=pl.ANY)


def dot(a, b, ca, cb):
    return lax.dot_general(a, b, (((ca,), (cb,)), ((), ())), preferred_element_type=F32)


def slot_of(place):
    chunk, back = place // 4, place % 4
    xl = (lax.axis_index("xl") + (chunk // 2) % 2) % 2
    zh = (lax.axis_index("zh") + 4 - back) % 4
    zl = (lax.axis_index("zl") + chunk % 2) % 2
    core = (lax.axis_index("core") + chunk // 4) % 2
    return xl * 16 + zh * 4 + zl * 2 + core


def fill_places(pk_ref, inv_ref):
    def one(place, carry):
        inv_ref[pk_ref[0, slot_of(place)]] = place
        return carry

    lax.fori_loop(0, 32, one, 0)


def user_of(ub_ref, tl_ref, logical):
    end0 = ub_ref[0, 0]
    end1 = end0 + ub_ref[0, 1]
    end2 = end1 + ub_ref[0, 2]
    user = (
        (logical >= end0).astype(I32) + (logical >= end1).astype(I32) + (logical >= end2).astype(I32)
    )
    first = jnp.where(user == 0, 0, jnp.where(user == 1, end0, jnp.where(user == 2, end1, end2)))
    return user, first, ub_ref[0, user], tl_ref[0, user]


def load_chunks(refs, buffer, sems):
    copies = [
        pltpu.make_async_copy(ref, buffer.at[pl.ds(4 * i, 4)], sems.at[i]) for i, ref in enumerate(refs)
    ]
    for copy in copies:
        copy.start()
    return copies


def iota(shape, axis):
    return lax.broadcasted_iota(I32, shape, axis)


def head_columns(quarters):
    head = (lax.axis_index("zh") + quarters) % 4
    return pl.ds(pl.multiple_of(head * 128, 128), 128)


def pack_first_kernel(k_ref, v_ref, *outs):
    for d in range(4):
        outs[d][0] = k_ref[:, head_columns(d)]
        outs[d][1] = v_ref[:, head_columns(d)]


def pack_second_kernel(q_ref, g_ref, t_ref, *outs):
    for d in range(4):
        outs[d][:128] = q_ref[:, head_columns(d)]
        outs[d][128:160] = t_ref[:, head_columns(d)]
        outs[d][160:] = g_ref[:, head_columns(d)]


def mixed_grad_kernel(c0, c1, c2, c3, w_ref, gm_ref, wbuf, sem):
    copy = pltpu.make_async_copy(
        w_ref.at[pl.ds(pl.multiple_of(lax.axis_index("zh") * 128, 128), 128)], wbuf, sem
    )
    copy.start()
    copy.wait()
    for d, cot in enumerate((c0, c1, c2, c3)):
        gm_ref[d] = dot(cot[...], wbuf[...], 1, 1)


def forward_kernel(ub, tl, pk, q_ref, gate_ref, gm_ref, *rest):
    chunks, (att_ref, stat_ref), (kv, inv, sems) = rest[:8], rest[8:10], rest[10:]
    copies = load_chunks(chunks, kv, sems)
    fill_places(pk, inv)
    for copy in copies:
        copy.wait()
    row = iota((128, 512), 0)
    col = iota((128, 512), 1)
    lane = iota((128, 128), 1)
    for slot in range(4):
        logical = pk[0, slot_of(slot)]
        user, first, blocks, tail = user_of(ub, tl, logical)
        own = logical - first
        query = q_ref[slot, :128]

        def step(j, acc):
            places = [inv[first + jnp.minimum(4 * j + i, own)] for i in range(4)]
            keys = jnp.concatenate([kv[p, 0] for p in places], axis=0)
            values = jnp.concatenate([kv[p, 1] for p in places], axis=0)
            logits = dot(query, keys, 1, 1) * SCALE
            silu = logits / (1.0 + jnp.exp(-logits))
            weights = jnp.where(col + (4 * j - own) * 128 <= row, silu, 0.0).astype(BF16)
            return acc + dot(weights, values, 1, 0)

        acc = lax.fori_loop(0, own // 4 + 1, step, jnp.zeros((128, 128), F32))
        limit = jnp.where(own == blocks - 1, tail, 128)
        valid = iota((128, 128), 0) < limit
        att = jnp.where(valid, acc, 0.0)
        att_ref[slot] = att
        grad = jnp.where(valid, gm_ref[slot] * gate_ref[slot].astype(F32), 0.0)
        mean = jnp.mean(att, axis=1, keepdims=True)
        centered = att - mean
        spread = jnp.sum(centered * centered, axis=1, keepdims=True)
        total = jnp.sum(grad, axis=1, keepdims=True)
        cross = jnp.sum(grad * centered, axis=1, keepdims=True)
        stats = jnp.where(
            lane == 0, mean, jnp.where(lane == 1, spread, jnp.where(lane == 2, total, cross))
        )
        stat_ref[:, pl.ds(slot * 128, 128)] = stats.T[:8]


def norm_kernel(
    ub, tl, pk, att_ref, s0, s1, s2, s3, gate_ref, gm_ref, da_ref, gg_ref, mixed_ref
):
    for slot in range(4):
        user, first, blocks, tail = user_of(ub, tl, pk[0, slot_of(slot)])
        own = pk[0, slot_of(slot)] - first
        limit = jnp.where(own == blocks - 1, tail, 128)
        valid = iota((128, 128), 0) < limit
        stat = jnp.concatenate(
            [s[:, pl.ds(((slot - e) % 4) * 128, 128)] for e, s in enumerate((s0, s1, s2, s3))], axis=0
        )
        stat = jnp.concatenate([stat, jnp.zeros((96, 128), F32)], axis=0).T
        means = [stat[:, 8 * h : 8 * h + 1] for h in range(4)]
        mean = (means[0] + means[1] + means[2] + means[3]) * 0.25
        var = jnp.zeros((128, 1), F32)
        total = jnp.zeros((128, 1), F32)
        cross = jnp.zeros((128, 1), F32)
        for h in range(4):
            away = means[h] - mean
            part = stat[:, 8 * h + 2 : 8 * h + 3]
            var = var + stat[:, 8 * h + 1 : 8 * h + 2] + 128.0 * away * away
            total = total + part
            cross = cross + stat[:, 8 * h + 3 : 8 * h + 4] + away * part
        inv_std = lax.rsqrt(var * (1.0 / 512) + EPS)
        normed = (att_ref[slot] - mean) * inv_std
        gate = gate_ref[slot].astype(F32)
        gmix = jnp.where(valid, gm_ref[slot], 0.0)
        grad = gmix * gate
        da = (grad - total * (1.0 / 512) - normed * (cross * inv_std * (1.0 / 512))) * inv_std
        da_ref[slot] = jnp.where(valid, da, 0.0).astype(BF16)
        gg_ref[slot] = (gmix * normed).astype(BF16)
        mixed_ref[pl.ds(slot * 128, 128), :] = jnp.where(valid, normed * gate, 0.0).astype(BF16)


def weight_kernel(mixed_ref, c0, c1, c2, c3, gw_ref):
    for part in range(4):
        term = jnp.zeros((128, 256), F32)
        for d, cot in enumerate((c0, c1, c2, c3)):
            term = term + dot(mixed_ref[pl.ds(d * 128, 128), :], cot[:, pl.ds(part * 256, 256)], 0, 0)
        term = term.astype(BF16)
        for r in range(8):
            for c in range(2):
                gw_ref[r * 8 + part * 2 + c] = term[r * 16 : r * 16 + 16, c * 128 : c * 128 + 128]


def score_kernel(ub, tl, pk, mixed_ref, cand_ref, *rest):
    chunks, (sc_ref,), (qp, sems) = rest[:8], rest[8:9], rest[9:]
    copies = load_chunks(chunks, qp, sems)
    item = iota((1024, 128), 0)
    place = item // 32
    chunk = place // 4
    held = (
        ((lax.axis_index("xl") + chunk // 2) % 2) * 16
        + ((lax.axis_index("zh") + 4 - place % 4) % 4) * 4
        + ((lax.axis_index("zl") + chunk) % 2) * 2
        + (lax.axis_index("core") + chunk // 4) % 2
    ) * 32 + item % 32
    for copy in copies:
        copy.wait()
    table = jnp.concatenate([qp[p, 128:160] for p in range(32)], axis=0)
    for slot in range(4):
        user = user_of(ub, tl, pk[0, slot_of(slot)])[0]
        pick = (held == cand_ref[pl.ds(user, 1), :]).astype(F32).astype(BF16)
        chosen = dot(table, pick, 0, 0).astype(BF16)
        sc_ref[slot] = dot(mixed_ref[pl.ds(slot * 128, 128), :], chosen, 1, 0).astype(BF16)


def query_kernel(ub, tl, pk, q_ref, da_ref, gg_ref, sc_ref, *rest):
    chunks, outs, (kv, inv, sems) = rest[:8], rest[8:12], rest[12:]
    copies = load_chunks(chunks, kv, sems)
    fill_places(pk, inv)
    for copy in copies:
        copy.wait()
    row = iota((128, 512), 0)
    col = iota((128, 512), 1)
    for slot in range(4):
        logical = pk[0, slot_of(slot)]
        first = user_of(ub, tl, logical)[1]
        own = logical - first
        query = q_ref[slot, :128]
        grad = da_ref[slot]

        def step(j, acc):
            places = [inv[first + jnp.minimum(4 * j + i, own)] for i in range(4)]
            keys = jnp.concatenate([kv[p, 0] for p in places], axis=0)
            values = jnp.concatenate([kv[p, 1] for p in places], axis=0)
            logits = dot(query, keys, 1, 1) * SCALE
            slopes = dot(grad, values, 1, 1)
            sigma = 1.0 / (1.0 + jnp.exp(-logits))
            slope = sigma * (1.0 + logits * (1.0 - sigma))
            ds = jnp.where(col + (4 * j - own) * 128 <= row, slopes * slope, 0.0).astype(BF16)
            return acc + dot(ds, keys, 1, 0)

        acc = lax.fori_loop(0, own // 4 + 1, step, jnp.zeros((128, 128), F32))
        outs[slot][0] = (acc * SCALE).astype(BF16)
        outs[slot][1] = gg_ref[slot]
        outs[slot][2] = sc_ref[slot]


def key_kernel(ub, tl, pk, kv_ref, *rest):
    qs, das, outs, (qbuf, dbuf, inv, qsems, dsems) = rest[:8], rest[8:16], rest[16:20], rest[20:]
    copies = load_chunks(qs, qbuf, qsems) + load_chunks(das, dbuf, dsems)
    fill_places(pk, inv)
    for copy in copies:
        copy.wait()
    row = iota((128, 512), 0)
    col = iota((128, 512), 1)
    for slot in range(4):
        logical = pk[0, slot_of(slot)]
        user, first, blocks, tail = user_of(ub, tl, logical)
        count = first + blocks - logical
        key = kv_ref[slot, 0]
        value = kv_ref[slot, 1]

        def step(j, carry):
            gk, gv = carry
            places = [inv[logical + jnp.minimum(4 * j + i, count - 1)] for i in range(4)]
            queries = jnp.concatenate([qbuf[p, :128] for p in places], axis=0)
            grads = jnp.concatenate([dbuf[p] for p in places], axis=0)
            logits = dot(key, queries, 1, 1) * SCALE
            slopes = dot(value, grads, 1, 1)
            sigma = 1.0 / (1.0 + jnp.exp(-logits))
            silu = logits * sigma
            slope = sigma * (1.0 + logits * (1.0 - sigma))
            later = col + j * 512
            allowed = (later >= row) & (later < count * 128)
            weights = jnp.where(allowed, silu, 0.0).astype(BF16)
            ds = jnp.where(allowed, slopes * slope, 0.0).astype(BF16)
            return gk + dot(ds, queries, 1, 0), gv + dot(weights, grads, 1, 0)

        zero = jnp.zeros((128, 128), F32)
        gk, gv = lax.fori_loop(0, (count + 3) // 4, step, (zero, zero))
        outs[slot][0] = (gk * SCALE).astype(BF16)
        outs[slot][1] = gv.astype(BF16)


def unpack_early_kernel(p0, p1, p2, p3, gq_ref, gg_ref, sc_ref):
    scores = jnp.zeros((128, 128), F32)
    for d, piece in enumerate((p0, p1, p2, p3)):
        gq_ref[:, head_columns(d)] = piece[0]
        gg_ref[:, head_columns(d)] = piece[1]
        scores = scores + piece[2].astype(F32)
    sc_ref[...] = scores


def unpack_late_kernel(p0, p1, p2, p3, gk_ref, gv_ref):
    for d, piece in enumerate((p0, p1, p2, p3)):
        gk_ref[:, head_columns(d)] = piece[0]
        gv_ref[:, head_columns(d)] = piece[1]


def assemble_kernel(own_ref, far_ref, out_ref):
    me = lax.axis_index("core")
    for r in range(8):
        for xl in range(2):
            for zh in range(4):
                for zl in range(2):
                    place = ((r * 2 + xl) * 4 + zh) * 2 + zl
                    rows = pl.ds(zh * 128 + r * 16, 16)
                    left = (xl * 4 + zl * 2) * 128
                    own = own_ref[place].astype(F32)
                    far = far_ref[place].astype(F32)
                    out_ref[rows, pl.ds(left, 128)] = jnp.where(me == 0, own, far)
                    out_ref[rows, pl.ds(left + 128, 128)] = jnp.where(me == 0, far, own)


def call(kernel, ins, outs, scratch=(), us=2):
    return pl.pallas_call(
        kernel,
        in_specs=[spec for spec, _ in ins],
        out_specs=[VM] * len(outs),
        out_shape=[jax.ShapeDtypeStruct(shape, kind) for shape, kind in outs],
        scratch_shapes=list(scratch),
        compiler_params=pltpu.CompilerParams(vmem_limit_bytes=32 << 20),
        cost_estimate=pl.CostEstimate(
            flops=us * 1000000000, bytes_accessed=us * 1000000, transcendentals=0
        ),
    )(*[value for _, value in ins])


def flip(array, axis):
    return lax.ppermute(array, axis, [(0, 1), (1, 0)])


def quarters_on(array, d):
    return lax.ppermute(array, "zh", [(i, (i + d) % 4) for i in range(4)])


def gather(array):
    z = flip(array, "zl")
    x = flip(array, "xl")
    d = lax.ppermute(array, ("xl", "zl"), [(i, 3 - i) for i in range(4)])
    near = [array, z, x, d]
    return near + [flip(piece, "core") for piece in near]


def vm(*arrays):
    return [(VM, a) for a in arrays]


def raw(arrays):
    return [(ANY, a) for a in arrays]


def to_heads(pieces):
    return [pieces[0]] + [quarters_on(pieces[d], d) for d in (1, 2, 3)]


def to_rows(pieces):
    return [pieces[0]] + [quarters_on(pieces[d], 4 - d) for d in (1, 2, 3)]


def body(
    query, key, value, gate, out_weight, items, cotangent, user_blocks, tail_rows, packing, cand_ids
):
    facts = [(SM, user_blocks), (SM, tail_rows), (SM, packing)]
    block = (4, 128, 128)
    places = pltpu.SMEM((32,), I32)
    sems = pltpu.SemaphoreType.DMA((8,))
    kv = jnp.stack(to_heads(call(pack_first_kernel, vm(key, value), [((2, 128, 128), BF16)] * 4)))
    kvs = gather(kv)
    table = dot(items, out_weight, 1, 1).astype(BF16)
    second = to_heads(call(pack_second_kernel, vm(query, gate, table), [((288, 128), BF16)] * 4))
    qp = jnp.stack([piece[:160] for piece in second])
    gate_h = jnp.stack([piece[160:] for piece in second])
    cots = to_heads([cotangent] * 4)
    qps = gather(qp)
    (gm,) = call(
        mixed_grad_kernel,
        vm(*cots) + raw([out_weight]),
        [(block, F32)],
        [pltpu.VMEM((128, 1024), BF16), pltpu.SemaphoreType.DMA],
    )
    att, stats = call(
        forward_kernel,
        facts + vm(qp, gate_h, gm) + raw(kvs),
        [(block, F32), ((8, 512), F32)],
        [pltpu.VMEM((32, 2, 128, 128), BF16), places, sems],
        us=6,
    )
    all_stats = to_heads([stats] * 4)
    da, gg, mixed = call(
        norm_kernel,
        facts + vm(att, *all_stats, gate_h, gm),
        [(block, BF16), (block, BF16), ((512, 128), BF16)],
    )
    das = gather(da)
    (gw,) = call(weight_kernel, vm(mixed, *cots), [((64, 16, 128), BF16)])
    parts = lax.all_to_all(
        gw, ("xh", "y", "xl", "zl", "core"), split_axis=0, concat_axis=0, tiled=True
    )
    (sc,) = call(
        score_kernel,
        facts + vm(mixed, cand_ids[0]) + raw(qps),
        [(block, BF16)],
        [pltpu.VMEM((32, 160, 128), BF16), sems],
    )
    early = call(
        query_kernel,
        facts + vm(qp, da, gg, sc) + raw(kvs),
        [((3, 128, 128), BF16)] * 4,
        [pltpu.VMEM((32, 2, 128, 128), BF16), places, sems],
        us=6,
    )
    early = to_rows(early)
    piece = jnp.sum(parts.astype(F32), axis=0).astype(BF16)
    near = lax.all_to_all(
        jnp.broadcast_to(piece[None], (128, 16, 128)),
        ("xh", "y", "xl", "zh", "zl"),
        split_axis=0,
        concat_axis=0,
        tiled=True,
    )
    late = call(
        key_kernel,
        facts + vm(kv) + raw(qps) + raw(das),
        [((2, 128, 128), BF16)] * 4,
        [
            pltpu.VMEM((32, 160, 128), BF16),
            pltpu.VMEM((32, 128, 128), BF16),
            places,
            sems,
            sems,
        ],
        us=8,
    )
    late = to_rows(late)
    far = flip(near, "core")
    (gow,) = call(assemble_kernel, vm(near, far), [((512, 1024), F32)])
    rows = (128, 512)
    gq, gg, scores = call(
        unpack_early_kernel, vm(*early), [(rows, BF16), (rows, BF16), ((128, 128), F32)]
    )
    gk, gv = call(unpack_late_kernel, vm(*late), [(rows, BF16)] * 2)
    return (scores, gq, gk, gv, gg, gow)


def solution(mesh):
    inner = Mesh(mesh.devices.reshape(SIZES), AXES)
    rows = P(DP + CTX, None)
    in_specs = (
        rows, rows, rows, rows, P(), P(CTX, None), rows,
        P(DP, None), P(DP, None), P(DP, None), P(DP, None, None),
    )
    out_specs = (rows, rows, rows, rows, rows, P())
    return jax.shard_map(body, mesh=inner, in_specs=in_specs, out_specs=out_specs, check_vma=False)
```

```python
import jax
import jax.numpy as jnp
from jax import lax
from jax.experimental import pallas as pl
from jax.experimental.pallas import tpu as pltpu
from jax.sharding import Mesh, PartitionSpec as P

AXES = ("xh", "y", "xl", "z", "core")
SIZES = (2, 4, 2, 8, 2)
DP = ("xh", "y")
CTX = ("xl", "z", "core")
SCALE = 128 ** (-0.5)
EPS = 1e-05
F32 = jnp.float32
BF16 = jnp.bfloat16
I32 = jnp.int32

VM = pl.BlockSpec(memory_space=pltpu.VMEM)
SM = pl.BlockSpec(memory_space=pltpu.SMEM)
HBM = pl.BlockSpec(memory_space=pltpu.HBM)


def dot(a, b, ca, cb):
    return lax.dot_general(a, b, (((ca,), (cb,)), ((), ())), preferred_element_type=F32)


def slot_of(place):
    down, other = place // 4, place % 4
    xl = (lax.axis_index("xl") + other // 2) % 2
    z = (lax.axis_index("z") + 8 - down) % 8
    core = (lax.axis_index("core") + other) % 2
    return xl * 16 + z * 2 + core


def fill_places(pk_ref, inv_ref):
    def one(place, carry):
        inv_ref[pk_ref[0, slot_of(place)]] = place
        return carry

    lax.fori_loop(0, 32, one, 0)


def user_of(ub_ref, tl_ref, logical):
    end0 = ub_ref[0, 0]
    end1 = end0 + ub_ref[0, 1]
    end2 = end1 + ub_ref[0, 2]
    user = (
        (logical >= end0).astype(I32) + (logical >= end1).astype(I32) + (logical >= end2).astype(I32)
    )
    first = jnp.where(user == 0, 0, jnp.where(user == 1, end0, jnp.where(user == 2, end1, end2)))
    return user, first, ub_ref[0, user], tl_ref[0, user]


def load_chunks(refs, buffer, sems):
    copies = [
        pltpu.make_async_copy(ref, buffer.at[pl.ds(4 * i, 4)], sems.at[i]) for i, ref in enumerate(refs)
    ]
    for copy in copies:
        copy.start()
    return copies


def iota(shape, axis):
    return lax.broadcasted_iota(I32, shape, axis)


def head_columns(other):
    xl = (lax.axis_index("xl") + other // 2) % 2
    core = (lax.axis_index("core") + other) % 2
    return pl.ds(pl.multiple_of((xl * 2 + core) * 128, 128), 128)


def pack_kernel(k_ref, v_ref, q_ref, g_ref, t_ref, o0, o1, o2, o3, rows, sems):
    copies = [
        pltpu.make_async_copy(ref, rows.at[i], sems.at[i])
        for i, ref in enumerate((k_ref, v_ref, q_ref, g_ref))
    ]
    for copy in copies:
        copy.start()
    outs = (o0, o1, o2, o3)
    for d, out in enumerate(outs):
        out[512:] = t_ref[:, head_columns(d)]
    for i, copy in enumerate(copies):
        copy.wait()
        for d, out in enumerate(outs):
            out[i * 128 : i * 128 + 128] = rows[i, :, head_columns(d)]


def mixed_grad_kernel(c0, c1, c2, c3, w_ref, gm_ref, wbuf, sem):
    copy = pltpu.make_async_copy(
        w_ref.at[head_columns(0)], wbuf, sem
    )
    copy.start()
    copy.wait()
    for d, cot in enumerate((c0, c1, c2, c3)):
        gm_ref[d] = dot(cot[...], wbuf[...], 1, 1)


def merge_kernel(p0, p1, p2, p3, kv_ref, qp_ref, gate_ref):
    for d, piece in enumerate((p0, p1, p2, p3)):
        kv_ref[d, 0] = piece[:128]
        kv_ref[d, 1] = piece[128:256]
        qp_ref[d, :128] = piece[256:384]
        qp_ref[d, 128:] = piece[512:]
        gate_ref[d] = piece[384:512]


def forward_kernel(ub, tl, pk, q_ref, gate_ref, gm_ref, *rest):
    chunks, (att_ref, stat_ref), (kv, inv, sems) = rest[:8], rest[8:10], rest[10:]
    copies = load_chunks(chunks, kv, sems)
    fill_places(pk, inv)
    for copy in copies:
        copy.wait()
    row = iota((128, 512), 0)
    col = iota((128, 512), 1)
    lane = iota((128, 128), 1)

    def one(slot, carry):
        logical = pk[0, slot_of(slot)]
        user, first, blocks, tail = user_of(ub, tl, logical)
        own = logical - first
        query = q_ref[slot, :128]

        def step(j, acc):
            places = [inv[first + jnp.minimum(4 * j + i, own)] for i in range(4)]
            keys = jnp.concatenate([kv[p, 0] for p in places], axis=0)
            values = jnp.concatenate([kv[p, 1] for p in places], axis=0)
            logits = dot(query, keys, 1, 1) * SCALE
            silu = logits / (1.0 + jnp.exp(-logits))
            weights = jnp.where(col + (4 * j - own) * 128 <= row, silu, 0.0).astype(BF16)
            return acc + dot(weights, values, 1, 0)

        acc = lax.fori_loop(0, own // 4 + 1, step, jnp.zeros((128, 128), F32))
        limit = jnp.where(own == blocks - 1, tail, 128)
        valid = iota((128, 128), 0) < limit
        att = jnp.where(valid, acc, 0.0)
        att_ref[slot] = att
        grad = jnp.where(valid, gm_ref[slot] * gate_ref[slot].astype(F32), 0.0)
        mean = jnp.mean(att, axis=1, keepdims=True)
        centered = att - mean
        spread = jnp.sum(centered * centered, axis=1, keepdims=True)
        total = jnp.sum(grad, axis=1, keepdims=True)
        cross = jnp.sum(grad * centered, axis=1, keepdims=True)
        stats = jnp.where(
            lane == 0, mean, jnp.where(lane == 1, spread, jnp.where(lane == 2, total, cross))
        )
        stat_ref[slot] = stats.T[:8]
        return carry

    lax.fori_loop(0, 4, one, 0)


def norm_kernel(
    ub, tl, pk, att_ref, s0, s1, s2, s3, gate_ref, gm_ref, da_ref, gg_ref, mixed_ref
):
    line = iota((128, 128), 0)
    for slot in range(4):
        user, first, blocks, tail = user_of(ub, tl, pk[0, slot_of(slot)])
        own = pk[0, slot_of(slot)] - first
        limit = jnp.where(own == blocks - 1, tail, 128)
        valid = line < limit
        stats = [s[slot ^ e] for e, s in enumerate((s0, s1, s2, s3))]
        mean = (stats[0][0:1] + stats[1][0:1] + stats[2][0:1] + stats[3][0:1]) * 0.25
        var = jnp.zeros((1, 128), F32)
        total = jnp.zeros((1, 128), F32)
        cross = jnp.zeros((1, 128), F32)
        for stat in stats:
            away = stat[0:1] - mean
            var = var + stat[1:2] + 128.0 * away * away
            total = total + stat[2:3]
            cross = cross + stat[3:4] + away * stat[2:3]
        inv_std = lax.rsqrt(var * (1.0 / 512) + EPS)
        rows = jnp.where(
            line == 0,
            mean,
            jnp.where(
                line == 1,
                inv_std,
                jnp.where(line == 2, total * (1.0 / 512), cross * inv_std * (1.0 / 512)),
            ),
        ).T
        mean, inv_std, total, cross = (rows[:, i : i + 1] for i in range(4))
        normed = (att_ref[slot] - mean) * inv_std
        gate = gate_ref[slot].astype(F32)
        gmix = jnp.where(valid, gm_ref[slot], 0.0)
        da = (gmix * gate - total - normed * cross) * inv_std
        da_ref[slot] = jnp.where(valid, da, 0.0).astype(BF16)
        gg_ref[slot] = (gmix * normed).astype(BF16)
        mixed_ref[pl.ds(slot * 128, 128), :] = jnp.where(valid, normed * gate, 0.0).astype(BF16)


def weight_kernel(mixed_ref, c0, c1, c2, c3, gw_ref):
    for part in range(4):
        term = jnp.zeros((128, 256), F32)
        for d, cot in enumerate((c0, c1, c2, c3)):
            term = term + dot(mixed_ref[pl.ds(d * 128, 128), :], cot[:, pl.ds(part * 256, 256)], 0, 0)
        term = term.astype(BF16)
        for r in range(8):
            for c in range(2):
                gw_ref[r * 8 + part * 2 + c] = term[r * 16 : r * 16 + 16, c * 128 : c * 128 + 128]


def score_kernel(ub, tl, pk, mixed_ref, cand_ref, *rest):
    chunks, (sc_ref,), (qp, sems) = rest[:8], rest[8:9], rest[9:]
    copies = load_chunks(chunks, qp, sems)
    row = iota((32, 128), 0)
    for copy in copies:
        copy.wait()
    table = jnp.concatenate([qp[p, 128:160] for p in range(32)], axis=0).T
    for slot in range(4):
        user = user_of(ub, tl, pk[0, slot_of(slot)])[0]
        cand = jnp.broadcast_to(cand_ref[pl.ds(user, 1), :], (32, 128))
        pick = jnp.concatenate(
            [(cand - slot_of(p) * 32 == row).astype(F32).astype(BF16) for p in range(32)], axis=0
        )
        chosen = dot(table, pick, 1, 0).astype(BF16)
        sc_ref[slot] = dot(mixed_ref[pl.ds(slot * 128, 128), :], chosen, 1, 0).astype(BF16)


def query_kernel(ub, tl, pk, q_ref, da_ref, gg_ref, sc_ref, *rest):
    chunks, outs, (kv, gq, inv, sems) = rest[:8], rest[8:12], rest[12:]
    copies = load_chunks(chunks, kv, sems)
    fill_places(pk, inv)
    for copy in copies:
        copy.wait()
    row = iota((128, 512), 0)
    col = iota((128, 512), 1)

    def one(slot, carry):
        logical = pk[0, slot_of(slot)]
        first = user_of(ub, tl, logical)[1]
        own = logical - first
        query = q_ref[slot, :128]
        grad = da_ref[slot]

        def step(j, acc):
            places = [inv[first + jnp.minimum(4 * j + i, own)] for i in range(4)]
            keys = jnp.concatenate([kv[p, 0] for p in places], axis=0)
            values = jnp.concatenate([kv[p, 1] for p in places], axis=0)
            logits = dot(query, keys, 1, 1) * SCALE
            slopes = dot(grad, values, 1, 1)
            sigma = 1.0 / (1.0 + jnp.exp(-logits))
            slope = sigma * (1.0 + logits * (1.0 - sigma))
            ds = jnp.where(col + (4 * j - own) * 128 <= row, slopes * slope, 0.0).astype(BF16)
            return acc + dot(ds, keys, 1, 0)

        acc = lax.fori_loop(0, own // 4 + 1, step, jnp.zeros((128, 128), F32))
        gq[slot] = (acc * SCALE).astype(BF16)
        return carry

    lax.fori_loop(0, 4, one, 0)
    for slot in range(4):
        outs[slot][0] = gq[slot]
        outs[slot][1] = gg_ref[slot]
        outs[slot][2] = sc_ref[slot]


def key_kernel(ub, tl, pk, kv_ref, *rest):
    qs, das, outs, (qbuf, dbuf, both, inv, qsems, dsems) = (
        rest[:8], rest[8:16], rest[16:20], rest[20:],
    )
    copies = load_chunks(qs, qbuf, qsems) + load_chunks(das, dbuf, dsems)
    fill_places(pk, inv)
    for copy in copies:
        copy.wait()
    row = iota((128, 512), 0)
    col = iota((128, 512), 1)

    def one(slot, carry):
        logical = pk[0, slot_of(slot)]
        user, first, blocks, tail = user_of(ub, tl, logical)
        count = first + blocks - logical
        key = kv_ref[slot, 0]
        value = kv_ref[slot, 1]

        def step(j, carry):
            gk, gv = carry
            places = [inv[logical + jnp.minimum(4 * j + i, count - 1)] for i in range(4)]
            queries = jnp.concatenate([qbuf[p, :128] for p in places], axis=0)
            grads = jnp.concatenate([dbuf[p] for p in places], axis=0)
            logits = dot(key, queries, 1, 1) * SCALE
            slopes = dot(value, grads, 1, 1)
            sigma = 1.0 / (1.0 + jnp.exp(-logits))
            silu = logits * sigma
            slope = sigma * (1.0 + logits * (1.0 - sigma))
            later = col + j * 512
            allowed = (later >= row) & (later < count * 128)
            weights = jnp.where(allowed, silu, 0.0).astype(BF16)
            ds = jnp.where(allowed, slopes * slope, 0.0).astype(BF16)
            return gk + dot(ds, queries, 1, 0), gv + dot(weights, grads, 1, 0)

        zero = jnp.zeros((128, 128), F32)
        gk, gv = lax.fori_loop(0, (count + 3) // 4, step, (zero, zero))
        both[slot, 0] = (gk * SCALE).astype(BF16)
        both[slot, 1] = gv.astype(BF16)
        return carry

    lax.fori_loop(0, 4, one, 0)
    for slot in range(4):
        outs[slot][...] = both[slot]


def unpack_early_kernel(p0, p1, p2, p3, gq_ref, gg_ref, sc_ref):
    scores = jnp.zeros((128, 128), F32)
    for d, piece in enumerate((p0, p1, p2, p3)):
        gq_ref[:, head_columns(d)] = piece[0]
        gg_ref[:, head_columns(d)] = piece[1]
        scores = scores + piece[2].astype(F32)
    sc_ref[...] = scores


def unpack_late_kernel(p0, p1, p2, p3, gk_ref, gv_ref):
    for d, piece in enumerate((p0, p1, p2, p3)):
        gk_ref[:, head_columns(d)] = piece[0]
        gv_ref[:, head_columns(d)] = piece[1]


def sum_kernel(parts_ref, out_ref):
    total = jnp.sum(parts_ref[...].astype(F32), axis=0).astype(BF16)
    for i in range(8):
        out_ref[i] = total


def spread_kernel(line_ref, out_ref):
    for i in range(16):
        out_ref[i] = line_ref[...]


def assemble_kernel(own_ref, far_ref, out_ref):
    me = lax.axis_index("core")
    for r in range(8):
        for xl in range(2):
            for z in range(8):
                own = own_ref[r * 2 + xl, z].astype(F32)
                far = far_ref[r * 2 + xl, z].astype(F32)
                for core in range(2):
                    rows = pl.ds((xl * 2 + core) * 128 + r * 16, 16)
                    out_ref[rows, pl.ds(z * 128, 128)] = jnp.where(me == core, own, far)


def call(kernel, ins, outs, scratch=(), us=2, mib=8):
    return pl.pallas_call(
        kernel,
        in_specs=[spec for spec, _ in ins],
        out_specs=[VM] * len(outs),
        out_shape=[jax.ShapeDtypeStruct(shape, kind) for shape, kind in outs],
        scratch_shapes=list(scratch),
        compiler_params=pltpu.CompilerParams(vmem_limit_bytes=mib << 20),
        cost_estimate=pl.CostEstimate(
            flops=us * 1000000000, bytes_accessed=us * 1000000, transcendentals=0
        ),
    )(*[value for _, value in ins])


def flip(array, axis):
    return lax.ppermute(array, axis, [(0, 1), (1, 0)])


def ring(array):
    up, down = [array], [array]
    for step in range(4):
        up.append(lax.ppermute(up[-1], "z", [(i, (i + 1) % 8) for i in range(8)]))
        if step < 3:
            down.append(lax.ppermute(down[-1], "z", [(i, (i + 7) % 8) for i in range(8)]))
    return up + down[:0:-1]


def after(value, *waits):
    return lax.optimization_barrier((value,) + waits)[0]


def vm(*arrays):
    return [(VM, a) for a in arrays]


def raw(arrays):
    return [(HBM, pltpu.with_memory_space_constraint(a, pltpu.HBM)) for a in arrays]


def swap(pieces):
    both = lax.ppermute(pieces[3], ("xl", "core"), [(i, 3 - i) for i in range(4)])
    return [pieces[0], flip(pieces[1], "core"), flip(pieces[2], "xl"), both]


def body(
    query, key, value, gate, out_weight, items, cotangent, user_blocks, tail_rows, packing, cand_ids
):
    facts = [(SM, user_blocks), (SM, tail_rows), (SM, packing)]
    block = (4, 128, 128)
    places = pltpu.SMEM((32,), I32)
    sems = pltpu.SemaphoreType.DMA((8,))
    kv_buffer = pltpu.VMEM((32, 2, 128, 128), BF16)
    table = dot(items, out_weight, 1, 1).astype(BF16)
    packed = call(
        pack_kernel,
        raw([key, value, query, gate]) + vm(table),
        [((544, 128), BF16)] * 4,
        [pltpu.VMEM((4, 128, 512), BF16), pltpu.SemaphoreType.DMA((4,))],
    )
    first = swap(packed)
    kv, qp, gate_h = call(
        merge_kernel,
        vm(*first),
        [((4, 2, 128, 128), BF16), ((4, 160, 128), BF16), (block, BF16)],
    )
    kvs = ring(kv)
    cots = [cotangent] + swap([after(cotangent, packed[0])] * 4)[1:]
    (gm,) = call(
        mixed_grad_kernel,
        vm(*cots) + raw([out_weight]),
        [(block, F32)],
        [pltpu.VMEM((128, 1024), BF16), pltpu.SemaphoreType.DMA],
    )
    att, stats = call(
        forward_kernel,
        facts + vm(qp, gate_h, gm) + raw(kvs),
        [(block, F32), ((4, 8, 128), F32)],
        [kv_buffer, places, sems],
        us=6,
    )
    qps = ring(after(qp, kvs[3], kvs[5]))
    stats = after(stats, qps[1], qps[7])
    all_stats = swap([stats] * 4)
    da, gg, mixed = call(
        norm_kernel,
        facts + vm(after(att, qps[2], qps[6]), *all_stats, gate_h, gm),
        [(block, BF16), (block, BF16), ((512, 128), BF16)],
    )
    das = ring(da)
    (gw,) = call(weight_kernel, vm(mixed, *cots), [((64, 16, 128), BF16)])
    parts = lax.all_to_all(after(gw, qps[3], qps[5], das[1], das[7]), ("xh", "y", "z"), split_axis=0, concat_axis=0, tiled=True)
    (sc,) = call(
        score_kernel,
        facts + vm(mixed, cand_ids[0]) + raw(qps),
        [(block, BF16)],
        [pltpu.VMEM((32, 160, 128), BF16), sems],
    )
    early = call(
        query_kernel,
        facts + vm(qp, da, gg, sc) + raw(kvs),
        [((3, 128, 128), BF16)] * 4,
        [kv_buffer, pltpu.VMEM(block, BF16), places, sems],
        us=6,
    )
    early = swap(early)
    (piece,) = call(sum_kernel, vm(parts), [((8, 16, 128), BF16)])
    line = lax.all_to_all(piece, "z", split_axis=0, concat_axis=0, tiled=True)
    (lines,) = call(spread_kernel, vm(line), [((16, 8, 16, 128), BF16)])
    near = lax.all_to_all(lines, ("xh", "y", "xl"), split_axis=0, concat_axis=0, tiled=True)
    late = call(
        key_kernel,
        facts + vm(kv) + raw(qps) + raw(das),
        [((2, 128, 128), BF16)] * 4,
        [
            pltpu.VMEM((32, 160, 128), BF16),
            pltpu.VMEM((32, 128, 128), BF16),
            pltpu.VMEM((4, 2, 128, 128), BF16),
            places,
            sems,
            sems,
        ],
        us=8,
        mib=12,
    )
    late = swap(late)
    far = flip(near, "core")
    (gow,) = call(assemble_kernel, vm(near, far), [((512, 1024), F32)])
    rows = (128, 512)
    gq, gg, scores = call(
        unpack_early_kernel, vm(*early), [(rows, BF16), (rows, BF16), ((128, 128), F32)]
    )
    gk, gv = call(unpack_late_kernel, vm(*late), [(rows, BF16)] * 2)
    return (scores, gq, gk, gv, gg, gow)


def solution(mesh):
    inner = Mesh(mesh.devices.reshape(SIZES), AXES)
    rows = P(DP + CTX, None)
    in_specs = (
        rows, rows, rows, rows, P(), P(CTX, None), rows,
        P(DP, None), P(DP, None), P(DP, None), P(DP, None, None),
    )
    out_specs = (rows, rows, rows, rows, rows, P())
    return jax.shard_map(body, mesh=inner, in_specs=in_specs, out_specs=out_specs, check_vma=False)
```

```python
import jax
import jax.numpy as jnp
from jax import lax
from jax.experimental import pallas as pl
from jax.experimental.pallas import tpu as pltpu
from jax.sharding import Mesh, PartitionSpec as P

AXES = ("xh", "y", "xl", "z", "core")
SIZES = (2, 4, 2, 8, 2)
DP = ("xh", "y")
CTX = ("xl", "z", "core")
SCALE = 128 ** (-0.5)
EPS = 1e-05
F32 = jnp.float32
BF16 = jnp.bfloat16
I32 = jnp.int32

VM = pl.BlockSpec(memory_space=pltpu.VMEM)
SM = pl.BlockSpec(memory_space=pltpu.SMEM)
HBM = pl.BlockSpec(memory_space=pltpu.HBM)


def dot(a, b, ca, cb):
    return lax.dot_general(a, b, (((ca,), (cb,)), ((), ())), preferred_element_type=F32)


def slot_of(place):
    down, other = place // 4, place % 4
    xl = (lax.axis_index("xl") + other // 2) % 2
    z = (lax.axis_index("z") + 8 - down) % 8
    core = (lax.axis_index("core") + other) % 2
    return xl * 16 + z * 2 + core


def fill_places(pk_ref, inv_ref):
    def one(place, carry):
        inv_ref[pk_ref[0, slot_of(place)]] = place
        return carry

    lax.fori_loop(0, 32, one, 0)


def user_of(ub_ref, tl_ref, logical):
    end0 = ub_ref[0, 0]
    end1 = end0 + ub_ref[0, 1]
    end2 = end1 + ub_ref[0, 2]
    user = (
        (logical >= end0).astype(I32) + (logical >= end1).astype(I32) + (logical >= end2).astype(I32)
    )
    first = jnp.where(user == 0, 0, jnp.where(user == 1, end0, jnp.where(user == 2, end1, end2)))
    return user, first, ub_ref[0, user], tl_ref[0, user]


def load_chunks(refs, buffer, sems):
    copies = [
        pltpu.make_async_copy(ref, buffer.at[pl.ds(4 * i, 4)], sems.at[i]) for i, ref in enumerate(refs)
    ]
    for copy in copies:
        copy.start()
    return copies


def iota(shape, axis):
    return lax.broadcasted_iota(I32, shape, axis)


def head_columns(other):
    xl = (lax.axis_index("xl") + other // 2) % 2
    core = (lax.axis_index("core") + other) % 2
    return pl.ds(pl.multiple_of((xl * 2 + core) * 128, 128), 128)


def pack_kernel(
    k_ref, v_ref, q_ref, g_ref, i_ref, w_ref, o0, o1, o2, o3, rows, items, weight, side, sems
):
    copies = [
        pltpu.make_async_copy(ref, to, sems.at[i])
        for i, (ref, to) in enumerate(
            (
                (k_ref, rows.at[0]),
                (v_ref, rows.at[1]),
                (q_ref, rows.at[2]),
                (g_ref, rows.at[3]),
                (i_ref, items),
                (w_ref, weight),
            )
        )
    ]
    for copy in copies:
        copy.start()
    outs = (o0, o1, o2, o3)
    for i in range(4):
        copies[i].wait()
        for d, out in enumerate(outs):
            out[i * 128 : i * 128 + 128] = rows[i, :, head_columns(d)]
    copies[4].wait()
    copies[5].wait()
    side[...] = dot(items[...], weight[...], 1, 1).astype(BF16)
    for d, out in enumerate(outs):
        out[512:] = side[:, head_columns(d)]


def mixed_grad_kernel(c0, c1, c2, c3, w_ref, gm_ref, wbuf, sem):
    copy = pltpu.make_async_copy(
        w_ref.at[head_columns(0)], wbuf, sem
    )
    copy.start()
    copy.wait()
    for d, cot in enumerate((c0, c1, c2, c3)):
        gm_ref[d] = dot(cot[...], wbuf[...], 1, 1)


def merge_kernel(p0, p1, p2, p3, kv_ref, qp_ref, gate_ref):
    for d, piece in enumerate((p0, p1, p2, p3)):
        kv_ref[d, 0] = piece[:128]
        kv_ref[d, 1] = piece[128:256]
        qp_ref[d, :128] = piece[256:384]
        qp_ref[d, 128:] = piece[512:]
        gate_ref[d] = piece[384:512]


def masked_step(query, kv, spots, reach, acc):
    keys = jnp.concatenate([kv[p, 0] for p in spots], axis=0)
    values = jnp.concatenate([kv[p, 1] for p in spots], axis=0)
    row = iota((128, 128), 0) - iota((128, 128), 1)
    logits = dot(query, keys, 1, 1) * SCALE
    silu = logits / (1.0 + jnp.exp(-logits))
    weights = [
        jnp.where(row >= reach[i] * 128, silu[:, i * 128 : i * 128 + 128], 0.0).astype(BF16)
        for i in range(4)
    ]
    return acc + dot(jnp.concatenate(weights, axis=1), values, 1, 0)


def forward_near_kernel(ub, tl, pk, q_ref, *rest):
    chunks, (att_ref,), (kv, inv, sems) = rest[:7], rest[7:8], rest[8:]
    copies = [
        pltpu.make_async_copy(ref, kv.at[pl.ds(4 * c, 4)], sems.at[c])
        for c, ref in zip((0, 1, 2, 3, 5, 6, 7), chunks)
    ]
    for copy in copies:
        copy.start()
    fill_places(pk, inv)
    for copy in copies:
        copy.wait()

    def one(slot, carry):
        logical = pk[0, slot_of(slot)]
        first = user_of(ub, tl, logical)[1]
        own = logical - first
        query = q_ref[slot, :128]

        def step(j, acc):
            spots, reach = [], []
            for i in range(4):
                entry = 4 * j + i
                place = inv[first + jnp.minimum(entry, own)]
                late = (place // 4 == 4) | (entry > own)
                spots.append(jnp.where(late, 0, place))
                reach.append(jnp.where(late, 1, jnp.where(entry == own, 0, -1)))
            return masked_step(query, kv, spots, reach, acc)

        att_ref[slot] = lax.fori_loop(0, own // 4 + 1, step, jnp.zeros((128, 128), F32))
        return carry

    lax.fori_loop(0, 4, one, 0)


def forward_far_kernel(
    ub, tl, pk, q_ref, gate_ref, gm_ref, near_ref, kv, att_ref, stat_ref
):
    lane = iota((128, 128), 1)

    def one(slot, carry):
        logical = pk[0, slot_of(slot)]
        user, first, blocks, tail = user_of(ub, tl, logical)
        own = logical - first
        reach = []
        for i in range(4):
            other = pk[0, slot_of(16 + i)]
            reach.append(jnp.where((other >= first) & (other < logical), -1, 1))
        acc = masked_step(q_ref[slot, :128], kv, range(4), reach, near_ref[slot])
        limit = jnp.where(own == blocks - 1, tail, 128)
        valid = iota((128, 128), 0) < limit
        att = jnp.where(valid, acc, 0.0)
        att_ref[slot] = att
        grad = jnp.where(valid, gm_ref[slot] * gate_ref[slot].astype(F32), 0.0)
        mean = jnp.mean(att, axis=1, keepdims=True)
        centered = att - mean
        spread = jnp.sum(centered * centered, axis=1, keepdims=True)
        total = jnp.sum(grad, axis=1, keepdims=True)
        cross = jnp.sum(grad * centered, axis=1, keepdims=True)
        stats = jnp.where(
            lane == 0, mean, jnp.where(lane == 1, spread, jnp.where(lane == 2, total, cross))
        )
        stat_ref[slot] = stats.T[:8]
        return carry

    lax.fori_loop(0, 4, one, 0)


def norm_kernel(
    ub, tl, pk, att_ref, s0, s1, s2, s3, gate_ref, gm_ref, da_ref, gg_ref, mixed_ref
):
    line = iota((128, 128), 0)
    for slot in range(4):
        user, first, blocks, tail = user_of(ub, tl, pk[0, slot_of(slot)])
        own = pk[0, slot_of(slot)] - first
        limit = jnp.where(own == blocks - 1, tail, 128)
        valid = line < limit
        stats = [s[slot ^ e] for e, s in enumerate((s0, s1, s2, s3))]
        mean = (stats[0][0:1] + stats[1][0:1] + stats[2][0:1] + stats[3][0:1]) * 0.25
        var = jnp.zeros((1, 128), F32)
        total = jnp.zeros((1, 128), F32)
        cross = jnp.zeros((1, 128), F32)
        for stat in stats:
            away = stat[0:1] - mean
            var = var + stat[1:2] + 128.0 * away * away
            total = total + stat[2:3]
            cross = cross + stat[3:4] + away * stat[2:3]
        inv_std = lax.rsqrt(var * (1.0 / 512) + EPS)
        rows = jnp.where(
            line == 0,
            mean,
            jnp.where(
                line == 1,
                inv_std,
                jnp.where(line == 2, total * (1.0 / 512), cross * inv_std * (1.0 / 512)),
            ),
        ).T
        mean, inv_std, total, cross = (rows[:, i : i + 1] for i in range(4))
        normed = (att_ref[slot] - mean) * inv_std
        gate = gate_ref[slot].astype(F32)
        gmix = jnp.where(valid, gm_ref[slot], 0.0)
        da = (gmix * gate - total - normed * cross) * inv_std
        da_ref[slot] = jnp.where(valid, da, 0.0).astype(BF16)
        gg_ref[slot] = (gmix * normed).astype(BF16)
        mixed_ref[pl.ds(slot * 128, 128), :] = jnp.where(valid, normed * gate, 0.0).astype(BF16)


def weight_kernel(mixed_ref, c0, c1, c2, c3, gw_ref):
    for part in range(4):
        term = jnp.zeros((128, 256), F32)
        for d, cot in enumerate((c0, c1, c2, c3)):
            term = term + dot(mixed_ref[pl.ds(d * 128, 128), :], cot[:, pl.ds(part * 256, 256)], 0, 0)
        term = term.astype(BF16)
        for r in range(8):
            for c in range(2):
                gw_ref[r * 8 + part * 2 + c] = term[r * 16 : r * 16 + 16, c * 128 : c * 128 + 128]


def score_kernel(ub, tl, pk, mixed_ref, cand_ref, *rest):
    chunks, (sc_ref,), (qp, sems) = rest[:8], rest[8:9], rest[9:]
    copies = load_chunks(chunks, qp, sems)
    row = iota((32, 128), 0)
    for copy in copies:
        copy.wait()
    table = jnp.concatenate([qp[p, 128:160] for p in range(32)], axis=0).T
    for slot in range(4):
        user = user_of(ub, tl, pk[0, slot_of(slot)])[0]
        cand = jnp.broadcast_to(cand_ref[pl.ds(user, 1), :], (32, 128))
        pick = jnp.concatenate(
            [(cand - slot_of(p) * 32 == row).astype(F32).astype(BF16) for p in range(32)], axis=0
        )
        chosen = dot(table, pick, 1, 0).astype(BF16)
        sc_ref[slot] = dot(mixed_ref[pl.ds(slot * 128, 128), :], chosen, 1, 0).astype(BF16)


def query_kernel(ub, tl, pk, q_ref, da_ref, gg_ref, *rest):
    chunks, outs, (kv, gq, inv, sems) = rest[:8], rest[8:12], rest[12:]
    copies = load_chunks(chunks, kv, sems)
    fill_places(pk, inv)
    for copy in copies:
        copy.wait()
    row = iota((128, 512), 0)
    col = iota((128, 512), 1)

    def one(slot, carry):
        logical = pk[0, slot_of(slot)]
        first = user_of(ub, tl, logical)[1]
        own = logical - first
        query = q_ref[slot, :128]
        grad = da_ref[slot]

        def step(j, acc):
            places = [inv[first + jnp.minimum(4 * j + i, own)] for i in range(4)]
            keys = jnp.concatenate([kv[p, 0] for p in places], axis=0)
            values = jnp.concatenate([kv[p, 1] for p in places], axis=0)
            logits = dot(query, keys, 1, 1) * SCALE
            slopes = dot(grad, values, 1, 1)
            sigma = 1.0 / (1.0 + jnp.exp(-logits))
            slope = sigma * (1.0 + logits * (1.0 - sigma))
            ds = jnp.where(col + (4 * j - own) * 128 <= row, slopes * slope, 0.0).astype(BF16)
            return acc + dot(ds, keys, 1, 0)

        acc = lax.fori_loop(0, own // 4 + 1, step, jnp.zeros((128, 128), F32))
        gq[slot] = (acc * SCALE).astype(BF16)
        return carry

    lax.fori_loop(0, 4, one, 0)
    for slot in range(4):
        outs[slot][0] = gq[slot]
        outs[slot][1] = gg_ref[slot]


def key_kernel(ub, tl, pk, kv_ref, sc_ref, *rest):
    qs, das, outs, (qbuf, dbuf, both, inv, qsems, dsems) = (
        rest[:8], rest[8:16], rest[16:20], rest[20:],
    )
    copies = load_chunks(qs, qbuf, qsems) + load_chunks(das, dbuf, dsems)
    fill_places(pk, inv)
    for copy in copies:
        copy.wait()
    row = iota((128, 512), 0)
    col = iota((128, 512), 1)

    def one(slot, carry):
        logical = pk[0, slot_of(slot)]
        user, first, blocks, tail = user_of(ub, tl, logical)
        count = first + blocks - logical
        key = kv_ref[slot, 0]
        value = kv_ref[slot, 1]

        def step(j, carry):
            gk, gv = carry
            places = [inv[logical + jnp.minimum(4 * j + i, count - 1)] for i in range(4)]
            queries = jnp.concatenate([qbuf[p, :128] for p in places], axis=0)
            grads = jnp.concatenate([dbuf[p] for p in places], axis=0)
            logits = dot(key, queries, 1, 1) * SCALE
            slopes = dot(value, grads, 1, 1)
            sigma = 1.0 / (1.0 + jnp.exp(-logits))
            silu = logits * sigma
            slope = sigma * (1.0 + logits * (1.0 - sigma))
            later = col + j * 512
            allowed = (later >= row) & (later < count * 128)
            weights = jnp.where(allowed, silu, 0.0).astype(BF16)
            ds = jnp.where(allowed, slopes * slope, 0.0).astype(BF16)
            return gk + dot(ds, queries, 1, 0), gv + dot(weights, grads, 1, 0)

        zero = jnp.zeros((128, 128), F32)
        gk, gv = lax.fori_loop(0, (count + 3) // 4, step, (zero, zero))
        both[slot, 0] = (gk * SCALE).astype(BF16)
        both[slot, 1] = gv.astype(BF16)
        return carry

    lax.fori_loop(0, 4, one, 0)
    for slot in range(4):
        outs[slot][:2] = both[slot]
        outs[slot][2] = sc_ref[slot]


def unpack_early_kernel(p0, p1, p2, p3, gq_ref, gg_ref):
    for d, piece in enumerate((p0, p1, p2, p3)):
        gq_ref[:, head_columns(d)] = piece[0]
        gg_ref[:, head_columns(d)] = piece[1]


def unpack_late_kernel(p0, p1, p2, p3, gk_ref, gv_ref, sc_ref):
    scores = jnp.zeros((128, 128), F32)
    for d, piece in enumerate((p0, p1, p2, p3)):
        gk_ref[:, head_columns(d)] = piece[0]
        gv_ref[:, head_columns(d)] = piece[1]
        scores = scores + piece[2].astype(F32)
    sc_ref[...] = scores


def sum_kernel(parts_ref, out_ref):
    total = jnp.sum(parts_ref[...].astype(F32), axis=0).astype(BF16)
    for i in range(8):
        out_ref[i] = total


def spread_kernel(line_ref, out_ref):
    for i in range(16):
        out_ref[i] = line_ref[...]


def assemble_kernel(own_ref, far_ref, out_ref):
    me = lax.axis_index("core")
    for r in range(8):
        for xl in range(2):
            for z in range(8):
                own = own_ref[r * 2 + xl, z].astype(F32)
                far = far_ref[r * 2 + xl, z].astype(F32)
                for core in range(2):
                    rows = pl.ds((xl * 2 + core) * 128 + r * 16, 16)
                    out_ref[rows, pl.ds(z * 128, 128)] = jnp.where(me == core, own, far)


def call(kernel, ins, outs, scratch=(), us=2, mib=8):
    return pl.pallas_call(
        kernel,
        in_specs=[spec for spec, _ in ins],
        out_specs=[VM] * len(outs),
        out_shape=[jax.ShapeDtypeStruct(shape, kind) for shape, kind in outs],
        scratch_shapes=list(scratch),
        compiler_params=pltpu.CompilerParams(vmem_limit_bytes=mib << 20),
        cost_estimate=pl.CostEstimate(
            flops=us * 1000000000, bytes_accessed=us * 1000000, transcendentals=0
        ),
    )(*[value for _, value in ins])


def flip(array, axis):
    return lax.ppermute(array, axis, [(0, 1), (1, 0)])


def up(array):
    return lax.ppermute(array, "z", [(i, (i + 1) % 8) for i in range(8)])


def down(array):
    return lax.ppermute(array, "z", [(i, (i + 7) % 8) for i in range(8)])


def ring(array, hold):
    ups, downs = [array], [array]
    for n in range(4):
        waits = hold(n)
        ups.append(up(after(ups[-1], *waits) if waits else ups[-1]))
        if n < 3:
            downs.append(down(after(downs[-1], *waits) if waits else downs[-1]))
    return ups + downs[:0:-1]


def after(value, *waits):
    return lax.optimization_barrier((value,) + waits)[0]


def vm(*arrays):
    return [(VM, a) for a in arrays]


def raw(arrays):
    return [(HBM, pltpu.with_memory_space_constraint(a, pltpu.HBM)) for a in arrays]


def swap(pieces):
    both = lax.ppermute(pieces[3], ("xl", "core"), [(i, 3 - i) for i in range(4)])
    return [pieces[0], flip(pieces[1], "core"), flip(pieces[2], "xl"), both]


def body(
    query, key, value, gate, out_weight, items, cotangent, user_blocks, tail_rows, packing, cand_ids
):
    facts = [(SM, user_blocks), (SM, tail_rows), (SM, packing)]
    block = (4, 128, 128)
    places = pltpu.SMEM((32,), I32)
    sems = pltpu.SemaphoreType.DMA((8,))
    kv_buffer = pltpu.VMEM((32, 2, 128, 128), BF16)
    packed = call(
        pack_kernel,
        raw([key, value, query, gate, items, out_weight]),
        [((544, 128), BF16)] * 4,
        [
            pltpu.VMEM((4, 128, 512), BF16),
            pltpu.VMEM((32, 1024), BF16),
            pltpu.VMEM((512, 1024), BF16),
            pltpu.VMEM((32, 512), BF16),
            pltpu.SemaphoreType.DMA((6,)),
        ],
    )
    first = swap(packed)
    kv, qp, gate_h = call(
        merge_kernel,
        vm(*first),
        [((4, 2, 128, 128), BF16), ((4, 160, 128), BF16), (block, BF16)],
    )
    cots = [cotangent] + swap([after(cotangent, first[2])] * 4)[1:]
    kvs = ring(kv, lambda n: cots[1:] if n == 2 else [])
    (gm,) = call(
        mixed_grad_kernel,
        vm(*cots) + raw([out_weight]),
        [(block, F32)],
        [pltpu.VMEM((128, 1024), BF16), pltpu.SemaphoreType.DMA],
    )
    (att_near,) = call(
        forward_near_kernel,
        facts + vm(qp) + raw(kvs[:4] + kvs[5:]),
        [(block, F32)],
        [kv_buffer, places, sems],
        us=6,
    )
    att, stats = call(
        forward_far_kernel,
        facts + vm(qp, gate_h, gm, att_near, kvs[4]),
        [(block, F32), ((4, 8, 128), F32)],
    )
    qps = ring(after(qp, kvs[3], kvs[5]), lambda n: [])
    stats = after(stats, qps[1], qps[7])
    all_stats = swap([stats] * 4)
    da, gg, mixed = call(
        norm_kernel,
        facts + vm(after(att, qps[2], qps[6]), *all_stats, gate_h, gm),
        [(block, BF16), (block, BF16), ((512, 128), BF16)],
    )
    (gw,) = call(weight_kernel, vm(mixed, *cots), [((64, 16, 128), BF16)])
    early = call(
        query_kernel,
        facts + vm(qp, da, gg) + raw(kvs),
        [((2, 128, 128), BF16)] * 4,
        [kv_buffer, pltpu.VMEM(block, BF16), places, sems],
        us=6,
    )
    first_up, first_down = up(da), down(da)
    parts = lax.all_to_all(
        after(gw, qps[3], qps[5], first_up, first_down),
        ("xh", "y", "z"),
        split_axis=0,
        concat_axis=0,
        tiled=True,
    )
    ups, downs = [da, first_up, up(first_up)], [da, first_down, down(first_down)]
    (piece,) = call(
        sum_kernel, vm(after(parts, ups[2], downs[2], early[0])), [((8, 16, 128), BF16)]
    )
    ups.append(up(after(ups[2], early[0])))
    downs.append(down(after(downs[2], early[0])))
    ups.append(up(ups[3]))
    das = ups + downs[:0:-1]
    (sc,) = call(
        score_kernel,
        facts + vm(mixed, cand_ids[0]) + raw(qps),
        [(block, BF16)],
        [pltpu.VMEM((32, 160, 128), BF16), sems],
    )
    early = swap(early)
    line = lax.all_to_all(piece, "z", split_axis=0, concat_axis=0, tiled=True)
    (lines,) = call(
        spread_kernel, vm(after(line, ups[3], downs[3], sc)), [((16, 8, 16, 128), BF16)]
    )
    near = lax.all_to_all(
        after(lines, ups[4]), ("xh", "y", "xl"), split_axis=0, concat_axis=0, tiled=True
    )
    late = call(
        key_kernel,
        facts + vm(kv, sc) + raw(qps) + raw(das),
        [((3, 128, 128), BF16)] * 4,
        [
            pltpu.VMEM((32, 160, 128), BF16),
            pltpu.VMEM((32, 128, 128), BF16),
            pltpu.VMEM((4, 2, 128, 128), BF16),
            places,
            sems,
            sems,
        ],
        us=8,
        mib=12,
    )
    late = swap(late)
    far = flip(after(near, late[0]), "core")
    (gow,) = call(assemble_kernel, vm(near, far), [((512, 1024), F32)])
    rows = (128, 512)
    gq, gg = call(unpack_early_kernel, vm(*early), [(rows, BF16)] * 2)
    gk, gv, scores = call(
        unpack_late_kernel, vm(*late), [(rows, BF16), (rows, BF16), ((128, 128), F32)]
    )
    return (scores, gq, gk, gv, gg, gow)


def solution(mesh):
    inner = Mesh(mesh.devices.reshape(SIZES), AXES)
    rows = P(DP + CTX, None)
    in_specs = (
        rows, rows, rows, rows, P(), P(CTX, None), rows,
        P(DP, None), P(DP, None), P(DP, None), P(DP, None, None),
    )
    out_specs = (rows, rows, rows, rows, rows, P())
    return jax.shard_map(body, mesh=inner, in_specs=in_specs, out_specs=out_specs, check_vma=False)
```

```python
import functools

import jax
import jax.numpy as jnp
from jax import lax
from jax.experimental import pallas as pl
from jax.experimental.pallas import tpu as pltpu
from jax.sharding import Mesh, PartitionSpec as P

AXES = ("xh", "y", "xl", "z", "core")
SIZES = (2, 4, 2, 8, 2)
DP = ("xh", "y")
CTX = ("xl", "z", "core")
SCALE = 128 ** (-0.5)
EPS = 1e-05
F32 = jnp.float32
BF16 = jnp.bfloat16
I32 = jnp.int32

VM = pl.BlockSpec(memory_space=pltpu.VMEM)
SM = pl.BlockSpec(memory_space=pltpu.SMEM)
HBM = pl.BlockSpec(memory_space=pltpu.HBM)


def dot(a, b, ca, cb):
    return lax.dot_general(a, b, (((ca,), (cb,)), ((), ())), preferred_element_type=F32)


def slot_of(place):
    down, other = place // 4, place % 4
    xl = (lax.axis_index("xl") + other // 2) % 2
    z = (lax.axis_index("z") + 8 - down) % 8
    core = (lax.axis_index("core") + other) % 2
    return xl * 16 + z * 2 + core


def fill_places(pk_ref, inv_ref):
    def one(place, carry):
        inv_ref[pk_ref[0, slot_of(place)]] = place
        return carry

    lax.fori_loop(0, 32, one, 0)


def user_of(ub_ref, tl_ref, logical):
    end0 = ub_ref[0, 0]
    end1 = end0 + ub_ref[0, 1]
    end2 = end1 + ub_ref[0, 2]
    user = (
        (logical >= end0).astype(I32) + (logical >= end1).astype(I32) + (logical >= end2).astype(I32)
    )
    first = jnp.where(user == 0, 0, jnp.where(user == 1, end0, jnp.where(user == 2, end1, end2)))
    return user, first, ub_ref[0, user], tl_ref[0, user]


def load_chunks(refs, buffer, sems):
    copies = [
        pltpu.make_async_copy(ref, buffer.at[pl.ds(4 * i, 4)], sems.at[i]) for i, ref in enumerate(refs)
    ]
    for copy in copies:
        copy.start()
    return copies


def iota(shape, axis):
    return lax.broadcasted_iota(I32, shape, axis)


def head_columns(other):
    xl = (lax.axis_index("xl") + other // 2) % 2
    core = (lax.axis_index("core") + other) % 2
    return pl.ds(pl.multiple_of((xl * 2 + core) * 128, 128), 128)


def pack_kernel(
    k_ref, v_ref, q_ref, g_ref, i_ref, w_ref, o0, o1, o2, o3, rows, items, weight, side, sems
):
    copies = [
        pltpu.make_async_copy(ref, to, sems.at[i])
        for i, (ref, to) in enumerate(
            (
                (k_ref, rows.at[0]),
                (v_ref, rows.at[1]),
                (q_ref, rows.at[2]),
                (g_ref, rows.at[3]),
                (i_ref, items),
                (w_ref, weight),
            )
        )
    ]
    for copy in copies:
        copy.start()
    outs = (o0, o1, o2, o3)
    for i in range(4):
        copies[i].wait()
        for d, out in enumerate(outs):
            out[i * 128 : i * 128 + 128] = rows[i, :, head_columns(d)]
    copies[4].wait()
    copies[5].wait()
    side[...] = dot(items[...], weight[...], 1, 1).astype(BF16)
    for d, out in enumerate(outs):
        out[512:] = side[:, head_columns(d)]


def mixed_grad_kernel(c0, c1, c2, c3, w_ref, gm_ref, wbuf, sem):
    copy = pltpu.make_async_copy(
        w_ref.at[head_columns(0)], wbuf, sem
    )
    copy.start()
    copy.wait()
    for d, cot in enumerate((c0, c1, c2, c3)):
        gm_ref[d] = dot(cot[...], wbuf[...], 1, 1)


def merge_kernel(p0, p1, p2, p3, kv_ref, qp_ref, gate_ref):
    for d, piece in enumerate((p0, p1, p2, p3)):
        kv_ref[d, 0] = piece[:128]
        kv_ref[d, 1] = piece[128:256]
        qp_ref[d, :128] = piece[256:384]
        qp_ref[d, 128:] = piece[512:]
        gate_ref[d] = piece[384:512]


def masked_step(query, kv, spots, reach, acc):
    keys = jnp.concatenate([kv[p, 0] for p in spots], axis=0)
    values = jnp.concatenate([kv[p, 1] for p in spots], axis=0)
    row = iota((128, 128), 0) - iota((128, 128), 1)
    logits = dot(query, keys, 1, 1) * SCALE
    silu = logits / (1.0 + jnp.exp(-logits))
    weights = [
        jnp.where(row >= reach[i] * 128, silu[:, i * 128 : i * 128 + 128], 0.0).astype(BF16)
        for i in range(4)
    ]
    return acc + dot(jnp.concatenate(weights, axis=1), values, 1, 0)


def forward_near_kernel(ub, tl, pk, q_ref, *rest):
    chunks, (att_ref,), (kv, inv, sems) = rest[:7], rest[7:8], rest[8:]
    copies = [
        pltpu.make_async_copy(ref, kv.at[pl.ds(4 * c, 4)], sems.at[c])
        for c, ref in zip((0, 1, 2, 3, 5, 6, 7), chunks)
    ]
    for copy in copies:
        copy.start()
    fill_places(pk, inv)
    for copy in copies:
        copy.wait()

    def one(slot, carry):
        logical = pk[0, slot_of(slot)]
        first = user_of(ub, tl, logical)[1]
        own = logical - first
        query = q_ref[slot, :128]

        def step(j, acc):
            spots, reach = [], []
            for i in range(4):
                entry = 4 * j + i
                place = inv[first + jnp.minimum(entry, own)]
                late = (place // 4 == 4) | (entry > own)
                spots.append(jnp.where(late, 0, place))
                reach.append(jnp.where(late, 1, jnp.where(entry == own, 0, -1)))
            return masked_step(query, kv, spots, reach, acc)

        att_ref[slot] = lax.fori_loop(0, own // 4 + 1, step, jnp.zeros((128, 128), F32))
        return carry

    lax.fori_loop(0, 4, one, 0)


def forward_far_kernel(
    ub, tl, pk, q_ref, gate_ref, gm_ref, near_ref, kv, att_ref, stat_ref
):
    lane = iota((128, 128), 1)

    def one(slot, carry):
        logical = pk[0, slot_of(slot)]
        user, first, blocks, tail = user_of(ub, tl, logical)
        own = logical - first
        reach = []
        for i in range(4):
            other = pk[0, slot_of(16 + i)]
            reach.append(jnp.where((other >= first) & (other < logical), -1, 1))
        acc = masked_step(q_ref[slot, :128], kv, range(4), reach, near_ref[slot])
        limit = jnp.where(own == blocks - 1, tail, 128)
        valid = iota((128, 128), 0) < limit
        att = jnp.where(valid, acc, 0.0)
        att_ref[slot] = att
        grad = jnp.where(valid, gm_ref[slot] * gate_ref[slot].astype(F32), 0.0)
        mean = jnp.mean(att, axis=1, keepdims=True)
        centered = att - mean
        spread = jnp.sum(centered * centered, axis=1, keepdims=True)
        total = jnp.sum(grad, axis=1, keepdims=True)
        cross = jnp.sum(grad * centered, axis=1, keepdims=True)
        stats = jnp.where(
            lane == 0, mean, jnp.where(lane == 1, spread, jnp.where(lane == 2, total, cross))
        )
        stat_ref[slot] = stats.T[:8]
        return carry

    lax.fori_loop(0, 4, one, 0)


def norm_kernel(
    ub, tl, pk, att_ref, s0, s1, s2, s3, gate_ref, gm_ref, da_ref, gg_ref, mixed_ref
):
    line = iota((128, 128), 0)
    for slot in range(4):
        user, first, blocks, tail = user_of(ub, tl, pk[0, slot_of(slot)])
        own = pk[0, slot_of(slot)] - first
        limit = jnp.where(own == blocks - 1, tail, 128)
        valid = line < limit
        stats = [s[slot ^ e] for e, s in enumerate((s0, s1, s2, s3))]
        mean = (stats[0][0:1] + stats[1][0:1] + stats[2][0:1] + stats[3][0:1]) * 0.25
        var = jnp.zeros((1, 128), F32)
        total = jnp.zeros((1, 128), F32)
        cross = jnp.zeros((1, 128), F32)
        for stat in stats:
            away = stat[0:1] - mean
            var = var + stat[1:2] + 128.0 * away * away
            total = total + stat[2:3]
            cross = cross + stat[3:4] + away * stat[2:3]
        inv_std = lax.rsqrt(var * (1.0 / 512) + EPS)
        rows = jnp.where(
            line == 0,
            mean,
            jnp.where(
                line == 1,
                inv_std,
                jnp.where(line == 2, total * (1.0 / 512), cross * inv_std * (1.0 / 512)),
            ),
        ).T
        mean, inv_std, total, cross = (rows[:, i : i + 1] for i in range(4))
        normed = (att_ref[slot] - mean) * inv_std
        gate = gate_ref[slot].astype(F32)
        gmix = jnp.where(valid, gm_ref[slot], 0.0)
        da = (gmix * gate - total - normed * cross) * inv_std
        da_ref[slot] = jnp.where(valid, da, 0.0).astype(BF16)
        gg_ref[slot] = (gmix * normed).astype(BF16)
        mixed_ref[pl.ds(slot * 128, 128), :] = jnp.where(valid, normed * gate, 0.0).astype(BF16)


def weight_kernel(mixed_ref, c0, c1, c2, c3, gw_ref):
    for part in range(4):
        term = jnp.zeros((128, 256), F32)
        for d, cot in enumerate((c0, c1, c2, c3)):
            term = term + dot(mixed_ref[pl.ds(d * 128, 128), :], cot[:, pl.ds(part * 256, 256)], 0, 0)
        gw_ref[2 * part] = term[:, :128].astype(BF16)
        gw_ref[2 * part + 1] = term[:, 128:].astype(BF16)


def score_kernel(ub, tl, pk, mixed_ref, cand_ref, *rest):
    chunks, (sc_ref,), (qp, sems) = rest[:8], rest[8:9], rest[9:]
    copies = load_chunks(chunks, qp, sems)
    row = iota((32, 128), 0)
    for copy in copies:
        copy.wait()
    table = jnp.concatenate([qp[p, 128:160] for p in range(32)], axis=0).T
    for slot in range(4):
        user = user_of(ub, tl, pk[0, slot_of(slot)])[0]
        cand = jnp.broadcast_to(cand_ref[pl.ds(user, 1), :], (32, 128))
        pick = jnp.concatenate(
            [(cand - slot_of(p) * 32 == row).astype(F32).astype(BF16) for p in range(32)], axis=0
        )
        chosen = dot(table, pick, 1, 0).astype(BF16)
        sc_ref[slot] = dot(mixed_ref[pl.ds(slot * 128, 128), :], chosen, 1, 0).astype(BF16)


def query_kernel(ub, tl, pk, q_ref, da_ref, gg_ref, *rest):
    chunks, outs, (kv, gq, inv, sems) = rest[:8], rest[8:12], rest[12:]
    copies = load_chunks(chunks, kv, sems)
    fill_places(pk, inv)
    for copy in copies:
        copy.wait()
    row = iota((128, 512), 0)
    col = iota((128, 512), 1)

    def one(slot, carry):
        logical = pk[0, slot_of(slot)]
        first = user_of(ub, tl, logical)[1]
        own = logical - first
        query = q_ref[slot, :128]
        grad = da_ref[slot]

        def step(j, acc):
            places = [inv[first + jnp.minimum(4 * j + i, own)] for i in range(4)]
            keys = jnp.concatenate([kv[p, 0] for p in places], axis=0)
            values = jnp.concatenate([kv[p, 1] for p in places], axis=0)
            logits = dot(query, keys, 1, 1) * SCALE
            slopes = dot(grad, values, 1, 1)
            sigma = 1.0 / (1.0 + jnp.exp(-logits))
            slope = sigma * (1.0 + logits * (1.0 - sigma))
            ds = jnp.where(col + (4 * j - own) * 128 <= row, slopes * slope, 0.0).astype(BF16)
            return acc + dot(ds, keys, 1, 0)

        acc = lax.fori_loop(0, own // 4 + 1, step, jnp.zeros((128, 128), F32))
        gq[slot] = (acc * SCALE).astype(BF16)
        return carry

    lax.fori_loop(0, 4, one, 0)
    for slot in range(4):
        outs[slot][0] = gq[slot]
        outs[slot][1] = gg_ref[slot]


def key_step(key, value, queries, grads, reach, carry):
    gk, gv = carry
    col = iota((128, 128), 1) - iota((128, 128), 0)
    logits = dot(key, queries, 1, 1) * SCALE
    slopes = dot(value, grads, 1, 1)
    sigma = 1.0 / (1.0 + jnp.exp(-logits))
    silu = logits * sigma
    change = slopes * (sigma * (1.0 + logits * (1.0 - sigma)))
    weights, ds = [], []
    for i in range(4):
        cols = slice(i * 128, i * 128 + 128)
        allowed = col >= reach[i] * 128
        weights.append(jnp.where(allowed, silu[:, cols], 0.0).astype(BF16))
        ds.append(jnp.where(allowed, change[:, cols], 0.0).astype(BF16))
    gk = gk + dot(jnp.concatenate(ds, axis=1), queries, 1, 0)
    gv = gv + dot(jnp.concatenate(weights, axis=1), grads, 1, 0)
    return gk, gv


def key_near_kernel(ub, tl, pk, kv_ref, *rest):
    qs, das, (sum_ref,), (qbuf, dbuf, inv, sems) = rest[:7], rest[7:14], rest[14:15], rest[15:]
    copies = []
    for i, c in enumerate((0, 1, 2, 3, 5, 6, 7)):
        copies.append(pltpu.make_async_copy(qs[i], qbuf.at[pl.ds(4 * c, 4)], sems.at[i]))
        copies.append(pltpu.make_async_copy(das[i], dbuf.at[pl.ds(4 * c, 4)], sems.at[7 + i]))
    for copy in copies:
        copy.start()
    fill_places(pk, inv)
    for copy in copies:
        copy.wait()

    def one(slot, carry):
        logical = pk[0, slot_of(slot)]
        user, first, blocks, tail = user_of(ub, tl, logical)
        count = first + blocks - logical

        def step(j, carry):
            spots, reach = [], []
            for i in range(4):
                entry = 4 * j + i
                place = inv[logical + jnp.minimum(entry, count - 1)]
                late = (place // 4 == 4) | (entry >= count)
                spots.append(jnp.where(late, 0, place))
                reach.append(jnp.where(late, 1, jnp.where(entry == 0, 0, -1)))
            queries = jnp.concatenate([qbuf[p, :128] for p in spots], axis=0)
            grads = jnp.concatenate([dbuf[p] for p in spots], axis=0)
            return key_step(kv_ref[slot, 0], kv_ref[slot, 1], queries, grads, reach, carry)

        zero = jnp.zeros((128, 128), F32)
        gk, gv = lax.fori_loop(0, (count + 3) // 4, step, (zero, zero))
        sum_ref[slot, 0] = gk
        sum_ref[slot, 1] = gv
        return carry

    lax.fori_loop(0, 4, one, 0)


def key_far_kernel(ub, tl, pk, kv_ref, near_ref, q_ref, da_ref, sc_ref, o0, o1, o2, o3, both):
    def one(slot, carry):
        logical = pk[0, slot_of(slot)]
        user, first, blocks, tail = user_of(ub, tl, logical)
        reach = []
        for i in range(4):
            other = pk[0, slot_of(16 + i)]
            reach.append(jnp.where((other > logical) & (other < first + blocks), -1, 1))
        queries = jnp.concatenate([q_ref[i, :128] for i in range(4)], axis=0)
        grads = jnp.concatenate([da_ref[i] for i in range(4)], axis=0)
        gk, gv = key_step(
            kv_ref[slot, 0], kv_ref[slot, 1], queries, grads, reach,
            (near_ref[slot, 0], near_ref[slot, 1]),
        )
        both[slot, 0] = (gk * SCALE).astype(BF16)
        both[slot, 1] = gv.astype(BF16)
        return carry

    lax.fori_loop(0, 4, one, 0)
    for slot, out in enumerate((o0, o1, o2, o3)):
        out[:2] = both[slot]
        out[2] = sc_ref[slot]


def unpack_early_kernel(p0, p1, p2, p3, gq_ref, gg_ref):
    for d, piece in enumerate((p0, p1, p2, p3)):
        gq_ref[:, head_columns(d)] = piece[0]
        gg_ref[:, head_columns(d)] = piece[1]


def unpack_late_kernel(p0, p1, p2, p3, gk_ref, gv_ref, sc_ref):
    scores = jnp.zeros((128, 128), F32)
    for d, piece in enumerate((p0, p1, p2, p3)):
        gk_ref[:, head_columns(d)] = piece[0]
        gv_ref[:, head_columns(d)] = piece[1]
        scores = scores + piece[2].astype(F32)
    sc_ref[...] = scores


def sum_kernel(copies, parts_ref, out_ref):
    total = jnp.sum(parts_ref[...].astype(F32), axis=0).astype(BF16)
    for i in range(copies):
        out_ref[i] = total


def assemble_kernel(own_ref, far_ref, out_ref):
    me = lax.axis_index("core")
    for group in range(8):
        for xl in range(2):
            own = own_ref[group * 2 + xl].astype(F32)
            far = far_ref[group * 2 + xl].astype(F32)
            for core in range(2):
                rows = pl.ds((xl * 2 + core) * 128, 128)
                out_ref[rows, pl.ds(group * 128, 128)] = jnp.where(me == core, own, far)


def call(kernel, ins, outs, scratch=(), us=2, mib=8):
    return pl.pallas_call(
        kernel,
        in_specs=[spec for spec, _ in ins],
        out_specs=[VM] * len(outs),
        out_shape=[jax.ShapeDtypeStruct(shape, kind) for shape, kind in outs],
        scratch_shapes=list(scratch),
        compiler_params=pltpu.CompilerParams(vmem_limit_bytes=mib << 20),
        cost_estimate=pl.CostEstimate(
            flops=us * 1000000000, bytes_accessed=us * 1000000, transcendentals=0
        ),
    )(*[value for _, value in ins])


def flip(array, axis):
    return lax.ppermute(array, axis, [(0, 1), (1, 0)])


def up(array):
    return lax.ppermute(array, "z", [(i, (i + 1) % 8) for i in range(8)])


def down(array):
    return lax.ppermute(array, "z", [(i, (i + 7) % 8) for i in range(8)])


def ring(array, hold):
    ups, downs = [array], [array]
    for n in range(4):
        waits = hold(n)
        ups.append(up(after(ups[-1], *waits) if waits else ups[-1]))
        if n < 3:
            downs.append(down(after(downs[-1], *waits) if waits else downs[-1]))
    return ups + downs[:0:-1]


def after(value, *waits):
    return lax.optimization_barrier((value,) + waits)[0]


def vm(*arrays):
    return [(VM, a) for a in arrays]


def raw(arrays):
    return [(HBM, pltpu.with_memory_space_constraint(a, pltpu.HBM)) for a in arrays]


def swap(pieces):
    both = lax.ppermute(pieces[3], ("xl", "core"), [(i, 3 - i) for i in range(4)])
    return [pieces[0], flip(pieces[1], "core"), flip(pieces[2], "xl"), both]


def body(
    query, key, value, gate, out_weight, items, cotangent, user_blocks, tail_rows, packing, cand_ids
):
    facts = [(SM, user_blocks), (SM, tail_rows), (SM, packing)]
    block = (4, 128, 128)
    places = pltpu.SMEM((32,), I32)
    sems = pltpu.SemaphoreType.DMA((8,))
    kv_buffer = pltpu.VMEM((32, 2, 128, 128), BF16)
    packed = call(
        pack_kernel,
        raw([key, value, query, gate, items, out_weight]),
        [((544, 128), BF16)] * 4,
        [
            pltpu.VMEM((4, 128, 512), BF16),
            pltpu.VMEM((32, 1024), BF16),
            pltpu.VMEM((512, 1024), BF16),
            pltpu.VMEM((32, 512), BF16),
            pltpu.SemaphoreType.DMA((6,)),
        ],
    )
    first = swap(packed)
    kv, qp, gate_h = call(
        merge_kernel,
        vm(*first),
        [((4, 2, 128, 128), BF16), ((4, 160, 128), BF16), (block, BF16)],
    )
    cots = [cotangent] + swap([after(cotangent, first[2])] * 4)[1:]
    kvs = ring(kv, lambda n: cots[1:] if n == 2 else [])
    (gm,) = call(
        mixed_grad_kernel,
        vm(*cots) + raw([out_weight]),
        [(block, F32)],
        [pltpu.VMEM((128, 1024), BF16), pltpu.SemaphoreType.DMA],
    )
    (att_near,) = call(
        forward_near_kernel,
        facts + vm(qp) + raw(kvs[:4] + kvs[5:]),
        [(block, F32)],
        [kv_buffer, places, sems],
        us=6,
    )
    att, stats = call(
        forward_far_kernel,
        facts + vm(qp, gate_h, gm, att_near, kvs[4]),
        [(block, F32), ((4, 8, 128), F32)],
    )
    qps = ring(after(qp, kvs[4]), lambda n: [])
    all_stats = swap([stats] * 4)
    da, gg, mixed = call(
        norm_kernel,
        facts + vm(after(att, qps[1], qps[7]), *all_stats, gate_h, gm),
        [(block, BF16), (block, BF16), ((512, 128), BF16)],
    )
    (gw,) = call(weight_kernel, vm(mixed, *cots), [((8, 128, 128), BF16)])
    early = call(
        query_kernel,
        facts + vm(qp, da, gg) + raw(kvs),
        [((2, 128, 128), BF16)] * 4,
        [kv_buffer, pltpu.VMEM(block, BF16), places, sems],
        us=6,
    )
    parts = lax.all_to_all(gw, ("xh", "y"), split_axis=0, concat_axis=0, tiled=True)
    ups, downs = [da, up(da)], [da, down(da)]
    (piece,) = call(
        functools.partial(sum_kernel, 8),
        vm(after(parts, ups[1], downs[1], qps[2], qps[6], early[0])),
        [((8, 128, 128), BF16)],
    )
    line = lax.all_to_all(piece, "z", split_axis=0, concat_axis=0, tiled=True)
    ups.append(up(after(ups[1], early[0])))
    downs.append(down(after(downs[1], early[0])))
    ups.append(up(ups[2]))
    downs.append(down(downs[2]))
    ups.append(up(ups[3]))
    das = ups + downs[:0:-1]
    (sc,) = call(
        score_kernel,
        facts + vm(mixed, cand_ids[0]) + raw(qps),
        [(block, BF16)],
        [pltpu.VMEM((32, 160, 128), BF16), sems],
    )
    early = swap(early)
    (lines,) = call(
        functools.partial(sum_kernel, 16),
        vm(after(line, ups[2], downs[2], *early[1:])),
        [((16, 128, 128), BF16)],
    )
    near = lax.all_to_all(lines, ("xh", "y", "xl"), split_axis=0, concat_axis=0, tiled=True)
    (key_sums,) = call(
        key_near_kernel,
        facts + vm(kv) + raw(qps[:4] + qps[5:]) + raw(das[:4] + das[5:]),
        [((4, 2, 128, 128), F32)],
        [
            pltpu.VMEM((32, 160, 128), BF16),
            pltpu.VMEM((32, 128, 128), BF16),
            places,
            pltpu.SemaphoreType.DMA((14,)),
        ],
        us=8,
    )
    late = call(
        key_far_kernel,
        facts + vm(kv, key_sums, qps[4], das[4], sc),
        [((3, 128, 128), BF16)] * 4,
        [pltpu.VMEM((4, 2, 128, 128), BF16)],
        us=3,
    )
    late = swap(late)
    far = flip(after(near, *late[1:]), "core")
    (gow,) = call(assemble_kernel, vm(near, far), [((512, 1024), F32)])
    rows = (128, 512)
    gq, gg = call(unpack_early_kernel, vm(*early), [(rows, BF16)] * 2)
    gk, gv, scores = call(
        unpack_late_kernel, vm(*late), [(rows, BF16), (rows, BF16), ((128, 128), F32)]
    )
    return (scores, gq, gk, gv, gg, gow)


def solution(mesh):
    inner = Mesh(mesh.devices.reshape(SIZES), AXES)
    rows = P(DP + CTX, None)
    in_specs = (
        rows, rows, rows, rows, P(), P(CTX, None), rows,
        P(DP, None), P(DP, None), P(DP, None), P(DP, None, None),
    )
    out_specs = (rows, rows, rows, rows, rows, P())
    return jax.shard_map(body, mesh=inner, in_specs=in_specs, out_specs=out_specs, check_vma=False)
```

```python
import functools

import jax
import jax.numpy as jnp
from jax import lax
from jax.experimental import pallas as pl
from jax.experimental.pallas import tpu as pltpu
from jax.sharding import Mesh, PartitionSpec as P

AXES = ("xh", "y", "xl", "z", "core")
SIZES = (2, 4, 2, 8, 2)
DP = ("xh", "y")
CTX = ("xl", "z", "core")
SCALE = 128 ** (-0.5)
EPS = 1e-05
F32 = jnp.float32
BF16 = jnp.bfloat16
I32 = jnp.int32

VM = pl.BlockSpec(memory_space=pltpu.VMEM)
SM = pl.BlockSpec(memory_space=pltpu.SMEM)
HBM = pl.BlockSpec(memory_space=pltpu.HBM)


def dot(a, b, ca, cb):
    return lax.dot_general(a, b, (((ca,), (cb,)), ((), ())), preferred_element_type=F32)


def slot_of(place):
    down, other = place // 4, place % 4
    xl = (lax.axis_index("xl") + other // 2) % 2
    z = (lax.axis_index("z") + 8 - down) % 8
    core = (lax.axis_index("core") + other) % 2
    return xl * 16 + z * 2 + core


def fill_places(pk_ref, inv_ref):
    def one(place, carry):
        inv_ref[pk_ref[0, slot_of(place)]] = place
        return carry

    lax.fori_loop(0, 32, one, 0)


def user_of(ub_ref, tl_ref, logical):
    end0 = ub_ref[0, 0]
    end1 = end0 + ub_ref[0, 1]
    end2 = end1 + ub_ref[0, 2]
    user = (
        (logical >= end0).astype(I32) + (logical >= end1).astype(I32) + (logical >= end2).astype(I32)
    )
    first = jnp.where(user == 0, 0, jnp.where(user == 1, end0, jnp.where(user == 2, end1, end2)))
    return user, first, ub_ref[0, user], tl_ref[0, user]


def load_chunks(refs, buffer, sems):
    copies = [
        pltpu.make_async_copy(ref, buffer.at[pl.ds(4 * i, 4)], sems.at[i]) for i, ref in enumerate(refs)
    ]
    for copy in copies:
        copy.start()
    return copies


def iota(shape, axis):
    return lax.broadcasted_iota(I32, shape, axis)


def head_columns(other):
    xl = (lax.axis_index("xl") + other // 2) % 2
    core = (lax.axis_index("core") + other) % 2
    return pl.ds(pl.multiple_of((xl * 2 + core) * 128, 128), 128)


def pack_kernel(
    k_ref, v_ref, q_ref, g_ref, i_ref, w_ref, o0, o1, o2, o3, rows, items, weight, side, sems
):
    copies = [
        pltpu.make_async_copy(ref, to, sems.at[i])
        for i, (ref, to) in enumerate(
            (
                (k_ref, rows.at[0]),
                (v_ref, rows.at[1]),
                (q_ref, rows.at[2]),
                (g_ref, rows.at[3]),
                (i_ref, items),
                (w_ref, weight),
            )
        )
    ]
    for copy in copies:
        copy.start()
    outs = (o0, o1, o2, o3)
    for i in range(4):
        copies[i].wait()
        for d, out in enumerate(outs):
            out[i * 128 : i * 128 + 128] = rows[i, :, head_columns(d)]
    copies[4].wait()
    copies[5].wait()
    side[...] = dot(items[...], weight[...], 1, 1).astype(BF16)
    for d, out in enumerate(outs):
        out[512:] = side[:, head_columns(d)]


def mixed_grad_kernel(c0, c1, c2, c3, w_ref, gm_ref, wbuf, sem):
    copy = pltpu.make_async_copy(
        w_ref.at[head_columns(0)], wbuf, sem
    )
    copy.start()
    copy.wait()
    for d, cot in enumerate((c0, c1, c2, c3)):
        gm_ref[d] = dot(cot[...], wbuf[...], 1, 1)


def merge_kernel(p0, p1, p2, p3, kv_ref, qp_ref, gate_ref):
    for d, piece in enumerate((p0, p1, p2, p3)):
        kv_ref[d, 0] = piece[:128]
        kv_ref[d, 1] = piece[128:256]
        qp_ref[d, :128] = piece[256:384]
        qp_ref[d, 128:] = piece[512:]
        gate_ref[d] = piece[384:512]


def masked_step(query, kv, spots, reach, acc):
    keys = jnp.concatenate([kv[p, 0] for p in spots], axis=0)
    values = jnp.concatenate([kv[p, 1] for p in spots], axis=0)
    row = iota((128, 128), 0) - iota((128, 128), 1)
    logits = dot(query, keys, 1, 1) * SCALE
    silu = logits / (1.0 + jnp.exp(-logits))
    weights = [
        jnp.where(row >= reach[i] * 128, silu[:, i * 128 : i * 128 + 128], 0.0).astype(BF16)
        for i in range(4)
    ]
    return acc + dot(jnp.concatenate(weights, axis=1), values, 1, 0)


def forward_near_kernel(ub, tl, pk, q_ref, *rest):
    chunks, (att_ref,), (kv, inv, sems) = rest[:7], rest[7:8], rest[8:]
    copies = [
        pltpu.make_async_copy(ref, kv.at[pl.ds(4 * c, 4)], sems.at[c])
        for c, ref in zip((0, 1, 2, 3, 5, 6, 7), chunks)
    ]
    for copy in copies:
        copy.start()
    fill_places(pk, inv)
    for copy in copies:
        copy.wait()

    def one(slot, carry):
        logical = pk[0, slot_of(slot)]
        first = user_of(ub, tl, logical)[1]
        own = logical - first
        query = q_ref[slot, :128]

        def step(j, acc):
            spots, reach = [], []
            for i in range(4):
                entry = 4 * j + i
                place = inv[first + jnp.minimum(entry, own)]
                late = (place // 4 == 4) | (entry > own)
                spots.append(jnp.where(late, 0, place))
                reach.append(jnp.where(late, 1, jnp.where(entry == own, 0, -1)))
            return masked_step(query, kv, spots, reach, acc)

        att_ref[slot] = lax.fori_loop(0, own // 4 + 1, step, jnp.zeros((128, 128), F32))
        return carry

    lax.fori_loop(0, 4, one, 0)


def forward_far_kernel(
    ub, tl, pk, q_ref, gate_ref, gm_ref, near_ref, kv, att_ref, stat_ref
):
    lane = iota((128, 128), 1)

    def one(slot, carry):
        logical = pk[0, slot_of(slot)]
        user, first, blocks, tail = user_of(ub, tl, logical)
        own = logical - first
        reach = []
        for i in range(4):
            other = pk[0, slot_of(16 + i)]
            reach.append(jnp.where((other >= first) & (other < logical), -1, 1))
        acc = masked_step(q_ref[slot, :128], kv, range(4), reach, near_ref[slot])
        limit = jnp.where(own == blocks - 1, tail, 128)
        valid = iota((128, 128), 0) < limit
        att = jnp.where(valid, acc, 0.0)
        att_ref[slot] = att
        grad = jnp.where(valid, gm_ref[slot] * gate_ref[slot].astype(F32), 0.0)
        mean = jnp.mean(att, axis=1, keepdims=True)
        centered = att - mean
        spread = jnp.sum(centered * centered, axis=1, keepdims=True)
        total = jnp.sum(grad, axis=1, keepdims=True)
        cross = jnp.sum(grad * centered, axis=1, keepdims=True)
        stats = jnp.where(
            lane == 0, mean, jnp.where(lane == 1, spread, jnp.where(lane == 2, total, cross))
        )
        stat_ref[slot] = stats.T[:8]
        return carry

    lax.fori_loop(0, 4, one, 0)


def norm_kernel(
    ub, tl, pk, att_ref, s0, s1, s2, s3, gate_ref, gm_ref, qp_ref, all_ref, gg_ref, mixed_ref
):
    line = iota((128, 128), 0)
    for slot in range(4):
        user, first, blocks, tail = user_of(ub, tl, pk[0, slot_of(slot)])
        own = pk[0, slot_of(slot)] - first
        limit = jnp.where(own == blocks - 1, tail, 128)
        valid = line < limit
        stats = [s[slot ^ e] for e, s in enumerate((s0, s1, s2, s3))]
        mean = (stats[0][0:1] + stats[1][0:1] + stats[2][0:1] + stats[3][0:1]) * 0.25
        var = jnp.zeros((1, 128), F32)
        total = jnp.zeros((1, 128), F32)
        cross = jnp.zeros((1, 128), F32)
        for stat in stats:
            away = stat[0:1] - mean
            var = var + stat[1:2] + 128.0 * away * away
            total = total + stat[2:3]
            cross = cross + stat[3:4] + away * stat[2:3]
        inv_std = lax.rsqrt(var * (1.0 / 512) + EPS)
        rows = jnp.where(
            line == 0,
            mean,
            jnp.where(
                line == 1,
                inv_std,
                jnp.where(line == 2, total * (1.0 / 512), cross * inv_std * (1.0 / 512)),
            ),
        ).T
        mean, inv_std, total, cross = (rows[:, i : i + 1] for i in range(4))
        normed = (att_ref[slot] - mean) * inv_std
        gate = gate_ref[slot].astype(F32)
        gmix = jnp.where(valid, gm_ref[slot], 0.0)
        da = (gmix * gate - total - normed * cross) * inv_std
        all_ref[slot, :160] = qp_ref[slot]
        all_ref[slot, 160:] = jnp.where(valid, da, 0.0).astype(BF16)
        gg_ref[slot] = (gmix * normed).astype(BF16)
        mixed_ref[pl.ds(slot * 128, 128), :] = jnp.where(valid, normed * gate, 0.0).astype(BF16)


def weight_kernel(mixed_ref, c0, c1, c2, c3, gw_ref):
    for part in range(4):
        term = jnp.zeros((128, 256), F32)
        for d, cot in enumerate((c0, c1, c2, c3)):
            term = term + dot(mixed_ref[pl.ds(d * 128, 128), :], cot[:, pl.ds(part * 256, 256)], 0, 0)
        gw_ref[2 * part] = term[:, :128].astype(BF16)
        gw_ref[2 * part + 1] = term[:, 128:].astype(BF16)


def score_kernel(ub, tl, pk, mixed_ref, cand_ref, *rest):
    chunks, (sc_ref,), (tables, sems) = rest[:8], rest[8:9], rest[9:]
    copies = [
        pltpu.make_async_copy(ref.at[:, pl.ds(128, 32)], tables.at[pl.ds(4 * i, 4)], sems.at[i])
        for i, ref in enumerate(chunks)
    ]
    for copy in copies:
        copy.start()
    row = iota((32, 128), 0)
    for copy in copies:
        copy.wait()
    table = jnp.concatenate([tables[p] for p in range(32)], axis=0).T
    for slot in range(4):
        user = user_of(ub, tl, pk[0, slot_of(slot)])[0]
        cand = jnp.broadcast_to(cand_ref[pl.ds(user, 1), :], (32, 128))
        pick = jnp.concatenate(
            [(cand - slot_of(p) * 32 == row).astype(F32).astype(BF16) for p in range(32)], axis=0
        )
        chosen = dot(table, pick, 1, 0).astype(BF16)
        sc_ref[slot] = dot(mixed_ref[pl.ds(slot * 128, 128), :], chosen, 1, 0).astype(BF16)


def query_kernel(ub, tl, pk, all_ref, gg_ref, *rest):
    chunks, outs, (kv, gq, inv, sems) = rest[:8], rest[8:12], rest[12:]
    copies = load_chunks(chunks, kv, sems)
    fill_places(pk, inv)
    for copy in copies:
        copy.wait()
    row = iota((128, 512), 0)
    col = iota((128, 512), 1)

    def one(slot, carry):
        logical = pk[0, slot_of(slot)]
        first = user_of(ub, tl, logical)[1]
        own = logical - first
        query = all_ref[slot, :128]
        grad = all_ref[slot, 160:]

        def step(j, acc):
            places = [inv[first + jnp.minimum(4 * j + i, own)] for i in range(4)]
            keys = jnp.concatenate([kv[p, 0] for p in places], axis=0)
            values = jnp.concatenate([kv[p, 1] for p in places], axis=0)
            logits = dot(query, keys, 1, 1) * SCALE
            slopes = dot(grad, values, 1, 1)
            sigma = 1.0 / (1.0 + jnp.exp(-logits))
            slope = sigma * (1.0 + logits * (1.0 - sigma))
            ds = jnp.where(col + (4 * j - own) * 128 <= row, slopes * slope, 0.0).astype(BF16)
            return acc + dot(ds, keys, 1, 0)

        acc = lax.fori_loop(0, own // 4 + 1, step, jnp.zeros((128, 128), F32))
        gq[slot] = (acc * SCALE).astype(BF16)
        return carry

    lax.fori_loop(0, 4, one, 0)
    for slot in range(4):
        outs[slot][0] = gq[slot]
        outs[slot][1] = gg_ref[slot]


def key_step(key, value, queries, grads, reach, carry):
    gk, gv = carry
    col = iota((128, 128), 1) - iota((128, 128), 0)
    logits = dot(key, queries, 1, 1) * SCALE
    slopes = dot(value, grads, 1, 1)
    sigma = 1.0 / (1.0 + jnp.exp(-logits))
    silu = logits * sigma
    change = slopes * (sigma * (1.0 + logits * (1.0 - sigma)))
    weights, ds = [], []
    for i in range(4):
        cols = slice(i * 128, i * 128 + 128)
        allowed = col >= reach[i] * 128
        weights.append(jnp.where(allowed, silu[:, cols], 0.0).astype(BF16))
        ds.append(jnp.where(allowed, change[:, cols], 0.0).astype(BF16))
    gk = gk + dot(jnp.concatenate(ds, axis=1), queries, 1, 0)
    gv = gv + dot(jnp.concatenate(weights, axis=1), grads, 1, 0)
    return gk, gv


def key_near_kernel(ub, tl, pk, kv_ref, *rest):
    chunks, (sum_ref,), (buf, inv, sems) = rest[:7], rest[7:8], rest[8:]
    copies = [
        pltpu.make_async_copy(ref, buf.at[pl.ds(4 * c, 4)], sems.at[c])
        for c, ref in zip((0, 1, 2, 3, 5, 6, 7), chunks)
    ]
    for copy in copies:
        copy.start()
    fill_places(pk, inv)
    for copy in copies:
        copy.wait()

    def one(slot, carry):
        logical = pk[0, slot_of(slot)]
        user, first, blocks, tail = user_of(ub, tl, logical)
        count = first + blocks - logical

        def step(j, carry):
            spots, reach = [], []
            for i in range(4):
                entry = 4 * j + i
                place = inv[logical + jnp.minimum(entry, count - 1)]
                late = (place // 4 == 4) | (entry >= count)
                spots.append(jnp.where(late, 0, place))
                reach.append(jnp.where(late, 1, jnp.where(entry == 0, 0, -1)))
            queries = jnp.concatenate([buf[p, :128] for p in spots], axis=0)
            grads = jnp.concatenate([buf[p, 160:] for p in spots], axis=0)
            return key_step(kv_ref[slot, 0], kv_ref[slot, 1], queries, grads, reach, carry)

        zero = jnp.zeros((128, 128), F32)
        gk, gv = lax.fori_loop(0, (count + 3) // 4, step, (zero, zero))
        sum_ref[slot, 0] = gk
        sum_ref[slot, 1] = gv
        return carry

    lax.fori_loop(0, 4, one, 0)


def key_far_kernel(
    ub, tl, pk, kv_ref, near_ref, sc_ref, all_ref, o0, o1, o2, o3, both, buf, sem
):
    copy = pltpu.make_async_copy(all_ref, buf, sem)
    copy.start()
    copy.wait()

    def one(slot, carry):
        logical = pk[0, slot_of(slot)]
        user, first, blocks, tail = user_of(ub, tl, logical)
        reach = []
        for i in range(4):
            other = pk[0, slot_of(16 + i)]
            reach.append(jnp.where((other > logical) & (other < first + blocks), -1, 1))
        queries = jnp.concatenate([buf[i, :128] for i in range(4)], axis=0)
        grads = jnp.concatenate([buf[i, 160:] for i in range(4)], axis=0)
        gk, gv = key_step(
            kv_ref[slot, 0], kv_ref[slot, 1], queries, grads, reach,
            (near_ref[slot, 0], near_ref[slot, 1]),
        )
        both[slot, 0] = (gk * SCALE).astype(BF16)
        both[slot, 1] = gv.astype(BF16)
        return carry

    lax.fori_loop(0, 4, one, 0)
    for slot, out in enumerate((o0, o1, o2, o3)):
        out[:2] = both[slot]
        out[2] = sc_ref[slot]


def unpack_early_kernel(p0, p1, p2, p3, gq_ref, gg_ref):
    for d, piece in enumerate((p0, p1, p2, p3)):
        gq_ref[:, head_columns(d)] = piece[0]
        gg_ref[:, head_columns(d)] = piece[1]


def unpack_late_kernel(p0, p1, p2, p3, gk_ref, gv_ref, sc_ref):
    scores = jnp.zeros((128, 128), F32)
    for d, piece in enumerate((p0, p1, p2, p3)):
        gk_ref[:, head_columns(d)] = piece[0]
        gv_ref[:, head_columns(d)] = piece[1]
        scores = scores + piece[2].astype(F32)
    sc_ref[...] = scores


def sum_kernel(copies, parts_ref, out_ref):
    total = jnp.sum(parts_ref[...].astype(F32), axis=0).astype(BF16)
    for i in range(copies):
        out_ref[i] = total


def assemble_kernel(own_ref, far_ref, out_ref):
    me = lax.axis_index("core")
    for group in range(8):
        for xl in range(2):
            own = own_ref[group * 2 + xl].astype(F32)
            far = far_ref[group * 2 + xl].astype(F32)
            for core in range(2):
                rows = pl.ds((xl * 2 + core) * 128, 128)
                out_ref[rows, pl.ds(group * 128, 128)] = jnp.where(me == core, own, far)


def call(kernel, ins, outs, scratch=(), us=2, mib=8):
    return pl.pallas_call(
        kernel,
        in_specs=[spec for spec, _ in ins],
        out_specs=[VM] * len(outs),
        out_shape=[jax.ShapeDtypeStruct(shape, kind) for shape, kind in outs],
        scratch_shapes=list(scratch),
        compiler_params=pltpu.CompilerParams(vmem_limit_bytes=mib << 20),
        cost_estimate=pl.CostEstimate(
            flops=us * 1000000000, bytes_accessed=us * 1000000, transcendentals=0
        ),
    )(*[value for _, value in ins])


def flip(array, axis):
    return lax.ppermute(array, axis, [(0, 1), (1, 0)])


def up(array):
    return lax.ppermute(array, "z", [(i, (i + 1) % 8) for i in range(8)])


def down(array):
    return lax.ppermute(array, "z", [(i, (i + 7) % 8) for i in range(8)])


def ring(array, hold):
    ups, downs = [array], [array]
    for n in range(4):
        waits = hold(n)
        ups.append(up(after(ups[-1], *waits) if waits else ups[-1]))
        if n < 3:
            downs.append(down(after(downs[-1], *waits) if waits else downs[-1]))
    return ups + downs[:0:-1]


def after(value, *waits):
    return lax.optimization_barrier((value,) + waits)[0]


def vm(*arrays):
    return [(VM, a) for a in arrays]


def raw(arrays):
    return [(HBM, pltpu.with_memory_space_constraint(a, pltpu.HBM)) for a in arrays]


def swap(pieces):
    both = lax.ppermute(pieces[3], ("xl", "core"), [(i, 3 - i) for i in range(4)])
    return [pieces[0], flip(pieces[1], "core"), flip(pieces[2], "xl"), both]


def body(
    query, key, value, gate, out_weight, items, cotangent, user_blocks, tail_rows, packing, cand_ids
):
    facts = [(SM, user_blocks), (SM, tail_rows), (SM, packing)]
    block = (4, 128, 128)
    places = pltpu.SMEM((32,), I32)
    sems = pltpu.SemaphoreType.DMA((8,))
    kv_buffer = pltpu.VMEM((32, 2, 128, 128), BF16)
    packed = call(
        pack_kernel,
        raw([key, value, query, gate, items, out_weight]),
        [((544, 128), BF16)] * 4,
        [
            pltpu.VMEM((4, 128, 512), BF16),
            pltpu.VMEM((32, 1024), BF16),
            pltpu.VMEM((512, 1024), BF16),
            pltpu.VMEM((32, 512), BF16),
            pltpu.SemaphoreType.DMA((6,)),
        ],
    )
    first = swap(packed)
    kv, qp, gate_h = call(
        merge_kernel,
        vm(*first),
        [((4, 2, 128, 128), BF16), ((4, 160, 128), BF16), (block, BF16)],
    )
    cots = [cotangent] + swap([after(cotangent, first[2])] * 4)[1:]
    kvs = ring(kv, lambda n: cots[1:] if n == 2 else [])
    (gm,) = call(
        mixed_grad_kernel,
        vm(*cots) + raw([out_weight]),
        [(block, F32)],
        [pltpu.VMEM((128, 1024), BF16), pltpu.SemaphoreType.DMA],
    )
    (att_near,) = call(
        forward_near_kernel,
        facts + vm(qp) + raw(kvs[:4] + kvs[5:]),
        [(block, F32)],
        [kv_buffer, places, sems],
        us=6,
    )
    att, stats = call(
        forward_far_kernel,
        facts + vm(qp, gate_h, gm, att_near, kvs[4]),
        [(block, F32), ((4, 8, 128), F32)],
    )
    all_stats = swap([stats] * 4)
    both, gg, mixed = call(
        norm_kernel,
        facts + vm(att, *all_stats, gate_h, gm, qp),
        [((4, 288, 128), BF16), (block, BF16), ((512, 128), BF16)],
    )
    (gw,) = call(weight_kernel, vm(mixed, *cots), [((8, 128, 128), BF16)])
    parts = lax.all_to_all(gw, ("xh", "y"), split_axis=0, concat_axis=0, tiled=True)
    ups, downs = [both, up(both)], [both, down(both)]
    early = call(
        query_kernel,
        facts + vm(after(both, ups[1], downs[1]), gg) + raw(kvs),
        [((2, 128, 128), BF16)] * 4,
        [kv_buffer, pltpu.VMEM(block, BF16), places, sems],
        us=8,
    )
    ups.append(up(ups[1]))
    downs.append(down(downs[1]))
    (piece,) = call(
        functools.partial(sum_kernel, 8),
        vm(after(parts, ups[2], downs[2], early[0])),
        [((8, 128, 128), BF16)],
        us=8,
    )
    line = lax.all_to_all(piece, "z", split_axis=0, concat_axis=0, tiled=True)
    ups.append(up(ups[2]))
    downs.append(down(downs[2]))
    ups.append(up(ups[3]))
    pairs = ups + downs[:0:-1]
    (sc,) = call(
        score_kernel,
        facts + vm(mixed, cand_ids[0]) + raw(pairs),
        [(block, BF16)],
        [pltpu.VMEM((32, 32, 128), BF16), sems],
    )
    early = swap(early)
    (lines,) = call(
        functools.partial(sum_kernel, 16),
        vm(after(line, ups[3], downs[3], *early[1:])),
        [((16, 128, 128), BF16)],
    )
    near = lax.all_to_all(lines, ("xh", "y", "xl"), split_axis=0, concat_axis=0, tiled=True)
    (key_sums,) = call(
        key_near_kernel,
        facts + vm(kv) + raw(pairs[:4] + pairs[5:]),
        [((4, 2, 128, 128), F32)],
        [pltpu.VMEM((32, 288, 128), BF16), places, sems],
        us=8,
    )
    late = call(
        key_far_kernel,
        facts + vm(kv, key_sums, sc) + raw([pairs[4]]),
        [((3, 128, 128), BF16)] * 4,
        [
            pltpu.VMEM((4, 2, 128, 128), BF16),
            pltpu.VMEM((4, 288, 128), BF16),
            pltpu.SemaphoreType.DMA,
        ],
        us=3,
    )
    late = swap(late)
    far = flip(after(near, *late[1:]), "core")
    (gow,) = call(assemble_kernel, vm(near, far), [((512, 1024), F32)])
    rows = (128, 512)
    gq, gg = call(unpack_early_kernel, vm(*early), [(rows, BF16)] * 2)
    gk, gv, scores = call(
        unpack_late_kernel, vm(*late), [(rows, BF16), (rows, BF16), ((128, 128), F32)]
    )
    return (scores, gq, gk, gv, gg, gow)


def solution(mesh):
    inner = Mesh(mesh.devices.reshape(SIZES), AXES)
    rows = P(DP + CTX, None)
    in_specs = (
        rows, rows, rows, rows, P(), P(CTX, None), rows,
        P(DP, None), P(DP, None), P(DP, None), P(DP, None, None),
    )
    out_specs = (rows, rows, rows, rows, rows, P())
    return jax.shard_map(body, mesh=inner, in_specs=in_specs, out_specs=out_specs, check_vma=False)
```

```python
import functools

import jax
import jax.numpy as jnp
from jax import lax
from jax.experimental import pallas as pl
from jax.experimental.pallas import tpu as pltpu
from jax.sharding import Mesh, PartitionSpec as P

AXES = ("xh", "y", "xl", "z", "core")
SIZES = (2, 4, 2, 8, 2)
DP = ("xh", "y")
CTX = ("xl", "z", "core")
SCALE = 128 ** (-0.5)
EPS = 1e-05
F32 = jnp.float32
BF16 = jnp.bfloat16
I32 = jnp.int32

VM = pl.BlockSpec(memory_space=pltpu.VMEM)
SM = pl.BlockSpec(memory_space=pltpu.SMEM)
HBM = pl.BlockSpec(memory_space=pltpu.HBM)


def dot(a, b, ca, cb):
    return lax.dot_general(a, b, (((ca,), (cb,)), ((), ())), preferred_element_type=F32)


def slot_of(place):
    down, other = place // 4, place % 4
    xl = (lax.axis_index("xl") + other // 2) % 2
    z = (lax.axis_index("z") + 8 - down) % 8
    core = (lax.axis_index("core") + other) % 2
    return xl * 16 + z * 2 + core


def fill_places(pk_ref, inv_ref):
    def one(place, carry):
        inv_ref[pk_ref[0, slot_of(place)]] = place
        return carry

    lax.fori_loop(0, 32, one, 0)


def user_of(ub_ref, tl_ref, logical):
    end0 = ub_ref[0, 0]
    end1 = end0 + ub_ref[0, 1]
    end2 = end1 + ub_ref[0, 2]
    user = (
        (logical >= end0).astype(I32) + (logical >= end1).astype(I32) + (logical >= end2).astype(I32)
    )
    first = jnp.where(user == 0, 0, jnp.where(user == 1, end0, jnp.where(user == 2, end1, end2)))
    return user, first, ub_ref[0, user], tl_ref[0, user]


def load_chunks(refs, buffer, sems):
    copies = [
        pltpu.make_async_copy(ref, buffer.at[pl.ds(4 * i, 4)], sems.at[i]) for i, ref in enumerate(refs)
    ]
    for copy in copies:
        copy.start()
    return copies


def iota(shape, axis):
    return lax.broadcasted_iota(I32, shape, axis)


def head_columns(other):
    xl = (lax.axis_index("xl") + other // 2) % 2
    core = (lax.axis_index("core") + other) % 2
    return pl.ds(pl.multiple_of((xl * 2 + core) * 128, 128), 128)


def pack_kernel(
    k_ref, v_ref, q_ref, g_ref, i_ref, w_ref, o0, o1, o2, o3, rows, items, weight, side, sems
):
    copies = [
        pltpu.make_async_copy(ref, to, sems.at[i])
        for i, (ref, to) in enumerate(
            (
                (k_ref, rows.at[0]),
                (v_ref, rows.at[1]),
                (q_ref, rows.at[2]),
                (g_ref, rows.at[3]),
                (i_ref, items),
                (w_ref, weight),
            )
        )
    ]
    for copy in copies:
        copy.start()
    outs = (o0, o1, o2, o3)
    for i in range(4):
        copies[i].wait()
        for d, out in enumerate(outs):
            out[i * 128 : i * 128 + 128] = rows[i, :, head_columns(d)]
    copies[4].wait()
    copies[5].wait()
    side[...] = dot(items[...], weight[...], 1, 1).astype(BF16)
    for d, out in enumerate(outs):
        out[512:] = side[:, head_columns(d)]


def mixed_grad_kernel(c0, c1, c2, c3, w_ref, gm_ref, wbuf, sem):
    copy = pltpu.make_async_copy(
        w_ref.at[head_columns(0)], wbuf, sem
    )
    copy.start()
    copy.wait()
    for d, cot in enumerate((c0, c1, c2, c3)):
        gm_ref[d] = dot(cot[...], wbuf[...], 1, 1)


def merge_kernel(p0, p1, p2, p3, kv_ref, qp_ref, gate_ref):
    for d, piece in enumerate((p0, p1, p2, p3)):
        kv_ref[d, 0] = piece[:128]
        kv_ref[d, 1] = piece[128:256]
        qp_ref[d, :128] = piece[256:384]
        qp_ref[d, 128:] = piece[512:]
        gate_ref[d] = piece[384:512]


def masked_step(query, kv, spots, reach, acc):
    keys = jnp.concatenate([kv[p, 0] for p in spots], axis=0)
    values = jnp.concatenate([kv[p, 1] for p in spots], axis=0)
    row = iota((128, 128), 0) - iota((128, 128), 1)
    logits = dot(query, keys, 1, 1) * SCALE
    silu = logits / (1.0 + jnp.exp(-logits))
    weights = [
        jnp.where(row >= reach[i] * 128, silu[:, i * 128 : i * 128 + 128], 0.0).astype(BF16)
        for i in range(4)
    ]
    return acc + dot(jnp.concatenate(weights, axis=1), values, 1, 0)


def forward_near_kernel(ub, tl, pk, q_ref, *rest):
    chunks, (att_ref,), (kv, inv, sems) = rest[:7], rest[7:8], rest[8:]
    copies = [
        pltpu.make_async_copy(ref, kv.at[pl.ds(4 * c, 4)], sems.at[c])
        for c, ref in zip((0, 1, 2, 3, 5, 6, 7), chunks)
    ]
    for copy in copies:
        copy.start()
    fill_places(pk, inv)
    for copy in copies:
        copy.wait()

    def one(slot, carry):
        logical = pk[0, slot_of(slot)]
        first = user_of(ub, tl, logical)[1]
        own = logical - first
        query = q_ref[slot, :128]

        def group(j, acc):
            spots, reach = [], []
            for i in range(4):
                entry = 4 * j + i
                place = inv[first + jnp.minimum(entry, own)]
                late = (place // 4 == 4) | (entry > own)
                spots.append(jnp.where(late, 0, place))
                reach.append(jnp.where(late, 1, jnp.where(entry == own, 0, -1)))
            return masked_step(query, kv, spots, reach, acc)

        def step(j, acc):
            return group(2 * j + 1, group(2 * j, acc))

        att_ref[slot] = lax.fori_loop(0, own // 8 + 1, step, jnp.zeros((128, 128), F32))
        return carry

    lax.fori_loop(0, 4, one, 0)


def forward_far_kernel(
    ub, tl, pk, q_ref, gate_ref, gm_ref, near_ref, kv, att_ref, stat_ref
):
    lane = iota((128, 128), 1)

    for slot in range(4):
        logical = pk[0, slot_of(slot)]
        user, first, blocks, tail = user_of(ub, tl, logical)
        own = logical - first
        reach = []
        for i in range(4):
            other = pk[0, slot_of(16 + i)]
            reach.append(jnp.where((other >= first) & (other < logical), -1, 1))
        acc = masked_step(q_ref[slot, :128], kv, range(4), reach, near_ref[slot])
        limit = jnp.where(own == blocks - 1, tail, 128)
        valid = iota((128, 128), 0) < limit
        att = jnp.where(valid, acc, 0.0)
        att_ref[slot] = att
        grad = jnp.where(valid, gm_ref[slot] * gate_ref[slot].astype(F32), 0.0)
        mean = jnp.mean(att, axis=1, keepdims=True)
        centered = att - mean
        spread = jnp.sum(centered * centered, axis=1, keepdims=True)
        total = jnp.sum(grad, axis=1, keepdims=True)
        cross = jnp.sum(grad * centered, axis=1, keepdims=True)
        stats = jnp.where(
            lane == 0, mean, jnp.where(lane == 1, spread, jnp.where(lane == 2, total, cross))
        )
        stat_ref[slot] = stats.T[:8]


def norm_kernel(
    ub, tl, pk, att_ref, s0, s1, s2, s3, gate_ref, gm_ref, qp_ref, all_ref, gg_ref, mixed_ref
):
    line = iota((128, 128), 0)
    for slot in range(4):
        user, first, blocks, tail = user_of(ub, tl, pk[0, slot_of(slot)])
        own = pk[0, slot_of(slot)] - first
        limit = jnp.where(own == blocks - 1, tail, 128)
        valid = line < limit
        stats = [s[slot ^ e] for e, s in enumerate((s0, s1, s2, s3))]
        mean = (stats[0][0:1] + stats[1][0:1] + stats[2][0:1] + stats[3][0:1]) * 0.25
        var = jnp.zeros((1, 128), F32)
        total = jnp.zeros((1, 128), F32)
        cross = jnp.zeros((1, 128), F32)
        for stat in stats:
            away = stat[0:1] - mean
            var = var + stat[1:2] + 128.0 * away * away
            total = total + stat[2:3]
            cross = cross + stat[3:4] + away * stat[2:3]
        inv_std = lax.rsqrt(var * (1.0 / 512) + EPS)
        rows = jnp.where(
            line == 0,
            mean,
            jnp.where(
                line == 1,
                inv_std,
                jnp.where(line == 2, total * (1.0 / 512), cross * inv_std * (1.0 / 512)),
            ),
        ).T
        mean, inv_std, total, cross = (rows[:, i : i + 1] for i in range(4))
        normed = (att_ref[slot] - mean) * inv_std
        gate = gate_ref[slot].astype(F32)
        gmix = jnp.where(valid, gm_ref[slot], 0.0)
        da = (gmix * gate - total - normed * cross) * inv_std
        all_ref[slot, :160] = qp_ref[slot]
        all_ref[slot, 160:] = jnp.where(valid, da, 0.0).astype(BF16)
        gg_ref[slot] = (gmix * normed).astype(BF16)
        mixed_ref[pl.ds(slot * 128, 128), :] = jnp.where(valid, normed * gate, 0.0).astype(BF16)


def weight_kernel(mixed_ref, c0, c1, c2, c3, gw_ref):
    for part in range(4):
        term = jnp.zeros((128, 256), F32)
        for d, cot in enumerate((c0, c1, c2, c3)):
            term = term + dot(mixed_ref[pl.ds(d * 128, 128), :], cot[:, pl.ds(part * 256, 256)], 0, 0)
        gw_ref[2 * part] = term[:, :128].astype(BF16)
        gw_ref[2 * part + 1] = term[:, 128:].astype(BF16)


def score_kernel(ub, tl, pk, mixed_ref, cand_ref, *rest):
    chunks, (sc_ref,), (tables, sems) = rest[:8], rest[8:9], rest[9:]
    copies = [
        pltpu.make_async_copy(ref.at[:, pl.ds(128, 32)], tables.at[pl.ds(4 * i, 4)], sems.at[i])
        for i, ref in enumerate(chunks)
    ]
    for copy in copies:
        copy.start()
    row = iota((32, 128), 0)
    for copy in copies:
        copy.wait()
    table = jnp.concatenate([tables[p] for p in range(32)], axis=0).T
    for slot in range(4):
        user = user_of(ub, tl, pk[0, slot_of(slot)])[0]
        cand = jnp.broadcast_to(cand_ref[pl.ds(user, 1), :], (32, 128))
        pick = jnp.concatenate(
            [(cand - slot_of(p) * 32 == row).astype(F32).astype(BF16) for p in range(32)], axis=0
        )
        chosen = dot(table, pick, 1, 0).astype(BF16)
        sc_ref[slot] = dot(mixed_ref[pl.ds(slot * 128, 128), :], chosen, 1, 0).astype(BF16)


def query_kernel(ub, tl, pk, all_ref, gg_ref, *rest):
    chunks, outs, (kv, gq, inv, sems) = rest[:8], rest[8:12], rest[12:]
    copies = load_chunks(chunks, kv, sems)
    fill_places(pk, inv)
    for copy in copies:
        copy.wait()
    row = iota((128, 512), 0)
    col = iota((128, 512), 1)

    def one(slot, carry):
        logical = pk[0, slot_of(slot)]
        first = user_of(ub, tl, logical)[1]
        own = logical - first
        query = all_ref[slot, :128]
        grad = all_ref[slot, 160:]

        def group(j, acc):
            places = [inv[first + jnp.minimum(4 * j + i, own)] for i in range(4)]
            keys = jnp.concatenate([kv[p, 0] for p in places], axis=0)
            values = jnp.concatenate([kv[p, 1] for p in places], axis=0)
            logits = dot(query, keys, 1, 1) * SCALE
            slopes = dot(grad, values, 1, 1)
            sigma = 1.0 / (1.0 + jnp.exp(-logits))
            slope = sigma * (1.0 + logits * (1.0 - sigma))
            ds = jnp.where(col + (4 * j - own) * 128 <= row, slopes * slope, 0.0).astype(BF16)
            return acc + dot(ds, keys, 1, 0)

        def step(j, acc):
            return group(2 * j + 1, group(2 * j, acc))

        acc = lax.fori_loop(0, own // 8 + 1, step, jnp.zeros((128, 128), F32))
        gq[slot] = (acc * SCALE).astype(BF16)
        return carry

    lax.fori_loop(0, 4, one, 0)
    for slot in range(4):
        outs[slot][0] = gq[slot]
        outs[slot][1] = gg_ref[slot]


def key_step(key, value, queries, grads, reach, carry):
    gk, gv = carry
    col = iota((128, 128), 1) - iota((128, 128), 0)
    logits = dot(key, queries, 1, 1) * SCALE
    slopes = dot(value, grads, 1, 1)
    sigma = 1.0 / (1.0 + jnp.exp(-logits))
    silu = logits * sigma
    change = slopes * (sigma * (1.0 + logits * (1.0 - sigma)))
    weights, ds = [], []
    for i in range(4):
        cols = slice(i * 128, i * 128 + 128)
        allowed = col >= reach[i] * 128
        weights.append(jnp.where(allowed, silu[:, cols], 0.0).astype(BF16))
        ds.append(jnp.where(allowed, change[:, cols], 0.0).astype(BF16))
    gk = gk + dot(jnp.concatenate(ds, axis=1), queries, 1, 0)
    gv = gv + dot(jnp.concatenate(weights, axis=1), grads, 1, 0)
    return gk, gv


def key_near_kernel(ub, tl, pk, kv_hbm, *rest):
    chunks, (sum_ref,), (kv_ref, buf, inv, sems) = rest[:7], rest[7:8], rest[8:]
    copies = [
        pltpu.make_async_copy(ref, buf.at[pl.ds(4 * c, 4)], sems.at[c])
        for c, ref in zip((0, 1, 2, 3, 5, 6, 7), chunks)
    ]
    copies.append(pltpu.make_async_copy(kv_hbm, kv_ref, sems.at[4]))
    for copy in copies:
        copy.start()
    fill_places(pk, inv)
    for copy in copies:
        copy.wait()

    def one(slot, carry):
        logical = pk[0, slot_of(slot)]
        user, first, blocks, tail = user_of(ub, tl, logical)
        count = first + blocks - logical

        def group(j, carry):
            spots, reach = [], []
            for i in range(4):
                entry = 4 * j + i
                place = inv[logical + jnp.minimum(entry, count - 1)]
                late = (place // 4 == 4) | (entry >= count)
                spots.append(jnp.where(late, 0, place))
                reach.append(jnp.where(late, 1, jnp.where(entry == 0, 0, -1)))
            queries = jnp.concatenate([buf[p, :128] for p in spots], axis=0)
            grads = jnp.concatenate([buf[p, 160:] for p in spots], axis=0)
            return key_step(kv_ref[slot, 0], kv_ref[slot, 1], queries, grads, reach, carry)

        zero = jnp.zeros((128, 128), F32)
        def step(j, carry):
            return group(2 * j + 1, group(2 * j, carry))

        gk, gv = lax.fori_loop(0, (count + 7) // 8, step, (zero, zero))
        sum_ref[slot, 0] = gk
        sum_ref[slot, 1] = gv
        return carry

    lax.fori_loop(0, 4, one, 0)


def key_far_kernel(
    ub, tl, pk, kv_hbm, near_ref, sc_ref, all_ref, o0, o1, o2, o3, kv_ref, buf, sems
):
    copies = [
        pltpu.make_async_copy(all_ref, buf, sems.at[0]),
        pltpu.make_async_copy(kv_hbm, kv_ref, sems.at[1]),
    ]
    for copy in copies:
        copy.start()
    for copy in copies:
        copy.wait()

    for slot, out in enumerate((o0, o1, o2, o3)):
        logical = pk[0, slot_of(slot)]
        user, first, blocks, tail = user_of(ub, tl, logical)
        reach = []
        for i in range(4):
            other = pk[0, slot_of(16 + i)]
            reach.append(jnp.where((other > logical) & (other < first + blocks), -1, 1))
        queries = jnp.concatenate([buf[i, :128] for i in range(4)], axis=0)
        grads = jnp.concatenate([buf[i, 160:] for i in range(4)], axis=0)
        gk, gv = key_step(
            kv_ref[slot, 0], kv_ref[slot, 1], queries, grads, reach,
            (near_ref[slot, 0], near_ref[slot, 1]),
        )
        out[0] = (gk * SCALE).astype(BF16)
        out[1] = gv.astype(BF16)
        out[2] = sc_ref[slot]


def unpack_early_kernel(p0, p1, p2, p3, gq_ref, gg_ref):
    for d, piece in enumerate((p0, p1, p2, p3)):
        gq_ref[:, head_columns(d)] = piece[0]
        gg_ref[:, head_columns(d)] = piece[1]


def unpack_late_kernel(p0, p1, p2, p3, gk_ref, gv_ref, sc_ref):
    scores = jnp.zeros((128, 128), F32)
    for d, piece in enumerate((p0, p1, p2, p3)):
        gk_ref[:, head_columns(d)] = piece[0]
        gv_ref[:, head_columns(d)] = piece[1]
        scores = scores + piece[2].astype(F32)
    sc_ref[...] = scores


def sum_kernel(copies, parts_ref, out_ref):
    total = jnp.sum(parts_ref[...].astype(F32), axis=0).astype(BF16)
    for i in range(copies):
        out_ref[i] = total


def assemble_kernel(own_ref, far_ref, out_ref):
    me = lax.axis_index("core")
    for group in range(8):
        for xl in range(2):
            own = own_ref[group * 2 + xl].astype(F32)
            far = far_ref[group * 2 + xl].astype(F32)
            for core in range(2):
                rows = pl.ds((xl * 2 + core) * 128, 128)
                out_ref[rows, pl.ds(group * 128, 128)] = jnp.where(me == core, own, far)


def call(kernel, ins, outs, scratch=(), us=2, mib=8):
    return pl.pallas_call(
        kernel,
        in_specs=[spec for spec, _ in ins],
        out_specs=[VM] * len(outs),
        out_shape=[jax.ShapeDtypeStruct(shape, kind) for shape, kind in outs],
        scratch_shapes=list(scratch),
        compiler_params=pltpu.CompilerParams(vmem_limit_bytes=mib << 20),
        cost_estimate=pl.CostEstimate(
            flops=us * 1000000000, bytes_accessed=us * 1000000, transcendentals=0
        ),
    )(*[value for _, value in ins])


def flip(array, axis):
    return lax.ppermute(array, axis, [(0, 1), (1, 0)])


def up(array):
    return lax.ppermute(array, "z", [(i, (i + 1) % 8) for i in range(8)])


def down(array):
    return lax.ppermute(array, "z", [(i, (i + 7) % 8) for i in range(8)])


def ring(array, hold):
    ups, downs = [array], [array]
    for n in range(4):
        waits = hold(n)
        ups.append(up(after(ups[-1], *waits) if waits else ups[-1]))
        if n < 3:
            downs.append(down(after(downs[-1], *waits) if waits else downs[-1]))
    return ups + downs[:0:-1]


def after(value, *waits):
    return lax.optimization_barrier((value,) + waits)[0]


def vm(*arrays):
    return [(VM, a) for a in arrays]


def raw(arrays):
    return [(HBM, pltpu.with_memory_space_constraint(a, pltpu.HBM)) for a in arrays]


def swap(pieces):
    both = lax.ppermute(pieces[3], ("xl", "core"), [(i, 3 - i) for i in range(4)])
    return [pieces[0], flip(pieces[1], "core"), flip(pieces[2], "xl"), both]


def body(
    query, key, value, gate, out_weight, items, cotangent, user_blocks, tail_rows, packing, cand_ids
):
    facts = [(SM, user_blocks), (SM, tail_rows), (SM, packing)]
    block = (4, 128, 128)
    places = pltpu.SMEM((32,), I32)
    sems = pltpu.SemaphoreType.DMA((8,))
    kv_buffer = pltpu.VMEM((32, 2, 128, 128), BF16)
    packed = call(
        pack_kernel,
        raw([key, value, query, gate, items, out_weight]),
        [((544, 128), BF16)] * 4,
        [
            pltpu.VMEM((4, 128, 512), BF16),
            pltpu.VMEM((32, 1024), BF16),
            pltpu.VMEM((512, 1024), BF16),
            pltpu.VMEM((32, 512), BF16),
            pltpu.SemaphoreType.DMA((6,)),
        ],
    )
    first = swap(packed)
    kv, qp, gate_h = call(
        merge_kernel,
        vm(*first),
        [((4, 2, 128, 128), BF16), ((4, 160, 128), BF16), (block, BF16)],
    )
    cots = [cotangent] + swap([after(cotangent, first[2])] * 4)[1:]
    kvs = ring(kv, lambda n: cots[1:] if n == 2 else [])
    (gm,) = call(
        mixed_grad_kernel,
        vm(*cots) + raw([out_weight]),
        [(block, F32)],
        [pltpu.VMEM((128, 1024), BF16), pltpu.SemaphoreType.DMA],
    )
    (att_near,) = call(
        forward_near_kernel,
        facts + vm(qp) + raw(kvs[:4] + kvs[5:]),
        [(block, F32)],
        [kv_buffer, places, sems],
        us=6,
    )
    att, stats = call(
        forward_far_kernel,
        facts + vm(qp, gate_h, gm, att_near, kvs[4]),
        [(block, F32), ((4, 8, 128), F32)],
    )
    all_stats = swap([stats] * 4)
    both, gg, mixed = call(
        norm_kernel,
        facts + vm(att, *all_stats, gate_h, gm, qp),
        [((4, 288, 128), BF16), (block, BF16), ((512, 128), BF16)],
    )
    (gw,) = call(weight_kernel, vm(mixed, *cots), [((8, 128, 128), BF16)])
    parts = lax.all_to_all(gw, ("xh", "y"), split_axis=0, concat_axis=0, tiled=True)
    ups, downs = [both, up(both)], [both, down(both)]
    early = call(
        query_kernel,
        facts + vm(after(both, ups[1], downs[1]), gg) + raw(kvs),
        [((2, 128, 128), BF16)] * 4,
        [kv_buffer, pltpu.VMEM(block, BF16), places, sems],
        us=8,
    )
    ups.append(up(ups[1]))
    downs.append(down(downs[1]))
    (piece,) = call(
        functools.partial(sum_kernel, 8),
        vm(after(parts, ups[2], downs[2], early[0])),
        [((8, 128, 128), BF16)],
        us=8,
    )
    line = lax.all_to_all(piece, "z", split_axis=0, concat_axis=0, tiled=True)
    ups.append(up(ups[2]))
    downs.append(down(downs[2]))
    ups.append(up(ups[3]))
    pairs = ups + downs[:0:-1]
    (sc,) = call(
        score_kernel,
        facts + vm(mixed, cand_ids[0]) + raw(pairs),
        [(block, BF16)],
        [pltpu.VMEM((32, 32, 128), BF16), sems],
    )
    early = swap([after(rows, piece) for rows in early])
    rows = (128, 512)
    gq, gg = call(unpack_early_kernel, vm(*early), [(rows, BF16)] * 2)
    (lines,) = call(
        functools.partial(sum_kernel, 16),
        vm(after(line, ups[3], downs[3], gq)),
        [((16, 128, 128), BF16)],
    )
    near = lax.all_to_all(lines, ("xh", "y", "xl"), split_axis=0, concat_axis=0, tiled=True)
    (key_sums,) = call(
        key_near_kernel,
        facts + raw([kv] + pairs[:4] + pairs[5:]),
        [((4, 2, 128, 128), F32)],
        [pltpu.VMEM((4, 2, 128, 128), BF16), pltpu.VMEM((32, 288, 128), BF16), places, sems],
        us=8,
    )
    late = call(
        key_far_kernel,
        facts + raw([kv]) + vm(key_sums, sc) + raw([pairs[4]]),
        [((3, 128, 128), BF16)] * 4,
        [
            pltpu.VMEM((4, 2, 128, 128), BF16),
            pltpu.VMEM((4, 288, 128), BF16),
            pltpu.SemaphoreType.DMA((2,)),
        ],
        us=3,
    )
    late = swap(late)
    far = flip(after(near, *late[1:]), "core")
    (gow,) = call(assemble_kernel, vm(near, far), [((512, 1024), F32)])
    gk, gv, scores = call(
        unpack_late_kernel, vm(*late), [(rows, BF16), (rows, BF16), ((128, 128), F32)]
    )
    return (scores, gq, gk, gv, gg, gow)


def solution(mesh):
    inner = Mesh(mesh.devices.reshape(SIZES), AXES)
    rows = P(DP + CTX, None)
    in_specs = (
        rows, rows, rows, rows, P(), P(CTX, None), rows,
        P(DP, None), P(DP, None), P(DP, None), P(DP, None, None),
    )
    out_specs = (rows, rows, rows, rows, rows, P())
    return jax.shard_map(body, mesh=inner, in_specs=in_specs, out_specs=out_specs, check_vma=False)
```

```python
import functools

import jax
import jax.numpy as jnp
from jax import lax
from jax.experimental import pallas as pl
from jax.experimental.pallas import tpu as pltpu
from jax.sharding import Mesh, PartitionSpec as P

AXES = ("xh", "y", "xl", "z", "core")
SIZES = (2, 4, 2, 8, 2)
DP = ("xh", "y")
CTX = ("xl", "z", "core")
SCALE = 128 ** (-0.5)
TO_EXP2 = -SCALE * 1.4426950408889634
EPS = 1e-05
F32 = jnp.float32
BF16 = jnp.bfloat16
I32 = jnp.int32

VM = pl.BlockSpec(memory_space=pltpu.VMEM)
SM = pl.BlockSpec(memory_space=pltpu.SMEM)
HBM = pl.BlockSpec(memory_space=pltpu.HBM)


def dot(a, b, ca, cb):
    return lax.dot_general(a, b, (((ca,), (cb,)), ((), ())), preferred_element_type=F32)


def slot_of(place):
    down, other = place // 4, place % 4
    xl = (lax.axis_index("xl") + other // 2) % 2
    z = (lax.axis_index("z") + 8 - down) % 8
    core = (lax.axis_index("core") + other) % 2
    return xl * 16 + z * 2 + core


def fill_places(pk_ref, inv_ref):
    def one(place, carry):
        inv_ref[pk_ref[0, slot_of(place)]] = place
        return carry

    lax.fori_loop(0, 32, one, 0)


def user_of(ub_ref, tl_ref, logical):
    end0 = ub_ref[0, 0]
    end1 = end0 + ub_ref[0, 1]
    end2 = end1 + ub_ref[0, 2]
    user = (
        (logical >= end0).astype(I32) + (logical >= end1).astype(I32) + (logical >= end2).astype(I32)
    )
    first = jnp.where(user == 0, 0, jnp.where(user == 1, end0, jnp.where(user == 2, end1, end2)))
    return user, first, ub_ref[0, user], tl_ref[0, user]


def load_chunks(refs, buffer, sems):
    copies = [
        pltpu.make_async_copy(ref, buffer.at[pl.ds(4 * i, 4)], sems.at[i]) for i, ref in enumerate(refs)
    ]
    for copy in copies:
        copy.start()
    return copies


def iota(shape, axis):
    return lax.broadcasted_iota(I32, shape, axis)


def head_columns(other):
    xl = (lax.axis_index("xl") + other // 2) % 2
    core = (lax.axis_index("core") + other) % 2
    return pl.ds(pl.multiple_of((xl * 2 + core) * 128, 128), 128)


def pack_kernel(
    k_ref, v_ref, q_ref, g_ref, i_ref, w_ref, o0, o1, o2, o3, rows, items, weight, side, sems
):
    copies = [
        pltpu.make_async_copy(ref, to, sems.at[i])
        for i, (ref, to) in enumerate(
            (
                (k_ref, rows.at[0]),
                (v_ref, rows.at[1]),
                (q_ref, rows.at[2]),
                (g_ref, rows.at[3]),
                (i_ref, items),
                (w_ref, weight),
            )
        )
    ]
    for copy in copies:
        copy.start()
    outs = (o0, o1, o2, o3)
    for i in range(4):
        copies[i].wait()
        for d, out in enumerate(outs):
            out[i * 128 : i * 128 + 128] = rows[i, :, head_columns(d)]
    copies[4].wait()
    copies[5].wait()
    side[...] = dot(items[...], weight[...], 1, 1).astype(BF16)
    for d, out in enumerate(outs):
        out[512:] = side[:, head_columns(d)]


def mixed_grad_kernel(c0, c1, c2, c3, w_ref, gm_ref, wbuf, sem):
    copy = pltpu.make_async_copy(
        w_ref.at[head_columns(0)], wbuf, sem
    )
    copy.start()
    copy.wait()
    for d, cot in enumerate((c0, c1, c2, c3)):
        gm_ref[d] = dot(cot[...], wbuf[...], 1, 1)


def merge_kernel(p0, p1, p2, p3, kv_ref, qp_ref, gate_ref):
    for d, piece in enumerate((p0, p1, p2, p3)):
        kv_ref[d, 0] = piece[:128]
        kv_ref[d, 1] = piece[128:256]
        qp_ref[d, :128] = piece[256:384]
        qp_ref[d, 128:] = piece[512:]
        gate_ref[d] = piece[384:512]


def sigmoid(raw):
    return 1.0 / (1.0 + jnp.exp2(raw * TO_EXP2))


def masked_step(query, kv, spots, reach, acc):
    keys = jnp.concatenate([kv[p, 0] for p in spots], axis=0)
    values = jnp.concatenate([kv[p, 1] for p in spots], axis=0)
    row = iota((128, 128), 0) - iota((128, 128), 1)
    raw = dot(query, keys, 1, 1)
    silu = raw * SCALE * sigmoid(raw)
    weights = [
        jnp.where(row >= reach[i] * 128, silu[:, i * 128 : i * 128 + 128], 0.0).astype(BF16)
        for i in range(4)
    ]
    return acc + dot(jnp.concatenate(weights, axis=1), values, 1, 0)


def forward_near_kernel(ub, tl, pk, q_ref, *rest):
    chunks, (att_ref,), (kv, inv, sems) = rest[:7], rest[7:8], rest[8:]
    copies = [
        pltpu.make_async_copy(ref, kv.at[pl.ds(4 * c, 4)], sems.at[c])
        for c, ref in zip((0, 1, 2, 3, 5, 6, 7), chunks)
    ]
    for copy in copies:
        copy.start()
    fill_places(pk, inv)
    for copy in copies:
        copy.wait()

    def one(slot, carry):
        logical = pk[0, slot_of(slot)]
        first = user_of(ub, tl, logical)[1]
        own = logical - first
        query = q_ref[slot, :128]

        def group(j, acc):
            spots, reach = [], []
            for i in range(4):
                entry = 4 * j + i
                place = inv[first + jnp.minimum(entry, own)]
                late = (place // 4 == 4) | (entry > own)
                spots.append(jnp.where(late, 0, place))
                reach.append(jnp.where(late, 1, jnp.where(entry == own, 0, -1)))
            return masked_step(query, kv, spots, reach, acc)

        def step(j, acc):
            return group(2 * j + 1, group(2 * j, acc))

        att_ref[slot] = lax.fori_loop(0, own // 8 + 1, step, jnp.zeros((128, 128), F32))
        return carry

    lax.fori_loop(0, 4, one, 0)


def forward_far_kernel(
    ub, tl, pk, q_ref, gate_ref, gm_ref, near_ref, kv, att_ref, stat_ref
):
    lane = iota((128, 128), 1)

    for slot in range(4):
        logical = pk[0, slot_of(slot)]
        user, first, blocks, tail = user_of(ub, tl, logical)
        own = logical - first
        reach = []
        for i in range(4):
            other = pk[0, slot_of(16 + i)]
            reach.append(jnp.where((other >= first) & (other < logical), -1, 1))
        acc = masked_step(q_ref[slot, :128], kv, range(4), reach, near_ref[slot])
        limit = jnp.where(own == blocks - 1, tail, 128)
        valid = iota((128, 128), 0) < limit
        att = jnp.where(valid, acc, 0.0)
        att_ref[slot] = att
        grad = jnp.where(valid, gm_ref[slot] * gate_ref[slot].astype(F32), 0.0)
        mean = jnp.mean(att, axis=1, keepdims=True)
        centered = att - mean
        spread = jnp.sum(centered * centered, axis=1, keepdims=True)
        total = jnp.sum(grad, axis=1, keepdims=True)
        cross = jnp.sum(grad * centered, axis=1, keepdims=True)
        stats = jnp.where(
            lane == 0, mean, jnp.where(lane == 1, spread, jnp.where(lane == 2, total, cross))
        )
        stat_ref[slot] = stats.T[:8]


def norm_kernel(
    ub, tl, pk, att_ref, s0, s1, s2, s3, gate_ref, gm_ref, qp_ref, all_ref, gg_ref, mixed_ref
):
    line = iota((128, 128), 0)
    for slot in range(4):
        user, first, blocks, tail = user_of(ub, tl, pk[0, slot_of(slot)])
        own = pk[0, slot_of(slot)] - first
        limit = jnp.where(own == blocks - 1, tail, 128)
        valid = line < limit
        stats = [s[slot ^ e] for e, s in enumerate((s0, s1, s2, s3))]
        mean = (stats[0][0:1] + stats[1][0:1] + stats[2][0:1] + stats[3][0:1]) * 0.25
        var = jnp.zeros((1, 128), F32)
        total = jnp.zeros((1, 128), F32)
        cross = jnp.zeros((1, 128), F32)
        for stat in stats:
            away = stat[0:1] - mean
            var = var + stat[1:2] + 128.0 * away * away
            total = total + stat[2:3]
            cross = cross + stat[3:4] + away * stat[2:3]
        inv_std = lax.rsqrt(var * (1.0 / 512) + EPS)
        rows = jnp.where(
            line == 0,
            mean,
            jnp.where(
                line == 1,
                inv_std,
                jnp.where(line == 2, total * (1.0 / 512), cross * inv_std * (1.0 / 512)),
            ),
        ).T
        mean, inv_std, total, cross = (rows[:, i : i + 1] for i in range(4))
        normed = (att_ref[slot] - mean) * inv_std
        gate = gate_ref[slot].astype(F32)
        gmix = jnp.where(valid, gm_ref[slot], 0.0)
        da = (gmix * gate - total - normed * cross) * inv_std
        all_ref[slot, :160] = qp_ref[slot]
        all_ref[slot, 160:] = jnp.where(valid, da, 0.0).astype(BF16)
        gg_ref[slot] = (gmix * normed).astype(BF16)
        mixed_ref[pl.ds(slot * 128, 128), :] = jnp.where(valid, normed * gate, 0.0).astype(BF16)


def weight_kernel(mixed_ref, c0, c1, c2, c3, gw_ref):
    for part in range(4):
        term = jnp.zeros((128, 256), F32)
        for d, cot in enumerate((c0, c1, c2, c3)):
            term = term + dot(mixed_ref[pl.ds(d * 128, 128), :], cot[:, pl.ds(part * 256, 256)], 0, 0)
        gw_ref[2 * part] = term[:, :128].astype(BF16)
        gw_ref[2 * part + 1] = term[:, 128:].astype(BF16)


def score_kernel(ub, tl, pk, mixed_ref, cand_ref, *rest):
    chunks, (sc_ref,), (tables, sems) = rest[:8], rest[8:9], rest[9:]
    copies = [
        pltpu.make_async_copy(ref.at[:, pl.ds(128, 32)], tables.at[pl.ds(4 * i, 4)], sems.at[i])
        for i, ref in enumerate(chunks)
    ]
    for copy in copies:
        copy.start()
    row = iota((32, 128), 0)
    for copy in copies:
        copy.wait()
    table = jnp.concatenate([tables[p] for p in range(32)], axis=0).T
    for slot in range(4):
        user = user_of(ub, tl, pk[0, slot_of(slot)])[0]
        cand = jnp.broadcast_to(cand_ref[pl.ds(user, 1), :], (32, 128))
        pick = jnp.concatenate(
            [(cand - slot_of(p) * 32 == row).astype(F32).astype(BF16) for p in range(32)], axis=0
        )
        chosen = dot(table, pick, 1, 0).astype(BF16)
        sc_ref[slot] = dot(mixed_ref[pl.ds(slot * 128, 128), :], chosen, 1, 0).astype(BF16)


def query_kernel(ub, tl, pk, all_ref, gg_ref, *rest):
    chunks, outs, (kv, gq, inv, sems) = rest[:8], rest[8:12], rest[12:]
    copies = load_chunks(chunks, kv, sems)
    fill_places(pk, inv)
    for copy in copies:
        copy.wait()
    row = iota((128, 512), 0)
    col = iota((128, 512), 1)

    def one(slot, carry):
        logical = pk[0, slot_of(slot)]
        first = user_of(ub, tl, logical)[1]
        own = logical - first
        query = all_ref[slot, :128]
        grad = all_ref[slot, 160:]

        def group(j, acc):
            places = [inv[first + jnp.minimum(4 * j + i, own)] for i in range(4)]
            keys = jnp.concatenate([kv[p, 0] for p in places], axis=0)
            values = jnp.concatenate([kv[p, 1] for p in places], axis=0)
            raw = dot(query, keys, 1, 1)
            slopes = dot(grad, values, 1, 1)
            sigma = sigmoid(raw)
            slope = sigma + raw * SCALE * sigma * (1.0 - sigma)
            ds = jnp.where(col + (4 * j - own) * 128 <= row, slopes * slope, 0.0).astype(BF16)
            return acc + dot(ds, keys, 1, 0)

        def step(j, acc):
            return group(2 * j + 1, group(2 * j, acc))

        acc = lax.fori_loop(0, own // 8 + 1, step, jnp.zeros((128, 128), F32))
        gq[slot] = (acc * SCALE).astype(BF16)
        return carry

    lax.fori_loop(0, 4, one, 0)
    for slot in range(4):
        outs[slot][0] = gq[slot]
        outs[slot][1] = gg_ref[slot]


def key_step(key, value, queries, grads, reach, carry):
    gk, gv = carry
    col = iota((128, 128), 1) - iota((128, 128), 0)
    raw = dot(key, queries, 1, 1)
    slopes = dot(value, grads, 1, 1)
    sigma = sigmoid(raw)
    silu = raw * SCALE * sigma
    change = slopes * (sigma + silu * (1.0 - sigma))
    weights, ds = [], []
    for i in range(4):
        cols = slice(i * 128, i * 128 + 128)
        allowed = col >= reach[i] * 128
        weights.append(jnp.where(allowed, silu[:, cols], 0.0).astype(BF16))
        ds.append(jnp.where(allowed, change[:, cols], 0.0).astype(BF16))
    gk = gk + dot(jnp.concatenate(ds, axis=1), queries, 1, 0)
    gv = gv + dot(jnp.concatenate(weights, axis=1), grads, 1, 0)
    return gk, gv


def key_near_kernel(ub, tl, pk, kv_hbm, *rest):
    chunks, (sum_ref,), (kv_ref, buf, inv, sems) = rest[:7], rest[7:8], rest[8:]
    copies = [
        pltpu.make_async_copy(ref, buf.at[pl.ds(4 * c, 4)], sems.at[c])
        for c, ref in zip((0, 1, 2, 3, 5, 6, 7), chunks)
    ]
    copies.append(pltpu.make_async_copy(kv_hbm, kv_ref, sems.at[4]))
    for copy in copies:
        copy.start()
    fill_places(pk, inv)
    for copy in copies:
        copy.wait()

    def one(slot, carry):
        logical = pk[0, slot_of(slot)]
        user, first, blocks, tail = user_of(ub, tl, logical)
        count = first + blocks - logical

        def group(j, carry):
            spots, reach = [], []
            for i in range(4):
                entry = 4 * j + i
                place = inv[logical + jnp.minimum(entry, count - 1)]
                late = (place // 4 == 4) | (entry >= count)
                spots.append(jnp.where(late, 0, place))
                reach.append(jnp.where(late, 1, jnp.where(entry == 0, 0, -1)))
            queries = jnp.concatenate([buf[p, :128] for p in spots], axis=0)
            grads = jnp.concatenate([buf[p, 160:] for p in spots], axis=0)
            return key_step(kv_ref[slot, 0], kv_ref[slot, 1], queries, grads, reach, carry)

        zero = jnp.zeros((128, 128), F32)
        def step(j, carry):
            return group(2 * j + 1, group(2 * j, carry))

        gk, gv = lax.fori_loop(0, (count + 7) // 8, step, (zero, zero))
        sum_ref[slot, 0] = gk
        sum_ref[slot, 1] = gv
        return carry

    lax.fori_loop(0, 4, one, 0)


def key_far_kernel(
    ub, tl, pk, kv_hbm, near_ref, sc_ref, all_ref, o0, o1, o2, o3, kv_ref, buf, sems
):
    copies = [
        pltpu.make_async_copy(all_ref, buf, sems.at[0]),
        pltpu.make_async_copy(kv_hbm, kv_ref, sems.at[1]),
    ]
    for copy in copies:
        copy.start()
    for copy in copies:
        copy.wait()

    for slot, out in enumerate((o0, o1, o2, o3)):
        logical = pk[0, slot_of(slot)]
        user, first, blocks, tail = user_of(ub, tl, logical)
        reach = []
        for i in range(4):
            other = pk[0, slot_of(16 + i)]
            reach.append(jnp.where((other > logical) & (other < first + blocks), -1, 1))
        queries = jnp.concatenate([buf[i, :128] for i in range(4)], axis=0)
        grads = jnp.concatenate([buf[i, 160:] for i in range(4)], axis=0)
        gk, gv = key_step(
            kv_ref[slot, 0], kv_ref[slot, 1], queries, grads, reach,
            (near_ref[slot, 0], near_ref[slot, 1]),
        )
        out[0] = (gk * SCALE).astype(BF16)
        out[1] = gv.astype(BF16)
        out[2] = sc_ref[slot]


def unpack_early_kernel(p0, p1, p2, p3, gq_ref, gg_ref):
    for d, piece in enumerate((p0, p1, p2, p3)):
        gq_ref[:, head_columns(d)] = piece[0]
        gg_ref[:, head_columns(d)] = piece[1]


def unpack_late_kernel(p0, p1, p2, p3, gk_ref, gv_ref, sc_ref):
    scores = jnp.zeros((128, 128), F32)
    for d, piece in enumerate((p0, p1, p2, p3)):
        gk_ref[:, head_columns(d)] = piece[0]
        gv_ref[:, head_columns(d)] = piece[1]
        scores = scores + piece[2].astype(F32)
    sc_ref[...] = scores


def sum_kernel(copies, parts_ref, out_ref):
    total = jnp.sum(parts_ref[...].astype(F32), axis=0).astype(BF16)
    for i in range(copies):
        out_ref[i] = total


def assemble_kernel(own_ref, far_ref, out_ref):
    me = lax.axis_index("core")
    for group in range(8):
        for xl in range(2):
            own = own_ref[group * 2 + xl].astype(F32)
            far = far_ref[group * 2 + xl].astype(F32)
            for core in range(2):
                rows = pl.ds((xl * 2 + core) * 128, 128)
                out_ref[rows, pl.ds(group * 128, 128)] = jnp.where(me == core, own, far)


def call(kernel, ins, outs, scratch=(), us=2, mib=8):
    return pl.pallas_call(
        kernel,
        in_specs=[spec for spec, _ in ins],
        out_specs=[VM] * len(outs),
        out_shape=[jax.ShapeDtypeStruct(shape, kind) for shape, kind in outs],
        scratch_shapes=list(scratch),
        compiler_params=pltpu.CompilerParams(vmem_limit_bytes=mib << 20),
        cost_estimate=pl.CostEstimate(
            flops=us * 1000000000, bytes_accessed=us * 1000000, transcendentals=0
        ),
    )(*[value for _, value in ins])


def flip(array, axis):
    return lax.ppermute(array, axis, [(0, 1), (1, 0)])


def up(array):
    return lax.ppermute(array, "z", [(i, (i + 1) % 8) for i in range(8)])


def down(array):
    return lax.ppermute(array, "z", [(i, (i + 7) % 8) for i in range(8)])


def ring(array, hold):
    ups, downs = [array], [array]
    for n in range(4):
        waits = hold(n)
        ups.append(up(after(ups[-1], *waits) if waits else ups[-1]))
        if n < 3:
            downs.append(down(after(downs[-1], *waits) if waits else downs[-1]))
    return ups + downs[:0:-1]


def after(value, *waits):
    return lax.optimization_barrier((value,) + waits)[0]


def vm(*arrays):
    return [(VM, a) for a in arrays]


def raw(arrays):
    return [(HBM, pltpu.with_memory_space_constraint(a, pltpu.HBM)) for a in arrays]


def swap(pieces):
    both = lax.ppermute(pieces[3], ("xl", "core"), [(i, 3 - i) for i in range(4)])
    return [pieces[0], flip(pieces[1], "core"), flip(pieces[2], "xl"), both]


def body(
    query, key, value, gate, out_weight, items, cotangent, user_blocks, tail_rows, packing, cand_ids
):
    facts = [(SM, user_blocks), (SM, tail_rows), (SM, packing)]
    block = (4, 128, 128)
    places = pltpu.SMEM((32,), I32)
    sems = pltpu.SemaphoreType.DMA((8,))
    kv_buffer = pltpu.VMEM((32, 2, 128, 128), BF16)
    packed = call(
        pack_kernel,
        raw([key, value, query, gate, items, out_weight]),
        [((544, 128), BF16)] * 4,
        [
            pltpu.VMEM((4, 128, 512), BF16),
            pltpu.VMEM((32, 1024), BF16),
            pltpu.VMEM((512, 1024), BF16),
            pltpu.VMEM((32, 512), BF16),
            pltpu.SemaphoreType.DMA((6,)),
        ],
    )
    first = swap(packed)
    kv, qp, gate_h = call(
        merge_kernel,
        vm(*first),
        [((4, 2, 128, 128), BF16), ((4, 160, 128), BF16), (block, BF16)],
    )
    cots = [cotangent] + swap([after(cotangent, first[2])] * 4)[1:]
    kvs = ring(kv, lambda n: cots[1:] if n == 2 else [])
    (gm,) = call(
        mixed_grad_kernel,
        vm(*cots) + raw([out_weight]),
        [(block, F32)],
        [pltpu.VMEM((128, 1024), BF16), pltpu.SemaphoreType.DMA],
    )
    (att_near,) = call(
        forward_near_kernel,
        facts + vm(qp) + raw(kvs[:4] + kvs[5:]),
        [(block, F32)],
        [kv_buffer, places, sems],
        us=6,
    )
    att, stats = call(
        forward_far_kernel,
        facts + vm(qp, gate_h, gm, att_near, kvs[4]),
        [(block, F32), ((4, 8, 128), F32)],
    )
    all_stats = swap([stats] * 4)
    both, gg, mixed = call(
        norm_kernel,
        facts + vm(att, *all_stats, gate_h, gm, qp),
        [((4, 288, 128), BF16), (block, BF16), ((512, 128), BF16)],
    )
    (gw,) = call(weight_kernel, vm(mixed, *cots), [((8, 128, 128), BF16)])
    parts = lax.all_to_all(gw, ("xh", "y"), split_axis=0, concat_axis=0, tiled=True)
    ups, downs = [both, up(both)], [both, down(both)]
    early = call(
        query_kernel,
        facts + vm(after(both, ups[1], downs[1]), gg) + raw(kvs),
        [((2, 128, 128), BF16)] * 4,
        [kv_buffer, pltpu.VMEM(block, BF16), places, sems],
        us=8,
    )
    ups.append(up(ups[1]))
    downs.append(down(downs[1]))
    (piece,) = call(
        functools.partial(sum_kernel, 8),
        vm(after(parts, ups[2], downs[2], early[0])),
        [((8, 128, 128), BF16)],
        us=8,
    )
    line = lax.all_to_all(piece, "z", split_axis=0, concat_axis=0, tiled=True)
    ups.append(up(ups[2]))
    downs.append(down(downs[2]))
    ups.append(up(ups[3]))
    pairs = ups + downs[:0:-1]
    (sc,) = call(
        score_kernel,
        facts + vm(mixed, cand_ids[0]) + raw(pairs),
        [(block, BF16)],
        [pltpu.VMEM((32, 32, 128), BF16), sems],
    )
    early = swap([after(rows, ups[3]) for rows in early])
    rows = (128, 512)
    gq, gg = call(unpack_early_kernel, vm(*early), [(rows, BF16)] * 2)
    (lines,) = call(
        functools.partial(sum_kernel, 16),
        vm(after(line, ups[3], downs[3], gq)),
        [((16, 128, 128), BF16)],
    )
    near = lax.all_to_all(lines, ("xh", "y", "xl"), split_axis=0, concat_axis=0, tiled=True)
    (key_sums,) = call(
        key_near_kernel,
        facts + raw([kv] + pairs[:4] + pairs[5:]),
        [((4, 2, 128, 128), F32)],
        [pltpu.VMEM((4, 2, 128, 128), BF16), pltpu.VMEM((32, 288, 128), BF16), places, sems],
        us=8,
    )
    late = call(
        key_far_kernel,
        facts + raw([kv]) + vm(key_sums, sc) + raw([pairs[4]]),
        [((3, 128, 128), BF16)] * 4,
        [
            pltpu.VMEM((4, 2, 128, 128), BF16),
            pltpu.VMEM((4, 288, 128), BF16),
            pltpu.SemaphoreType.DMA((2,)),
        ],
        us=3,
    )
    late = swap(late)
    far = flip(after(near, *late[1:]), "core")
    (gow,) = call(assemble_kernel, vm(near, far), [((512, 1024), F32)])
    gk, gv, scores = call(
        unpack_late_kernel, vm(*late), [(rows, BF16), (rows, BF16), ((128, 128), F32)]
    )
    return (scores, gq, gk, gv, gg, gow)


def solution(mesh):
    inner = Mesh(mesh.devices.reshape(SIZES), AXES)
    rows = P(DP + CTX, None)
    in_specs = (
        rows, rows, rows, rows, P(), P(CTX, None), rows,
        P(DP, None), P(DP, None), P(DP, None), P(DP, None, None),
    )
    out_specs = (rows, rows, rows, rows, rows, P())
    return jax.shard_map(body, mesh=inner, in_specs=in_specs, out_specs=out_specs, check_vma=False)
```

```python
import functools

import jax
import jax.numpy as jnp
from jax import lax
from jax.experimental import pallas as pl
from jax.experimental.pallas import tpu as pltpu
from jax.sharding import Mesh, PartitionSpec as P

AXES = ("xh", "y", "xl", "z", "core")
SIZES = (2, 4, 2, 8, 2)
DP = ("xh", "y")
CTX = ("xl", "z", "core")
SCALE = 128 ** (-0.5)
TO_EXP2 = -SCALE * 1.4426950408889634
EPS = 1e-05
F32 = jnp.float32
BF16 = jnp.bfloat16
I32 = jnp.int32

VM = pl.BlockSpec(memory_space=pltpu.VMEM)
SM = pl.BlockSpec(memory_space=pltpu.SMEM)
HBM = pl.BlockSpec(memory_space=pltpu.HBM)


def dot(a, b, ca, cb):
    return lax.dot_general(a, b, (((ca,), (cb,)), ((), ())), preferred_element_type=F32)


def slot_of(place):
    down, other = place // 4, place % 4
    xl = (lax.axis_index("xl") + other // 2) % 2
    z = (lax.axis_index("z") + 8 - down) % 8
    core = (lax.axis_index("core") + other) % 2
    return xl * 16 + z * 2 + core


def fill_places(pk_ref, inv_ref):
    def one(place, carry):
        inv_ref[pk_ref[0, slot_of(place)]] = place
        return carry

    lax.fori_loop(0, 32, one, 0)


def user_of(ub_ref, tl_ref, logical):
    end0 = ub_ref[0, 0]
    end1 = end0 + ub_ref[0, 1]
    end2 = end1 + ub_ref[0, 2]
    user = (
        (logical >= end0).astype(I32) + (logical >= end1).astype(I32) + (logical >= end2).astype(I32)
    )
    first = jnp.where(user == 0, 0, jnp.where(user == 1, end0, jnp.where(user == 2, end1, end2)))
    return user, first, ub_ref[0, user], tl_ref[0, user]


def load_chunks(refs, buffer, sems):
    copies = [
        pltpu.make_async_copy(ref, buffer.at[pl.ds(4 * i, 4)], sems.at[i]) for i, ref in enumerate(refs)
    ]
    for copy in copies:
        copy.start()
    return copies


def iota(shape, axis):
    return lax.broadcasted_iota(I32, shape, axis)


def head_columns(other):
    xl = (lax.axis_index("xl") + other // 2) % 2
    core = (lax.axis_index("core") + other) % 2
    return pl.ds(pl.multiple_of((xl * 2 + core) * 128, 128), 128)


def pack_kernel(
    k_ref, v_ref, q_ref, g_ref, i_ref, w_ref, o0, o1, o2, o3, rows, items, weight, side, sems
):
    copies = [
        pltpu.make_async_copy(ref, to, sems.at[i])
        for i, (ref, to) in enumerate(
            (
                (k_ref, rows.at[0]),
                (v_ref, rows.at[1]),
                (q_ref, rows.at[2]),
                (g_ref, rows.at[3]),
                (i_ref, items),
                (w_ref, weight),
            )
        )
    ]
    for copy in copies:
        copy.start()
    outs = (o0, o1, o2, o3)
    for i in range(4):
        copies[i].wait()
        for d, out in enumerate(outs):
            out[i * 128 : i * 128 + 128] = rows[i, :, head_columns(d)]
    copies[4].wait()
    copies[5].wait()
    side[...] = dot(items[...], weight[...], 1, 1).astype(BF16)
    for d, out in enumerate(outs):
        out[512:] = side[:, head_columns(d)]


def mixed_grad_kernel(c0, c1, c2, c3, w_ref, gm_ref, wbuf, sem):
    copy = pltpu.make_async_copy(
        w_ref.at[head_columns(0)], wbuf, sem
    )
    copy.start()
    copy.wait()
    for d, cot in enumerate((c0, c1, c2, c3)):
        gm_ref[d] = dot(cot[...], wbuf[...], 1, 1)


def merge_kernel(p0, p1, p2, p3, kv_ref, qp_ref, gate_ref):
    for d, piece in enumerate((p0, p1, p2, p3)):
        kv_ref[d, 0] = piece[:128]
        kv_ref[d, 1] = piece[128:256]
        qp_ref[d, :128] = piece[256:384]
        qp_ref[d, 128:] = piece[512:]
        gate_ref[d] = piece[384:512]


def sigmoid(raw):
    return 1.0 / (1.0 + jnp.exp2(raw * TO_EXP2))


def masked_step(query, kv, spots, reach, acc):
    keys = jnp.concatenate([kv[p, 0] for p in spots], axis=0)
    values = jnp.concatenate([kv[p, 1] for p in spots], axis=0)
    row = iota((128, 128), 0) - iota((128, 128), 1)
    raw = dot(query, keys, 1, 1)
    silu = raw * SCALE * sigmoid(raw)
    weights = [
        jnp.where(row >= reach[i] * 128, silu[:, i * 128 : i * 128 + 128], 0.0).astype(BF16)
        for i in range(4)
    ]
    return acc + dot(jnp.concatenate(weights, axis=1), values, 1, 0)


def forward_near_kernel(ub, tl, pk, q_ref, *rest):
    chunks, (att_ref,), (kv, inv, sems) = rest[:7], rest[7:8], rest[8:]
    copies = [
        pltpu.make_async_copy(ref, kv.at[pl.ds(4 * c, 4)], sems.at[c])
        for c, ref in zip((0, 1, 2, 3, 5, 6, 7), chunks)
    ]
    for copy in copies:
        copy.start()
    fill_places(pk, inv)
    for copy in copies:
        copy.wait()

    def one(slot, carry):
        logical = pk[0, slot_of(slot)]
        first = user_of(ub, tl, logical)[1]
        own = logical - first
        query = q_ref[slot, :128]

        def group(j, acc):
            spots, reach = [], []
            for i in range(4):
                entry = 4 * j + i
                place = inv[first + jnp.minimum(entry, own)]
                late = (place // 4 == 4) | (entry > own)
                spots.append(jnp.where(late, 0, place))
                reach.append(jnp.where(late, 1, jnp.where(entry == own, 0, -1)))
            return masked_step(query, kv, spots, reach, acc)

        def step(j, acc):
            return group(2 * j + 1, group(2 * j, acc))

        att_ref[slot] = lax.fori_loop(0, own // 8 + 1, step, jnp.zeros((128, 128), F32))
        return carry

    lax.fori_loop(0, 4, one, 0)


def forward_far_kernel(
    ub, tl, pk, q_ref, gate_ref, gm_ref, near_ref, kv, att_ref, stat_ref
):
    lane = iota((128, 128), 1)

    for slot in range(4):
        logical = pk[0, slot_of(slot)]
        user, first, blocks, tail = user_of(ub, tl, logical)
        own = logical - first
        reach = []
        for i in range(4):
            other = pk[0, slot_of(16 + i)]
            reach.append(jnp.where((other >= first) & (other < logical), -1, 1))
        acc = masked_step(q_ref[slot, :128], kv, range(4), reach, near_ref[slot])
        limit = jnp.where(own == blocks - 1, tail, 128)
        valid = iota((128, 128), 0) < limit
        att = jnp.where(valid, acc, 0.0)
        att_ref[slot] = att
        grad = jnp.where(valid, gm_ref[slot] * gate_ref[slot].astype(F32), 0.0)
        mean = jnp.mean(att, axis=1, keepdims=True)
        centered = att - mean
        spread = jnp.sum(centered * centered, axis=1, keepdims=True)
        total = jnp.sum(grad, axis=1, keepdims=True)
        cross = jnp.sum(grad * centered, axis=1, keepdims=True)
        stats = jnp.where(
            lane == 0, mean, jnp.where(lane == 1, spread, jnp.where(lane == 2, total, cross))
        )
        stat_ref[slot] = stats.T[:8]


def norm_kernel(
    ub, tl, pk, att_ref, s0, s1, s2, s3, gate_ref, gm_ref, qp_ref, all_ref, gg_ref, mixed_ref
):
    line = iota((128, 128), 0)
    for slot in range(4):
        user, first, blocks, tail = user_of(ub, tl, pk[0, slot_of(slot)])
        own = pk[0, slot_of(slot)] - first
        limit = jnp.where(own == blocks - 1, tail, 128)
        valid = line < limit
        stats = [s[slot ^ e] for e, s in enumerate((s0, s1, s2, s3))]
        mean = (stats[0][0:1] + stats[1][0:1] + stats[2][0:1] + stats[3][0:1]) * 0.25
        var = jnp.zeros((1, 128), F32)
        total = jnp.zeros((1, 128), F32)
        cross = jnp.zeros((1, 128), F32)
        for stat in stats:
            away = stat[0:1] - mean
            var = var + stat[1:2] + 128.0 * away * away
            total = total + stat[2:3]
            cross = cross + stat[3:4] + away * stat[2:3]
        inv_std = lax.rsqrt(var * (1.0 / 512) + EPS)
        rows = jnp.where(
            line == 0,
            mean,
            jnp.where(
                line == 1,
                inv_std,
                jnp.where(line == 2, total * (1.0 / 512), cross * inv_std * (1.0 / 512)),
            ),
        ).T
        mean, inv_std, total, cross = (rows[:, i : i + 1] for i in range(4))
        normed = (att_ref[slot] - mean) * inv_std
        gate = gate_ref[slot].astype(F32)
        gmix = jnp.where(valid, gm_ref[slot], 0.0)
        da = (gmix * gate - total - normed * cross) * inv_std
        all_ref[slot, :160] = qp_ref[slot]
        all_ref[slot, 160:] = jnp.where(valid, da, 0.0).astype(BF16)
        gg_ref[slot] = (gmix * normed).astype(BF16)
        mixed_ref[pl.ds(slot * 128, 128), :] = jnp.where(valid, normed * gate, 0.0).astype(BF16)


def weight_kernel(mixed_ref, c0, c1, c2, c3, gw_ref):
    for part in range(4):
        term = jnp.zeros((128, 256), F32)
        for d, cot in enumerate((c0, c1, c2, c3)):
            term = term + dot(mixed_ref[pl.ds(d * 128, 128), :], cot[:, pl.ds(part * 256, 256)], 0, 0)
        gw_ref[2 * part] = term[:, :128].astype(BF16)
        gw_ref[2 * part + 1] = term[:, 128:].astype(BF16)


def score_kernel(ub, tl, pk, mixed_ref, cand_ref, *rest):
    chunks, (sc_ref,), (tables, sems) = rest[:8], rest[8:9], rest[9:]
    copies = [
        pltpu.make_async_copy(ref.at[:, pl.ds(128, 32)], tables.at[pl.ds(4 * i, 4)], sems.at[i])
        for i, ref in enumerate(chunks)
    ]
    for copy in copies:
        copy.start()
    row = iota((32, 128), 0)
    for copy in copies:
        copy.wait()
    table = jnp.concatenate([tables[p] for p in range(32)], axis=0).T
    for slot in range(4):
        user = user_of(ub, tl, pk[0, slot_of(slot)])[0]
        cand = jnp.broadcast_to(cand_ref[pl.ds(user, 1), :], (32, 128))
        pick = jnp.concatenate(
            [(cand - slot_of(p) * 32 == row).astype(F32).astype(BF16) for p in range(32)], axis=0
        )
        chosen = dot(table, pick, 1, 0).astype(BF16)
        sc_ref[slot] = dot(mixed_ref[pl.ds(slot * 128, 128), :], chosen, 1, 0).astype(BF16)


def query_kernel(ub, tl, pk, all_ref, gg_ref, *rest):
    chunks, outs, (kv, gq, inv, sems) = rest[:8], rest[8:12], rest[12:]
    copies = load_chunks(chunks, kv, sems)
    fill_places(pk, inv)
    for copy in copies:
        copy.wait()
    row = iota((128, 512), 0)
    col = iota((128, 512), 1)

    def one(slot, carry):
        logical = pk[0, slot_of(slot)]
        first = user_of(ub, tl, logical)[1]
        own = logical - first
        query = all_ref[slot, :128]
        grad = all_ref[slot, 160:]

        def group(j, acc):
            places = [inv[first + jnp.minimum(4 * j + i, own)] for i in range(4)]
            keys = jnp.concatenate([kv[p, 0] for p in places], axis=0)
            values = jnp.concatenate([kv[p, 1] for p in places], axis=0)
            raw = dot(query, keys, 1, 1)
            slopes = dot(grad, values, 1, 1)
            sigma = sigmoid(raw)
            slope = sigma + raw * SCALE * sigma * (1.0 - sigma)
            ds = jnp.where(col + (4 * j - own) * 128 <= row, slopes * slope, 0.0).astype(BF16)
            return acc + dot(ds, keys, 1, 0)

        def step(j, acc):
            return group(2 * j + 1, group(2 * j, acc))

        acc = lax.fori_loop(0, own // 8 + 1, step, jnp.zeros((128, 128), F32))
        gq[slot] = (acc * SCALE).astype(BF16)
        return carry

    lax.fori_loop(0, 4, one, 0)
    for slot in range(4):
        outs[slot][0] = gq[slot]
        outs[slot][1] = gg_ref[slot]


def key_step(key, value, queries, grads, reach, carry):
    gk, gv = carry
    col = iota((128, 128), 1) - iota((128, 128), 0)
    raw = dot(key, queries, 1, 1)
    slopes = dot(value, grads, 1, 1)
    sigma = sigmoid(raw)
    silu = raw * SCALE * sigma
    change = slopes * (sigma + silu * (1.0 - sigma))
    weights, ds = [], []
    for i in range(4):
        cols = slice(i * 128, i * 128 + 128)
        allowed = col >= reach[i] * 128
        weights.append(jnp.where(allowed, silu[:, cols], 0.0).astype(BF16))
        ds.append(jnp.where(allowed, change[:, cols], 0.0).astype(BF16))
    gk = gk + dot(jnp.concatenate(ds, axis=1), queries, 1, 0)
    gv = gv + dot(jnp.concatenate(weights, axis=1), grads, 1, 0)
    return gk, gv


def key_near_kernel(ub, tl, pk, kv_hbm, *rest):
    chunks, (sum_ref,), (kv_ref, buf, inv, sems) = rest[:7], rest[7:8], rest[8:]
    copies = [
        pltpu.make_async_copy(ref, buf.at[pl.ds(4 * c, 4)], sems.at[c])
        for c, ref in zip((0, 1, 2, 3, 5, 6, 7), chunks)
    ]
    copies.append(pltpu.make_async_copy(kv_hbm, kv_ref, sems.at[4]))
    for copy in copies:
        copy.start()
    fill_places(pk, inv)
    for copy in copies:
        copy.wait()

    def one(slot, carry):
        logical = pk[0, slot_of(slot)]
        user, first, blocks, tail = user_of(ub, tl, logical)
        count = first + blocks - logical

        def group(j, carry):
            spots, reach = [], []
            for i in range(4):
                entry = 4 * j + i
                place = inv[logical + jnp.minimum(entry, count - 1)]
                late = (place // 4 == 4) | (entry >= count)
                spots.append(jnp.where(late, 0, place))
                reach.append(jnp.where(late, 1, jnp.where(entry == 0, 0, -1)))
            queries = jnp.concatenate([buf[p, :128] for p in spots], axis=0)
            grads = jnp.concatenate([buf[p, 160:] for p in spots], axis=0)
            return key_step(kv_ref[slot, 0], kv_ref[slot, 1], queries, grads, reach, carry)

        zero = jnp.zeros((128, 128), F32)
        def step(j, carry):
            return group(2 * j + 1, group(2 * j, carry))

        gk, gv = lax.fori_loop(0, (count + 7) // 8, step, (zero, zero))
        sum_ref[slot, 0] = gk
        sum_ref[slot, 1] = gv
        return carry

    lax.fori_loop(0, 4, one, 0)


def key_far_kernel(
    ub, tl, pk, kv_hbm, near_ref, sc_ref, all_ref, o0, o1, o2, o3, kv_ref, buf, sems
):
    copies = [
        pltpu.make_async_copy(all_ref, buf, sems.at[0]),
        pltpu.make_async_copy(kv_hbm, kv_ref, sems.at[1]),
    ]
    for copy in copies:
        copy.start()
    for copy in copies:
        copy.wait()

    for slot, out in enumerate((o0, o1, o2, o3)):
        logical = pk[0, slot_of(slot)]
        user, first, blocks, tail = user_of(ub, tl, logical)
        reach = []
        for i in range(4):
            other = pk[0, slot_of(16 + i)]
            reach.append(jnp.where((other > logical) & (other < first + blocks), -1, 1))
        queries = jnp.concatenate([buf[i, :128] for i in range(4)], axis=0)
        grads = jnp.concatenate([buf[i, 160:] for i in range(4)], axis=0)
        gk, gv = key_step(
            kv_ref[slot, 0], kv_ref[slot, 1], queries, grads, reach,
            (near_ref[slot, 0], near_ref[slot, 1]),
        )
        out[0] = (gk * SCALE).astype(BF16)
        out[1] = gv.astype(BF16)
        out[2] = sc_ref[slot]


def unpack_early_kernel(p0, p1, p2, p3, gq_ref, gg_ref):
    for d, piece in enumerate((p0, p1, p2, p3)):
        gq_ref[:, head_columns(d)] = piece[0]
        gg_ref[:, head_columns(d)] = piece[1]


def unpack_late_kernel(p0, p1, p2, p3, gk_ref, gv_ref, sc_ref):
    scores = jnp.zeros((128, 128), F32)
    for d, piece in enumerate((p0, p1, p2, p3)):
        gk_ref[:, head_columns(d)] = piece[0]
        gv_ref[:, head_columns(d)] = piece[1]
        scores = scores + piece[2].astype(F32)
    sc_ref[...] = scores


def sum_kernel(copies, parts_ref, out_ref):
    total = jnp.sum(parts_ref[...].astype(F32), axis=0).astype(BF16)
    for i in range(copies):
        out_ref[i] = total


def assemble_kernel(own_ref, far_ref, out_ref):
    me = lax.axis_index("core")
    for group in range(8):
        for xl in range(2):
            own = own_ref[group * 2 + xl].astype(F32)
            far = far_ref[group * 2 + xl].astype(F32)
            for core in range(2):
                rows = pl.ds((xl * 2 + core) * 128, 128)
                out_ref[rows, pl.ds(group * 128, 128)] = jnp.where(me == core, own, far)


def call(kernel, ins, outs, scratch=(), us=2, mib=8):
    return pl.pallas_call(
        kernel,
        in_specs=[spec for spec, _ in ins],
        out_specs=[VM] * len(outs),
        out_shape=[jax.ShapeDtypeStruct(shape, kind) for shape, kind in outs],
        scratch_shapes=list(scratch),
        compiler_params=pltpu.CompilerParams(vmem_limit_bytes=mib << 20),
        cost_estimate=pl.CostEstimate(
            flops=us * 1000000000, bytes_accessed=us * 1000000, transcendentals=0
        ),
    )(*[value for _, value in ins])


def flip(array, axis):
    return lax.ppermute(array, axis, [(0, 1), (1, 0)])


def up(array):
    return lax.ppermute(array, "z", [(i, (i + 1) % 8) for i in range(8)])


def down(array):
    return lax.ppermute(array, "z", [(i, (i + 7) % 8) for i in range(8)])


def ring(array, hold):
    ups, downs = [array], [array]
    for n in range(4):
        waits = hold(n)
        ups.append(up(after(ups[-1], *waits) if waits else ups[-1]))
        if n < 3:
            downs.append(down(after(downs[-1], *waits) if waits else downs[-1]))
    return ups + downs[:0:-1]


def after(value, *waits):
    return lax.optimization_barrier((value,) + waits)[0]


def vm(*arrays):
    return [(VM, a) for a in arrays]


def raw(arrays):
    return [(HBM, pltpu.with_memory_space_constraint(a, pltpu.HBM)) for a in arrays]


def loose(arrays):
    return [(HBM, a) if i in (3, 4) else raw([a])[0] for i, a in enumerate(arrays)]


def swap(pieces):
    both = lax.ppermute(pieces[3], ("xl", "core"), [(i, 3 - i) for i in range(4)])
    return [pieces[0], flip(pieces[1], "core"), flip(pieces[2], "xl"), both]


def body(
    query, key, value, gate, out_weight, items, cotangent, user_blocks, tail_rows, packing, cand_ids
):
    facts = [(SM, user_blocks), (SM, tail_rows), (SM, packing)]
    block = (4, 128, 128)
    places = pltpu.SMEM((32,), I32)
    sems = pltpu.SemaphoreType.DMA((8,))
    kv_buffer = pltpu.VMEM((32, 2, 128, 128), BF16)
    packed = call(
        pack_kernel,
        raw([key, value, query, gate, items, out_weight]),
        [((544, 128), BF16)] * 4,
        [
            pltpu.VMEM((4, 128, 512), BF16),
            pltpu.VMEM((32, 1024), BF16),
            pltpu.VMEM((512, 1024), BF16),
            pltpu.VMEM((32, 512), BF16),
            pltpu.SemaphoreType.DMA((6,)),
        ],
    )
    first = swap(packed)
    kv, qp, gate_h = call(
        merge_kernel,
        vm(*first),
        [((4, 2, 128, 128), BF16), ((4, 160, 128), BF16), (block, BF16)],
    )
    cots = [cotangent] + swap([after(cotangent, first[2])] * 4)[1:]
    kvs = ring(kv, lambda n: cots[1:] if n == 2 else [])
    (gm,) = call(
        mixed_grad_kernel,
        vm(*cots) + raw([out_weight]),
        [(block, F32)],
        [pltpu.VMEM((128, 1024), BF16), pltpu.SemaphoreType.DMA],
    )
    (att_near,) = call(
        forward_near_kernel,
        facts + vm(qp) + loose(kvs[:4] + kvs[5:]),
        [(block, F32)],
        [kv_buffer, places, sems],
        us=6,
    )
    att, stats = call(
        forward_far_kernel,
        facts + vm(qp, gate_h, gm, att_near, kvs[4]),
        [(block, F32), ((4, 8, 128), F32)],
    )
    all_stats = swap([stats] * 4)
    both, gg, mixed = call(
        norm_kernel,
        facts + vm(att, *all_stats, gate_h, gm, qp),
        [((4, 288, 128), BF16), (block, BF16), ((512, 128), BF16)],
    )
    (gw,) = call(weight_kernel, vm(mixed, *cots), [((8, 128, 128), BF16)])
    parts = lax.all_to_all(gw, ("xh", "y"), split_axis=0, concat_axis=0, tiled=True)
    ups, downs = [both, up(both)], [both, down(both)]
    early = call(
        query_kernel,
        facts + vm(after(both, ups[1], downs[1]), gg) + raw(kvs),
        [((2, 128, 128), BF16)] * 4,
        [kv_buffer, pltpu.VMEM(block, BF16), places, sems],
        us=8,
    )
    ups.append(up(ups[1]))
    downs.append(down(downs[1]))
    (piece,) = call(
        functools.partial(sum_kernel, 8),
        vm(after(parts, ups[2], downs[2], early[0])),
        [((8, 128, 128), BF16)],
        us=8,
    )
    line = lax.all_to_all(piece, "z", split_axis=0, concat_axis=0, tiled=True)
    ups.append(up(ups[2]))
    downs.append(down(downs[2]))
    ups.append(up(ups[3]))
    pairs = ups + downs[:0:-1]
    (sc,) = call(
        score_kernel,
        facts + vm(mixed, cand_ids[0]) + raw(pairs),
        [(block, BF16)],
        [pltpu.VMEM((32, 32, 128), BF16), sems],
    )
    early = swap([after(rows, ups[3]) for rows in early])
    rows = (128, 512)
    gq, gg = call(unpack_early_kernel, vm(*early), [(rows, BF16)] * 2)
    (lines,) = call(
        functools.partial(sum_kernel, 16),
        vm(after(line, ups[3], downs[3], gq)),
        [((16, 128, 128), BF16)],
    )
    near = lax.all_to_all(lines, ("xh", "y", "xl"), split_axis=0, concat_axis=0, tiled=True)
    (key_sums,) = call(
        key_near_kernel,
        facts + raw([kv]) + loose(pairs[:4] + pairs[5:]),
        [((4, 2, 128, 128), F32)],
        [pltpu.VMEM((4, 2, 128, 128), BF16), pltpu.VMEM((32, 288, 128), BF16), places, sems],
        us=8,
    )
    late = call(
        key_far_kernel,
        facts + raw([kv]) + vm(key_sums, sc) + raw([pairs[4]]),
        [((3, 128, 128), BF16)] * 4,
        [
            pltpu.VMEM((4, 2, 128, 128), BF16),
            pltpu.VMEM((4, 288, 128), BF16),
            pltpu.SemaphoreType.DMA((2,)),
        ],
        us=3,
    )
    late = swap(late)
    far = flip(after(near, *late[1:]), "core")
    (gow,) = call(assemble_kernel, vm(near, far), [((512, 1024), F32)])
    gk, gv, scores = call(
        unpack_late_kernel, vm(*late), [(rows, BF16), (rows, BF16), ((128, 128), F32)]
    )
    return (scores, gq, gk, gv, gg, gow)


def solution(mesh):
    inner = Mesh(mesh.devices.reshape(SIZES), AXES)
    rows = P(DP + CTX, None)
    in_specs = (
        rows, rows, rows, rows, P(), P(CTX, None), rows,
        P(DP, None), P(DP, None), P(DP, None), P(DP, None, None),
    )
    out_specs = (rows, rows, rows, rows, rows, P())
    return jax.shard_map(body, mesh=inner, in_specs=in_specs, out_specs=out_specs, check_vma=False)
```
